32 devices in a mesh: groups: 2 (over y), dp: 4 (over z), landmark: 4 (over x, core).
Axes of the slice: x: 2, y: 2, z: 4, core: 2. Of those that a mesh axis runs over, the one named last changes fastest.
Arguments:
- images: bfloat16 [256, 1024], P(('groups', 'dp')), parts along dimension 0, may hold values from -6 to 6, as said below
- captions: bfloat16 [256, 768], P(('groups', 'dp')), parts along dimension 0, may hold values from -6 to 6, as said below
- caption_of: int32 [256], P(('groups', 'dp')), parts along dimension 0, may hold values from 0 to 31, as said below
- image_landmarks: bfloat16 [16384, 1024], P(('landmark', 'dp')), may hold values from -6 to 6
- image_gamma: float32 [16384], P(('landmark', 'dp')), may hold values from 8 to 40
- text_landmarks: bfloat16 [4096, 768], P(('dp', 'landmark')), may hold values from -6 to 6
- text_gamma: float32 [4096], P(('dp', 'landmark')), may hold values from 8 to 40
Outputs:
- zstat: float32 [32768, 4096], P(('groups', 'landmark'), 'dp'), parts along dimension 0
- image_mean: float32 [32768], P(('groups', 'landmark', 'dp')), parts along dimension 0
- text_mean: float32 [8192], P(('groups', 'dp', 'landmark')), parts along dimension 0
The draws below stay inside these ranges and needn't reach their ends.
There are 2 independent parts, one for each index of `groups`. The reference program is written for one: setup_inputs(seed, part) draws one part's arguments, and reference() takes and returns one part's arrays. A program takes and returns all parts, laid end to end along the dimension named above; an argument that names none is the same for every part. Nothing has to cross between parts.
Inputs may be any that keep to these rules, and one draw needn't show every extreme that they name: `caption_of`: within each aligned block of 32 rows (the pairs of one index of dp) the values are a permutation of 0 to 31. `images`: image rows are embeddings; no row is zero. `captions`: caption rows are embeddings; no row is zero.
All inputs are finite; a program needn't handle non-finite values.
Results may differ from the reference program's by a relative error of at most 0.03.
Values may be sent and summed in bfloat16 or wider, within the bound.
A program may use at most 128 MiB of HBM per device.

```python
import math
import jax
import jax.numpy as jnp
from jax import lax

D_IMG = 1024
D_TXT = 768
IMG_LM = 16384
TXT_LM = 4096
BLOCK = 32
PAIRS = 128


def paired_draw(key):
    shared = jax.random.normal(jax.random.fold_in(key, 11), (PAIRS, D_IMG), jnp.float32)
    noise = jax.random.normal(jax.random.fold_in(key, 12), (PAIRS, D_TXT), jnp.float32)
    return (jnp.clip(shared, -6.0, 6.0), jnp.clip(noise, -6.0, 6.0))


def pair_order(key):
    block_keys = jax.random.split(jax.random.fold_in(key, 13), PAIRS // BLOCK)
    orders = jax.vmap(lambda single: jax.random.permutation(single, BLOCK))(block_keys)
    return orders.reshape(PAIRS).astype(jnp.int32)


def draw_images(key, part):
    shared, noise = paired_draw(key)
    return shared.astype(jnp.bfloat16)


def draw_captions(key, part):
    shared, noise = paired_draw(key)
    order = pair_order(key)
    values = jnp.clip(0.8 * shared[:, :D_TXT] + 0.6 * noise, -6.0, 6.0)
    target = jnp.arange(PAIRS, dtype=jnp.int32) // BLOCK * BLOCK + order
    placed = jnp.zeros((PAIRS, D_TXT), jnp.float32).at[target].set(values)
    return placed.astype(jnp.bfloat16)


def draw_caption_of(key, part):
    return pair_order(key)


def shard_levels(stream_key, dims, cuts, smallest, largest):
    def one(axis_at, blocks):
        heights = jax.random.uniform(jax.random.fold_in(jax.random.fold_in(stream_key, 6), axis_at), (blocks,), jnp.float32, smallest / len(cuts), largest / len(cuts))
        return jnp.repeat(jnp.exp(heights), dims[axis_at] // blocks).reshape((-1,) + (1,) * (len(dims) - axis_at - 1))

    gain = one(*cuts[0])
    for cut in cuts[1:]:
        gain = gain * one(*cut)
    return gain


def normal_values(rng, dims, scale, reach, shards=(), kind=jnp.bfloat16):
    result = scale * jax.random.normal(rng, dims, jnp.float32)
    if shards:
        result = result * shard_levels(rng, dims, shards, -0.22, 0.18)
    return jnp.clip(result, -reach, reach).astype(kind)


def setup_inputs(seed: int = 0, part: int = 0) -> dict:
    arg_keys = jax.random.split(jax.random.key(seed), 8)
    part_splits = jax.random.split(jax.random.fold_in(arg_keys[7], part), 8)
    return {
        "images": draw_images(jax.random.fold_in(jax.random.fold_in(arg_keys[7], part), 71), part),
        "captions": draw_captions(jax.random.fold_in(jax.random.fold_in(arg_keys[7], part), 71), part),
        "caption_of": draw_caption_of(jax.random.fold_in(jax.random.fold_in(arg_keys[7], part), 71), part),
        "image_landmarks": normal_values(arg_keys[3], (IMG_LM, D_IMG), 1.0, 6.0, ((0, 16),)),
        "image_gamma": jnp.clip(jnp.exp(math.log(40.0) - 1.609438 * jax.random.uniform(arg_keys[4], (IMG_LM,), jnp.float32) ** shard_levels(arg_keys[4], (IMG_LM,), ((0, 16),), -0.2, 0.2)), 8.0, 40.0),
        "text_landmarks": normal_values(arg_keys[5], (TXT_LM, D_TXT), 1.0, 6.0, ((0, 16),)),
        "text_gamma": jnp.clip(jnp.exp(math.log(40.0) - 1.609438 * jax.random.uniform(arg_keys[6], (TXT_LM,), jnp.float32) ** shard_levels(arg_keys[6], (TXT_LM,), ((0, 16),), -0.2, 0.2)), 8.0, 40.0),
    }


def unit_rows(values):
    wide = values.astype(jnp.float32)
    return wide * lax.rsqrt(lax.optimization_barrier(jnp.sum(wide * wide, axis=-1, keepdims=True)) + 1e-06)

def features(left, right):
    inner = lax.dot_general(left, right, (((1,), (1,)), ((), ())), preferred_element_type=jnp.float32)
    return jnp.exp(inner).astype(jnp.bfloat16)

def reference(images, captions, caption_of, image_landmarks, image_gamma, text_landmarks, text_gamma):
    rows_index = jnp.arange(PAIRS, dtype=jnp.int32) // BLOCK * BLOCK + caption_of.astype(jnp.int32)
    paired = jnp.take(captions, rows_index, axis=0)
    image_unit = unit_rows(images).astype(jnp.bfloat16)
    caption_unit = unit_rows(paired).astype(jnp.bfloat16)
    image_keys = (unit_rows(image_landmarks) * image_gamma[:, None]).astype(jnp.bfloat16)
    text_keys = (unit_rows(text_landmarks) * text_gamma[:, None]).astype(jnp.bfloat16)
    image_feats = features(image_unit, image_keys)
    text_feats = features(caption_unit, text_keys)
    image_wide = image_feats.astype(jnp.float32)
    text_wide = text_feats.astype(jnp.float32)
    image_mean = lax.optimization_barrier(jnp.mean(image_wide, axis=0))
    text_mean = lax.optimization_barrier(jnp.mean(text_wide, axis=0))
    image_dev = image_wide - image_mean
    text_dev = text_wide - text_mean
    image_var = lax.optimization_barrier(jnp.mean(image_dev * image_dev, axis=0))
    text_var = lax.optimization_barrier(jnp.mean(text_dev * text_dev, axis=0))
    moment = lax.dot_general(image_feats, text_feats, (((0,), (0,)), ((), ())), preferred_element_type=jnp.float32) / PAIRS
    centred = moment - image_mean[:, None] * text_mean[None, :]
    zstat = math.sqrt(PAIRS) * centred * lax.rsqrt(image_var + 1e-06)[:, None] * lax.rsqrt(text_var + 1e-06)[None, :]
    return (zstat, image_mean, text_mean)
```

```python
import functools
import math

import jax
import jax.numpy as jnp
from jax import lax
from jax.experimental import pallas as pl
from jax.experimental.pallas import tpu as pltpu
from jax.sharding import PartitionSpec as P

MESH = pl.DeviceIdType.MESH
EPS = 1e-06


def unit_rows(wide):
    return wide * lax.rsqrt(jnp.sum(wide * wide, axis=-1, keepdims=True) + EPS)


def diagonal(size):
    return lax.broadcasted_iota(jnp.int32, (size, size), 0) == lax.broadcasted_iota(
        jnp.int32, (size, size), 1
    )


def scaled_keys(marks_ref, gamma_ref, keys_ref):
    total = marks_ref.shape[0]
    size = min(128, total)

    def step(at, carry):
        rows = pl.ds(pl.multiple_of(at * size, size), size)
        unit = unit_rows(marks_ref[rows, :].astype(jnp.float32))
        gamma = jnp.sum(
            jnp.where(diagonal(size), gamma_ref[:, rows], 0.0), axis=1, keepdims=True
        )
        keys_ref[rows, :] = (unit * gamma).astype(jnp.bfloat16)
        return carry

    lax.fori_loop(0, total // size, step, 0)


def standard_features(keys, units, mean_ref, start, scale):
    rows, pairs = keys.shape[0], units.shape[0]
    inner = lax.dot_general(
        keys, units, (((1,), (1,)), ((), ())), preferred_element_type=jnp.float32
    )
    feats = jnp.exp(inner).astype(jnp.bfloat16).astype(jnp.float32)
    mean = jnp.sum(feats, axis=1, keepdims=True) * (1.0 / pairs)
    dev = feats - mean
    var = jnp.sum(dev * dev, axis=1, keepdims=True) * (1.0 / pairs)
    size = min(128, rows)
    for at in range(0, rows, size):
        mean_ref[:, start + at : start + at + size] = jnp.sum(
            jnp.where(diagonal(size), mean[at : at + size], 0.0), axis=0, keepdims=True
        )
    return (dev * (lax.rsqrt(var + EPS) * scale)).astype(jnp.bfloat16)


def exchange_kernel(
    dp, lm, split, chunks, late,
    images_hbm, captions_hbm, order_hbm, marks_hbm, gamma_hbm, words_hbm, text_gamma_hbm,
    f_all, g_all, image_mean_ref, text_mean_ref, relay,
    images_ref, captions_ref, order_ref, marks, gamma_ref, words, text_gamma_ref,
    u_all, c_all, keys, text_keys,
    load_sem,
    u_send, u_recv, u_mate_send, u_mate_recv,
    c_send, c_recv, c_mate_send, c_mate_recv,
    right_send, left_send, f_recv, g_send, g_recv,
):
    me, lane = lax.axis_index("dp"), lax.axis_index("landmark")
    block = images_ref.shape[0]
    part = block // split
    own = marks.shape[0]
    text_own = words.shape[0]
    pairs = u_all.shape[0]
    rows_each = own // chunks

    loads = [
        pltpu.make_async_copy(src, dst, load_sem.at[at])
        for at, (src, dst) in enumerate((
            (images_hbm, images_ref), (marks_hbm, marks), (gamma_hbm, gamma_ref),
            (captions_hbm, captions_ref), (order_hbm, order_ref),
            (words_hbm, words), (text_gamma_hbm, text_gamma_ref),
        ))
    ]
    for load in loads:
        load.start()

    barrier = pltpu.get_barrier_semaphore()
    for k in range(1, dp):
        pl.semaphore_signal(
            barrier, inc=1, device_id={"dp": lax.rem(me + k, dp)}, device_id_type=MESH
        )
    for k in range(1, lm):
        pl.semaphore_signal(
            barrier, inc=1, device_id={"landmark": lax.rem(lane + k, lm)}, device_id_type=MESH
        )

    mine = pl.ds(pl.multiple_of(me * block, block), block)
    loads[0].wait()
    u_all[mine, :] = unit_rows(images_ref[...].astype(jnp.float32)).astype(jnp.bfloat16)
    pl.semaphore_wait(barrier, dp - 1 + lm - 1)

    side = lax.rem(lane, split)
    mate = lane + 1 - 2 * side

    def half(shard):
        return pl.ds(pl.multiple_of(shard * block + side * part, part), part)

    def other_half(shard):
        return pl.ds(pl.multiple_of(shard * block + (1 - side) * part, part), part)

    def block_copy(buf, send, recv, k, shard, target):
        return pltpu.make_async_remote_copy(
            src_ref=buf.at[half(shard), :], dst_ref=buf.at[half(shard), :],
            send_sem=send.at[k], recv_sem=recv.at[shard],
            device_id={"dp": target}, device_id_type=MESH,
        )

    def mate_copy(buf, send, recv, k, shard, rows):
        return pltpu.make_async_remote_copy(
            src_ref=buf.at[rows, :], dst_ref=buf.at[rows, :],
            send_sem=send.at[k], recv_sem=recv.at[shard],
            device_id={"landmark": mate}, device_id_type=MESH,
        )

    sends = []

    def spread(buf, send, recv):
        for k in range(1, dp):
            copy = block_copy(buf, send, recv, k - 1, me, lax.rem(me + k, dp))
            copy.start()
            sends.append(copy)

    spread(u_all, u_send, u_recv)

    def collect(buf, send, recv, mate_send, mate_recv):
        for k in range(1, dp):
            shard = lax.rem(me + dp - k, dp)
            block_copy(buf, send, recv, k - 1, shard, me).wait_recv()
            if split > 1:
                copy = mate_copy(buf, mate_send, mate_recv, k - 1, shard, half(shard))
                copy.start()
                sends.append(copy)
        if split > 1:
            for k in range(1, dp):
                shard = lax.rem(me + dp - k, dp)
                mate_copy(
                    buf, mate_send, mate_recv, k - 1, shard, other_half(shard)
                ).wait_recv()

    loads[3].wait()
    loads[4].wait()
    picks = (
        lax.broadcasted_iota(jnp.int32, (block, block), 0) == order_ref[...]
    ).astype(jnp.bfloat16)
    paired = lax.dot_general(
        picks, captions_ref[...], (((0,), (0,)), ((), ())), preferred_element_type=jnp.float32
    )
    c_all[mine, :] = unit_rows(paired).astype(jnp.bfloat16)
    spread(c_all, c_send, c_recv)
    loads[1].wait()
    loads[2].wait()
    scaled_keys(marks, gamma_ref, keys)
    def f_rows(shard, c):
        return pl.ds(pl.multiple_of(shard * own + c * rows_each, rows_each), rows_each)

    def hop(shard, c, send, target):
        return pltpu.make_async_remote_copy(
            src_ref=f_all.at[f_rows(shard, c), :], dst_ref=f_all.at[f_rows(shard, c), :],
            send_sem=send.at[shard, c], recv_sem=f_recv.at[shard, c],
            device_id={"dp": target}, device_id_type=MESH,
        )

    def to_right(shard, c):
        return hop(shard, c, right_send, jnp.minimum(me + 1, dp - 1))

    def to_left(shard, c):
        return hop(shard, c, left_send, jnp.maximum(me - 1, 0))

    collect(u_all, u_send, u_recv, u_mate_send, u_mate_recv)
    for c in range(chunks):
        at = c * rows_each
        f_all[f_rows(me, c), :] = standard_features(
            keys[at : at + rows_each, :], u_all[...], image_mean_ref, at, 1.0
        )

        @pl.when(me < dp - 1)
        def _():
            to_right(me, c).start()

        @pl.when(me > 0)
        def _():
            to_left(me, c).start()

    loads[5].wait()
    loads[6].wait()
    scaled_keys(words, text_gamma_ref, text_keys)
    collect(c_all, c_send, c_recv, c_mate_send, c_mate_recv)
    text_mine = pl.ds(pl.multiple_of(lane * text_own, text_own), text_own)
    g_all[text_mine, :] = standard_features(
        text_keys[...], c_all[...], text_mean_ref, 0, 1.0 / math.sqrt(pairs)
    )

    def g_copy(k, shard, target):
        rows = pl.ds(pl.multiple_of(shard * text_own, text_own), text_own)
        return pltpu.make_async_remote_copy(
            src_ref=g_all.at[rows, :], dst_ref=g_all.at[rows, :],
            send_sem=g_send.at[k], recv_sem=g_recv.at[shard],
            device_id={"landmark": target}, device_id_type=MESH,
        )

    for k in range(1, lm):
        copy = g_copy(k - 1, lane, lax.rem(lane + k, lm))
        copy.start()
        sends.append(copy)

    hops = dp - 2 if late else dp - 1
    for d in range(1, hops + 1):
        for c in range(chunks):

            @pl.when(me - d >= 0)
            def _():
                to_left(me - d, c).wait_recv()
                if d < hops:

                    @pl.when(me < dp - 1)
                    def _():
                        to_right(me - d, c).start()

            @pl.when(me + d < dp)
            def _():
                to_right(me + d, c).wait_recv()
                if d < hops:

                    @pl.when(me > 0)
                    def _():
                        to_left(me + d, c).start()

            if late and d == hops:
                at = pl.ds(c * rows_each, rows_each)

                @pl.when(me == dp - 2)
                def _():
                    relay[at, :] = f_all[f_rows(0, c), :]

                @pl.when(me == 1)
                def _():
                    relay[at, :] = f_all[f_rows(dp - 1, c), :]

    for k in range(1, lm):
        shard = lax.rem(lane + lm - k, lm)
        g_copy(k - 1, shard, lane).wait_recv()

    for copy in sends:
        copy.wait_send()
    for shard in range(dp):
        for c in range(chunks):

            @pl.when(jnp.logical_and(shard <= me, me < jnp.minimum(dp - 1, shard + hops)))
            def _():
                to_right(shard, c).wait_send()

            @pl.when(jnp.logical_and(shard >= me, me > jnp.maximum(0, shard - hops)))
            def _():
                to_left(shard, c).wait_send()


def product_kernel(
    tile, slots, dp, late, f_ref, g_ref, image_mean_in, text_mean_in,
    z_hbm, image_mean_ref, text_mean_ref, buf, sem,
):
    own = f_ref.shape[0] // dp
    steps = (f_ref.shape[0] - late * own) // tile
    first = jnp.where(lax.axis_index("dp") == 0, 0, own) if late else 0

    def rows(at):
        return pl.ds(pl.multiple_of(first + at * tile, tile), tile)

    def out(at):
        slot = lax.rem(at, slots)
        return pltpu.make_async_copy(buf.at[slot], z_hbm.at[rows(at), :], sem.at[slot])

    def step(at, carry):
        @pl.when(at >= slots)
        def _():
            out(at - slots).wait()

        buf[lax.rem(at, slots)] = lax.dot_general(
            f_ref[rows(at), :], g_ref[...], (((1,), (1,)), ((), ())),
            preferred_element_type=jnp.float32,
        )
        out(at).start()
        return carry

    lax.fori_loop(0, steps, step, 0)
    image_mean_ref[...] = image_mean_in[...]
    text_mean_ref[...] = text_mean_in[...]
    for at in range(max(0, steps - slots), steps):
        out(jnp.int32(at)).wait()


def late_kernel(tile, dp, f_ref, got_ref, g_ref, z_in, z_hbm, buf, sem):
    me = lax.axis_index("dp")
    own = got_ref.shape[0]
    first = jnp.where(me == 0, (dp - 1) * own, 0)
    inner = jnp.logical_and(me > 0, me < dp - 1)

    def out(at):
        rows = pl.ds(pl.multiple_of(first + at * tile, tile), tile)
        return pltpu.make_async_copy(buf.at[at], z_hbm.at[rows, :], sem.at[at])

    for at in range(own // tile):
        rows = pl.ds(at * tile, tile)
        mine = f_ref[pl.ds(pl.multiple_of(first + at * tile, tile), tile), :]
        buf[at] = lax.dot_general(
            jnp.where(inner, mine, got_ref[rows, :]), g_ref[...],
            (((1,), (1,)), ((), ())), preferred_element_type=jnp.float32,
        )
        out(at).start()
    for at in range(own // tile):
        out(at).wait()


def per_device(
    images, captions, caption_of, image_landmarks, image_gamma, text_landmarks, text_gamma
):
    dp, lm = lax.axis_size("dp"), lax.axis_size("landmark")
    block, width = images.shape
    text_width = captions.shape[1]
    own, text_own = image_landmarks.shape[0], text_landmarks.shape[0]
    pairs = block * dp
    split = 2 if lm % 2 == 0 else 1
    chunks = max(1, own // 256)
    late = dp >= 4
    bf16, f32 = jnp.bfloat16, jnp.float32
    vmem = pl.BlockSpec(memory_space=pltpu.VMEM)
    hbm = pl.BlockSpec(memory_space=pltpu.HBM)
    dma = pltpu.SemaphoreType.DMA
    f, g, image_mean, text_mean, relay = pl.pallas_call(
        functools.partial(exchange_kernel, dp, lm, split, chunks, late),
        out_shape=(
            jax.ShapeDtypeStruct((dp * own, pairs), bf16),
            jax.ShapeDtypeStruct((lm * text_own, pairs), bf16),
            jax.ShapeDtypeStruct((1, own), f32),
            jax.ShapeDtypeStruct((1, text_own), f32),
            jax.ShapeDtypeStruct((own, pairs), bf16),
        ),
        in_specs=[hbm] * 7,
        out_specs=(vmem, vmem, vmem, vmem, vmem),
        scratch_shapes=[
            pltpu.VMEM((block, width), bf16),
            pltpu.VMEM((block, text_width), bf16),
            pltpu.VMEM((1, block), jnp.int32),
            pltpu.VMEM((own, width), bf16),
            pltpu.VMEM((1, own), f32),
            pltpu.VMEM((text_own, text_width), bf16),
            pltpu.VMEM((1, text_own), f32),
            pltpu.VMEM((pairs, width), bf16),
            pltpu.VMEM((pairs, text_width), bf16),
            pltpu.VMEM((own, width), bf16),
            pltpu.VMEM((text_own, text_width), bf16),
            dma((7,)),
            dma((dp,)), dma((dp,)), dma((dp,)), dma((dp,)),
            dma((dp,)), dma((dp,)), dma((dp,)), dma((dp,)),
            dma((dp, chunks)), dma((dp, chunks)), dma((dp, chunks)),
            dma((lm,)), dma((lm,)),
        ],
        compiler_params=pltpu.CompilerParams(
            collective_id=0, has_side_effects=True, vmem_limit_bytes=40 * 2**20
        ),
        name="exchange",
    )(
        *(
            pltpu.with_memory_space_constraint(value, pltpu.HBM)
            for value in (
                images, captions, caption_of[None, :], image_landmarks, image_gamma[None, :],
                text_landmarks, text_gamma[None, :],
            )
        )
    )
    rows, columns = dp * own, lm * text_own
    tile = math.gcd(own, 256)
    ahead = rows - late * own
    slots = min(4, ahead // tile)
    if late:
        got = lax.ppermute(relay, "dp", ((dp - 2, dp - 1), (1, 0)))
    zstat, image_mean, text_mean = pl.pallas_call(
        functools.partial(product_kernel, tile, slots, dp, late),
        out_shape=(
            jax.ShapeDtypeStruct((rows, columns), f32),
            jax.ShapeDtypeStruct((1, own), f32),
            jax.ShapeDtypeStruct((1, text_own), f32),
        ),
        in_specs=[vmem] * 4,
        out_specs=(hbm, vmem, vmem),
        scratch_shapes=[pltpu.VMEM((slots, tile, columns), f32), dma((slots,))],
        compiler_params=pltpu.CompilerParams(vmem_limit_bytes=40 * 2**20),
        cost_estimate=pl.CostEstimate(
            flops=2 * ahead * columns * pairs, bytes_accessed=4 * ahead * columns, transcendentals=0
        ),
        name="product",
    )(f, g, image_mean, text_mean)
    if late:
        zstat = pl.pallas_call(
            functools.partial(late_kernel, tile, dp),
            out_shape=jax.ShapeDtypeStruct((rows, columns), f32),
            in_specs=[vmem, vmem, vmem, hbm],
            out_specs=hbm,
            scratch_shapes=[pltpu.VMEM((own // tile, tile, columns), f32), dma((own // tile,))],
            input_output_aliases={3: 0},
            compiler_params=pltpu.CompilerParams(vmem_limit_bytes=40 * 2**20),
            cost_estimate=pl.CostEstimate(
                flops=2 * own * columns * pairs, bytes_accessed=4 * own * columns, transcendentals=0
            ),
            name="late_product",
        )(f, got, g, zstat)
    return (zstat, image_mean[0], text_mean[0])


def solution(mesh):
    in_specs = (
        P(("groups", "dp"), None),
        P(("groups", "dp"), None),
        P(("groups", "dp")),
        P(("landmark", "dp"), None),
        P(("landmark", "dp")),
        P(("dp", "landmark"), None),
        P(("dp", "landmark")),
    )
    out_specs = (
        P(("groups", "landmark"), "dp"),
        P(("groups", "landmark", "dp")),
        P(("groups", "dp", "landmark")),
    )
    return jax.shard_map(
        per_device, mesh=mesh, in_specs=in_specs, out_specs=out_specs, check_vma=False
    )
```

```python
import functools
import math

import jax
import jax.numpy as jnp
from jax import lax
from jax.experimental import pallas as pl
from jax.experimental.pallas import tpu as pltpu
from jax.sharding import PartitionSpec as P

MESH = pl.DeviceIdType.MESH
EPS = 1e-06
LATE = 4
U_WAYS = 2
C_WAYS = 4


def unit_rows(wide):
    return wide * lax.rsqrt(jnp.sum(wide * wide, axis=-1, keepdims=True) + EPS)


def diagonal(size):
    return lax.broadcasted_iota(jnp.int32, (size, size), 0) == lax.broadcasted_iota(
        jnp.int32, (size, size), 1
    )


def scaled_keys(marks_ref, gamma_ref, keys_ref):
    total = marks_ref.shape[0]
    size = min(128, total)

    def step(at, carry):
        rows = pl.ds(pl.multiple_of(at * size, size), size)
        unit = unit_rows(marks_ref[rows, :].astype(jnp.float32))
        gamma = jnp.sum(
            jnp.where(diagonal(size), gamma_ref[:, rows], 0.0), axis=1, keepdims=True
        )
        keys_ref[rows, :] = (unit * gamma).astype(jnp.bfloat16)
        return carry

    lax.fori_loop(0, total // size, step, 0)


def standard_features(keys, units, mean_ref, start, scale):
    rows, pairs = keys.shape[0], units.shape[0]
    inner = lax.dot_general(
        keys, units, (((1,), (1,)), ((), ())), preferred_element_type=jnp.float32
    )
    feats = jnp.exp(inner).astype(jnp.bfloat16).astype(jnp.float32)
    mean = jnp.sum(feats, axis=1, keepdims=True) * (1.0 / pairs)
    dev = feats - mean
    var = jnp.sum(dev * dev, axis=1, keepdims=True) * (1.0 / pairs)
    size = min(128, rows)
    for at in range(0, rows, size):
        mean_ref[:, start + at : start + at + size] = jnp.sum(
            jnp.where(diagonal(size), mean[at : at + size], 0.0), axis=0, keepdims=True
        )
    return (dev * (lax.rsqrt(var + EPS) * scale)).astype(jnp.bfloat16)


def exchange_kernel(
    dp, lm, split, chunks,
    images_hbm, captions_hbm, order_hbm, marks_hbm, gamma_hbm, words_hbm, text_gamma_hbm,
    f_all, g_all, image_mean_ref, text_mean_ref,
    images_ref, captions_ref, order_ref, marks, gamma_ref, words, text_gamma_ref,
    u_all, c_all, keys, text_keys,
    load_sem,
    u_send, u_recv, u_mate_send, u_mate_recv,
    c_send, c_recv, c_mate_send, c_mate_recv,
    right_send, left_send, f_recv, g_send, g_recv,
):
    me, lane = lax.axis_index("dp"), lax.axis_index("landmark")
    block = images_ref.shape[0]
    part = block // split
    own = marks.shape[0]
    text_own = words.shape[0]
    pairs = u_all.shape[0]
    rows_each = own // chunks

    loads = [
        pltpu.make_async_copy(src, dst, load_sem.at[at])
        for at, (src, dst) in enumerate((
            (images_hbm, images_ref), (marks_hbm, marks), (gamma_hbm, gamma_ref),
            (captions_hbm, captions_ref), (order_hbm, order_ref),
            (words_hbm, words), (text_gamma_hbm, text_gamma_ref),
        ))
    ]
    for load in loads:
        load.start()

    barrier = pltpu.get_barrier_semaphore()
    for k in range(1, dp):
        pl.semaphore_signal(
            barrier, inc=1, device_id={"dp": lax.rem(me + k, dp)}, device_id_type=MESH
        )
    for k in range(1, lm):
        pl.semaphore_signal(
            barrier, inc=1, device_id={"landmark": lax.rem(lane + k, lm)}, device_id_type=MESH
        )

    mine = pl.ds(pl.multiple_of(me * block, block), block)
    loads[0].wait()
    u_all[mine, :] = unit_rows(images_ref[...].astype(jnp.float32)).astype(jnp.bfloat16)
    pl.semaphore_wait(barrier, dp - 1 + lm - 1)

    side = lax.rem(lane, split)
    mate = lane + 1 - 2 * side

    def half(shard):
        return pl.ds(pl.multiple_of(shard * block + side * part, part), part)

    def other_half(shard):
        return pl.ds(pl.multiple_of(shard * block + (1 - side) * part, part), part)

    def block_copy(buf, send, recv, k, shard, target):
        return pltpu.make_async_remote_copy(
            src_ref=buf.at[half(shard), :], dst_ref=buf.at[half(shard), :],
            send_sem=send.at[k], recv_sem=recv.at[shard],
            device_id={"dp": target}, device_id_type=MESH,
        )

    def mate_copy(buf, send, recv, k, shard, rows):
        return pltpu.make_async_remote_copy(
            src_ref=buf.at[rows, :], dst_ref=buf.at[rows, :],
            send_sem=send.at[k], recv_sem=recv.at[shard],
            device_id={"landmark": mate}, device_id_type=MESH,
        )

    sends = []

    def spread(buf, send, recv):
        for k in range(1, dp):
            copy = block_copy(buf, send, recv, k - 1, me, lax.rem(me + k, dp))
            copy.start()
            sends.append(copy)

    spread(u_all, u_send, u_recv)

    def collect(buf, send, recv, mate_send, mate_recv):
        for k in range(1, dp):
            shard = lax.rem(me + dp - k, dp)
            block_copy(buf, send, recv, k - 1, shard, me).wait_recv()
            if split > 1:
                copy = mate_copy(buf, mate_send, mate_recv, k - 1, shard, half(shard))
                copy.start()
                sends.append(copy)
        if split > 1:
            for k in range(1, dp):
                shard = lax.rem(me + dp - k, dp)
                mate_copy(
                    buf, mate_send, mate_recv, k - 1, shard, other_half(shard)
                ).wait_recv()

    loads[3].wait()
    loads[4].wait()
    picks = (
        lax.broadcasted_iota(jnp.int32, (block, block), 0) == order_ref[...]
    ).astype(jnp.bfloat16)
    paired = lax.dot_general(
        picks, captions_ref[...], (((0,), (0,)), ((), ())), preferred_element_type=jnp.float32
    )
    c_all[mine, :] = unit_rows(paired).astype(jnp.bfloat16)
    spread(c_all, c_send, c_recv)
    loads[1].wait()
    loads[2].wait()
    scaled_keys(marks, gamma_ref, keys)
    def f_rows(shard, c):
        return pl.ds(pl.multiple_of(shard * own + c * rows_each, rows_each), rows_each)

    def hop(shard, c, send, target):
        return pltpu.make_async_remote_copy(
            src_ref=f_all.at[f_rows(shard, c), :], dst_ref=f_all.at[f_rows(shard, c), :],
            send_sem=send.at[shard, c], recv_sem=f_recv.at[shard, c],
            device_id={"dp": target}, device_id_type=MESH,
        )

    def to_right(shard, c):
        return hop(shard, c, right_send, jnp.minimum(me + 1, dp - 1))

    def to_left(shard, c):
        return hop(shard, c, left_send, jnp.maximum(me - 1, 0))

    collect(u_all, u_send, u_recv, u_mate_send, u_mate_recv)
    for c in range(chunks):
        at = c * rows_each
        f_all[f_rows(me, c), :] = standard_features(
            keys[at : at + rows_each, :], u_all[...], image_mean_ref, at, 1.0
        )

        @pl.when(me < dp - 1)
        def _():
            to_right(me, c).start()

        @pl.when(me > 0)
        def _():
            to_left(me, c).start()

    loads[5].wait()
    loads[6].wait()
    scaled_keys(words, text_gamma_ref, text_keys)
    collect(c_all, c_send, c_recv, c_mate_send, c_mate_recv)
    text_mine = pl.ds(pl.multiple_of(lane * text_own, text_own), text_own)
    g_all[text_mine, :] = standard_features(
        text_keys[...], c_all[...], text_mean_ref, 0, 1.0 / math.sqrt(pairs)
    )

    def g_copy(k, shard, target):
        rows = pl.ds(pl.multiple_of(shard * text_own, text_own), text_own)
        return pltpu.make_async_remote_copy(
            src_ref=g_all.at[rows, :], dst_ref=g_all.at[rows, :],
            send_sem=g_send.at[k], recv_sem=g_recv.at[shard],
            device_id={"landmark": target}, device_id_type=MESH,
        )

    for k in range(1, lm):
        copy = g_copy(k - 1, lane, lax.rem(lane + k, lm))
        copy.start()
        sends.append(copy)

    for d in range(1, dp):
        for c in range(chunks):

            @pl.when(me - d >= 0)
            def _():
                to_left(me - d, c).wait_recv()

                @pl.when(me < dp - 1)
                def _():
                    to_right(me - d, c).start()

            @pl.when(me + d < dp)
            def _():
                to_right(me + d, c).wait_recv()

                @pl.when(me > 0)
                def _():
                    to_left(me + d, c).start()

    for k in range(1, lm):
        shard = lax.rem(lane + lm - k, lm)
        g_copy(k - 1, shard, lane).wait_recv()

    for copy in sends:
        copy.wait_send()
    for shard in range(dp):
        for c in range(chunks):

            @pl.when(jnp.logical_and(shard <= me, me < dp - 1))
            def _():
                to_right(shard, c).wait_send()

            @pl.when(jnp.logical_and(shard >= me, me > 0))
            def _():
                to_left(shard, c).wait_send()


def near_first(shard):
    return (
        shard,
        shard + 1 - 2 * lax.rem(shard, 2),
        2 - shard // 2,
        3 - 3 * (shard // 2),
    )


def aligned(start, size):
    return pl.ds(pl.multiple_of(start, size), size)


def standard_columns(feats, scale):
    pairs = feats.shape[0]
    mean = jnp.sum(feats, axis=0, keepdims=True) * (1.0 / pairs)
    dev = feats - mean
    var = jnp.sum(dev * dev, axis=0, keepdims=True) * (1.0 / pairs)
    return jnp.transpose(dev * (lax.rsqrt(var + EPS) * scale)).astype(jnp.bfloat16), mean


def blocks_kernel(
    late,
    images_hbm, captions_hbm, order_hbm, marks_hbm, gamma_hbm, words_hbm, text_gamma_hbm,
    f_all, g_all, image_mean_ref, text_mean_ref, relay,
    images_ref, captions_ref, order_ref, marks, gamma_ref, words, text_gamma_ref,
    u_all, c_all, keys, text_keys, raw,
    load_sem, mark_sem, u_sems, c_sems,
    right_send, left_send, f_recv, g_send, g_recv,
):
    dp, lm, cuts = 4, 4, 4
    me, lane = lax.axis_index("dp"), lax.axis_index("landmark")
    block = images_ref.shape[0]
    part = block // 2
    own = marks.shape[0]
    text_own = words.shape[0]
    pairs = block * dp
    piece = own // cuts

    loads = [
        pltpu.make_async_copy(src, dst, load_sem.at[at])
        for at, (src, dst) in enumerate((
            (images_hbm, images_ref), (captions_hbm, captions_ref), (order_hbm, order_ref),
            (gamma_hbm, gamma_ref), (words_hbm, words), (text_gamma_hbm, text_gamma_ref),
        ))
    ]
    mark_loads = [
        pltpu.make_async_copy(
            marks_hbm.at[pl.ds(at * piece, piece), :], marks.at[pl.ds(at * piece, piece), :],
            mark_sem.at[at],
        )
        for at in range(cuts)
    ]
    for load in loads[:4] + mark_loads + loads[4:]:
        load.start()

    barrier = pltpu.get_barrier_semaphore()
    for k in range(1, dp):
        pl.semaphore_signal(
            barrier, inc=1, device_id={"dp": lax.rem(me + k, dp)}, device_id_type=MESH
        )
    for k in range(1, lm):
        pl.semaphore_signal(
            barrier, inc=1, device_id={"landmark": lax.rem(lane + k, lm)}, device_id_type=MESH
        )

    half, core = lane // 2, lax.rem(lane, 2)
    mate = lane + 1 - 2 * core
    across = lax.rem(lane + 2, lm)
    order = near_first(me)
    mine = aligned(me * block, block)
    sends = []

    def launch(copy):
        copy.start()
        sends.append(copy)

    def portion(buf, sems, stage, k, shard, h, side, device):
        wide = buf.shape[1] // 2
        columns = pl.ds(0, 2 * wide) if h is None else aligned(h * wide, wide)
        ref = buf.at[aligned(shard * block + side * part, part), columns]
        return pltpu.make_async_remote_copy(
            src_ref=ref, dst_ref=ref, send_sem=sems.at[0, stage, k],
            recv_sem=sems.at[1, stage, shard], device_id=device, device_id_type=MESH,
        )

    def z_copy(buf, sems, ways, k, shard):
        h = half if ways == 4 else None
        return portion(buf, sems, 0, k, shard, h, core, {"dp": order[k]})

    def x_copy(buf, sems, k, h):
        return portion(buf, sems, 1, k, order[k], h, core, {"landmark": across})

    def mate_copy(buf, sems, stage, k, h, side):
        return portion(buf, sems, stage, k, order[k], h, side, {"landmark": mate})

    def spread(buf, sems, ways):
        for k in range(1, dp):
            launch(z_copy(buf, sems, ways, k, me))

    def pass_on(buf, sems, ways):
        for k in range(1, dp):
            z_copy(buf, sems, ways, k, order[k]).wait_recv()
            h = half if ways == 4 else None
            if ways == 4:
                launch(x_copy(buf, sems, k, h))
            launch(mate_copy(buf, sems, 2, k, h, core))

    def pass_across(buf, sems, ways):
        if ways == 4:
            for k in range(1, dp):
                x_copy(buf, sems, k, 1 - half).wait_recv()
                launch(mate_copy(buf, sems, 3, k, 1 - half, core))

    def gather(buf, sems, ways):
        for k in range(1, dp):
            if ways == 4:
                mate_copy(buf, sems, 2, k, half, 1 - core).wait_recv()
                mate_copy(buf, sems, 3, k, 1 - half, 1 - core).wait_recv()
            else:
                mate_copy(buf, sems, 2, k, None, 1 - core).wait_recv()

    loads[0].wait()
    u_all[mine, :] = unit_rows(images_ref[...].astype(jnp.float32)).astype(jnp.bfloat16)
    pl.semaphore_wait(barrier, dp - 1 + lm - 1)
    spread(u_all, u_sems, U_WAYS)
    loads[1].wait()
    loads[2].wait()
    picks = (
        lax.broadcasted_iota(jnp.int32, (block, block), 0) == order_ref[...]
    ).astype(jnp.bfloat16)
    paired = lax.dot_general(
        picks, captions_ref[...], (((0,), (0,)), ((), ())), preferred_element_type=jnp.float32
    )
    c_all[mine, :] = unit_rows(paired).astype(jnp.bfloat16)

    loads[3].wait()
    for at in range(cuts):
        mark_loads[at].wait()
        rows = pl.ds(at * piece, piece)
        scaled_keys(marks.at[rows, :], gamma_ref.at[:, rows], keys.at[rows, :])

    def hop(shard, j, send, target, rows):
        if j == 0:
            ref = raw.at[shard, pl.ds(0, block), pl.ds(0, rows)]
        else:
            ref = raw.at[shard, pl.ds(block, pairs - block), pl.ds((j - 1) * piece, piece)]
        return pltpu.make_async_remote_copy(
            src_ref=ref, dst_ref=ref,
            send_sem=send.at[shard, j], recv_sem=f_recv.at[shard, j],
            device_id={"dp": target}, device_id_type=MESH,
        )

    def to_right(shard, j, rows=own):
        return hop(shard, j, right_send, jnp.minimum(me + 1, dp - 1), rows)

    def to_left(shard, j, rows=own):
        return hop(shard, j, left_send, jnp.maximum(me - 1, 0), rows)

    def send_own(j):
        @pl.when(me < dp - 1)
        def _():
            to_right(me, j).start()

        @pl.when(me > 0)
        def _():
            to_left(me, j).start()

    def features(units, rows):
        inner = lax.dot_general(
            units, keys[rows, :], (((1,), (1,)), ((), ())), preferred_element_type=jnp.float32
        )
        return jnp.exp(inner).astype(jnp.bfloat16)

    raw[me, :block, :] = features(u_all[mine, :], pl.ds(0, own))
    send_own(0)
    spread(c_all, c_sems, C_WAYS)
    loads[4].wait()
    loads[5].wait()
    scaled_keys(words, text_gamma_ref, text_keys)
    pass_on(u_all, u_sems, U_WAYS)
    pass_across(u_all, u_sems, U_WAYS)
    gather(u_all, u_sems, U_WAYS)
    others = jnp.concatenate(
        [u_all[aligned(lax.rem(me + k, dp) * block, block), :] for k in range(1, dp)], axis=0
    )
    for j in range(1, cuts + 1):
        rows = pl.ds((j - 1) * piece, piece)
        raw[me, block:, (j - 1) * piece : j * piece] = features(others, rows)
        send_own(j)
        if j == 1:
            pass_on(c_all, c_sems, C_WAYS)

    hops = dp - 2 if late == cuts else dp - 1
    early_rows = own - late * piece

    def rows_of(d):
        return early_rows if d == dp - 1 else own

    def last_of(d):
        return cuts - late if d == dp - 1 else cuts

    def receive(d, j):
        @pl.when(me - d >= 0)
        def _():
            to_left(me - d, j, rows_of(d)).wait_recv()
            if d < hops and j <= last_of(d + 1):

                @pl.when(me < dp - 1)
                def _():
                    to_right(me - d, j, rows_of(d + 1)).start()

        @pl.when(me + d < dp)
        def _():
            to_right(me + d, j, rows_of(d)).wait_recv()
            if d < hops and j <= last_of(d + 1):

                @pl.when(me > 0)
                def _():
                    to_left(me + d, j, rows_of(d + 1)).start()

    def standardize(shard, j, mean_ref=None):
        for at in range((j - 1) * piece, j * piece, 128):
            columns = slice(at, at + 128)
            feats = jnp.concatenate(
                [
                    raw[shard, aligned(lax.rem(p - shard + dp, dp) * block, block), columns]
                    for p in range(dp)
                ],
                axis=0,
            )
            rows, mean = standard_columns(feats.astype(jnp.float32), 1.0)
            f_all[aligned(shard * own + at, 128), :] = rows
            if mean_ref is not None:
                mean_ref[:, columns] = mean

    receive(1, 0)
    pass_across(c_all, c_sems, C_WAYS)
    for j in range(1, cuts + 1):
        standardize(me, j, image_mean_ref)
    receive(1, 1)
    gather(c_all, c_sems, C_WAYS)
    inner = lax.dot_general(
        c_all[...], text_keys[...], (((1,), (1,)), ((), ())), preferred_element_type=jnp.float32
    )
    rows, text_mean_ref[...] = standard_columns(
        jnp.exp(inner).astype(jnp.bfloat16).astype(jnp.float32), 1.0 / math.sqrt(pairs)
    )
    g_all[aligned(lane * text_own, text_own), :] = rows

    def g_copy(k, shard, target):
        rows = aligned(shard * text_own, text_own)
        return pltpu.make_async_remote_copy(
            src_ref=g_all.at[rows, :], dst_ref=g_all.at[rows, :],
            send_sem=g_send.at[k], recv_sem=g_recv.at[shard],
            device_id={"landmark": target}, device_id_type=MESH,
        )

    for k in range(1, lm):
        launch(g_copy(k - 1, lane, lax.rem(lane + k, lm)))

    for d in range(1, hops + 1):
        for j in range(1 if d == 1 else 0, last_of(d) + 1):
            if d > 1 or j > 1:
                receive(d, j)
            if j:

                @pl.when(me - d >= 0)
                def _():
                    standardize(me - d, j)

                @pl.when(me + d < dp)
                def _():
                    standardize(me + d, j)

            if d == dp - 2 and j > cuts - late:
                at = (j - 1) * piece
                rows = pl.ds(at - early_rows, piece)

                @pl.when(me == dp - 2)
                def _():
                    relay[rows, :] = f_all[pl.ds(at, piece), :]

                @pl.when(me == 1)
                def _():
                    relay[rows, :] = f_all[pl.ds((dp - 1) * own + at, piece), :]

    for k in range(1, lm):
        shard = lax.rem(lane + lm - k, lm)
        g_copy(k - 1, shard, lane).wait_recv()
    for copy in sends:
        copy.wait_send()
    for shard in range(dp):
        for d in range(hops):
            for j in range(last_of(d + 1) + 1):

                @pl.when(jnp.logical_and(me == shard + d, me < dp - 1))
                def _():
                    to_right(shard, j, rows_of(d + 1)).wait_send()

                @pl.when(jnp.logical_and(me == shard - d, me > 0))
                def _():
                    to_left(shard, j, rows_of(d + 1)).wait_send()


def product_kernel(
    tile, slots, dp, late_rows, f_ref, g_ref, image_mean_in, text_mean_in,
    z_hbm, image_mean_ref, text_mean_ref, buf, sem,
):
    total = f_ref.shape[0]
    steps = (total - late_rows) // tile
    edge = total // dp - late_rows

    def rows(at):
        start = at * tile
        if late_rows:
            skip = jnp.logical_and(lax.axis_index("dp") > 0, start >= edge)
            start = start + jnp.where(skip, late_rows, 0)
        return pl.ds(pl.multiple_of(start, tile), tile)

    def out(at):
        slot = lax.rem(at, slots)
        return pltpu.make_async_copy(buf.at[slot], z_hbm.at[rows(at), :], sem.at[slot])

    def step(at, carry):
        @pl.when(at >= slots)
        def _():
            out(at - slots).wait()

        buf[lax.rem(at, slots)] = lax.dot_general(
            f_ref[rows(at), :], g_ref[...], (((1,), (1,)), ((), ())),
            preferred_element_type=jnp.float32,
        )
        out(at).start()
        return carry

    lax.fori_loop(0, steps, step, 0)
    image_mean_ref[...] = image_mean_in[...]
    text_mean_ref[...] = text_mean_in[...]
    for at in range(max(0, steps - slots), steps):
        out(jnp.int32(at)).wait()


def late_kernel(tile, dp, f_ref, got_ref, g_ref, z_in, z_hbm, buf, sem):
    me = lax.axis_index("dp")
    late_rows = got_ref.shape[0]
    own = f_ref.shape[0] // dp
    first = jnp.where(me == 0, dp * own, own) - late_rows
    inner = jnp.logical_and(me > 0, me < dp - 1)

    def rows(at):
        return pl.ds(pl.multiple_of(first + at * tile, tile), tile)

    def out(at):
        return pltpu.make_async_copy(buf.at[at], z_hbm.at[rows(at), :], sem.at[at])

    for at in range(late_rows // tile):
        buf[at] = lax.dot_general(
            jnp.where(inner, f_ref[rows(at), :], got_ref[pl.ds(at * tile, tile), :]),
            g_ref[...], (((1,), (1,)), ((), ())), preferred_element_type=jnp.float32,
        )
        out(at).start()
    for at in range(late_rows // tile):
        out(at).wait()


def per_device(
    images, captions, caption_of, image_landmarks, image_gamma, text_landmarks, text_gamma
):
    dp, lm = lax.axis_size("dp"), lax.axis_size("landmark")
    block, width = images.shape
    text_width = captions.shape[1]
    own, text_own = image_landmarks.shape[0], text_landmarks.shape[0]
    pairs = block * dp
    bf16, f32 = jnp.bfloat16, jnp.float32
    vmem = pl.BlockSpec(memory_space=pltpu.VMEM)
    hbm = pl.BlockSpec(memory_space=pltpu.HBM)
    dma = pltpu.SemaphoreType.DMA
    blocks = (
        dp == 4 and lm == 4 and block % 32 == 0 and own % 512 == 0 and text_own % 128 == 0
        and width % 256 == 0 and text_width % 256 == 0
    )
    late_rows = own * LATE // 4 if blocks else 0
    operands = [
        pltpu.with_memory_space_constraint(value, pltpu.HBM)
        for value in (
            images, captions, caption_of[None, :], image_landmarks, image_gamma[None, :],
            text_landmarks, text_gamma[None, :],
        )
    ]
    results = [
        jax.ShapeDtypeStruct((dp * own, pairs), bf16),
        jax.ShapeDtypeStruct((lm * text_own, pairs), bf16),
        jax.ShapeDtypeStruct((1, own), f32),
        jax.ShapeDtypeStruct((1, text_own), f32),
    ]
    held = [
        pltpu.VMEM((block, width), bf16),
        pltpu.VMEM((block, text_width), bf16),
        pltpu.VMEM((1, block), jnp.int32),
        pltpu.VMEM((own, width), bf16),
        pltpu.VMEM((1, own), f32),
        pltpu.VMEM((text_own, text_width), bf16),
        pltpu.VMEM((1, text_own), f32),
    ]
    params = pltpu.CompilerParams(
        collective_id=0, has_side_effects=True, vmem_limit_bytes=40 * 2**20
    )
    if blocks:
        f, g, image_mean, text_mean, relay = pl.pallas_call(
            functools.partial(blocks_kernel, LATE),
            out_shape=results + [jax.ShapeDtypeStruct((max(late_rows, 16), pairs), bf16)],
            in_specs=[hbm] * 7,
            out_specs=[vmem] * 5,
            scratch_shapes=held + [
                pltpu.VMEM((pairs, width), bf16),
                pltpu.VMEM((pairs, text_width), bf16),
                pltpu.VMEM((own, width), bf16),
                pltpu.VMEM((text_own, text_width), bf16),
                pltpu.VMEM((dp, pairs, own), bf16),
                dma((6,)), dma((4,)), dma((2, 4, dp)), dma((2, 4, dp)),
                dma((dp, 5)), dma((dp, 5)), dma((dp, 5)),
                dma((lm,)), dma((lm,)),
            ],
            compiler_params=params,
            name="block_exchange",
        )(*operands)
    else:
        split = 2 if lm % 2 == 0 else 1
        chunks = max(1, own // 256)
        f, g, image_mean, text_mean = pl.pallas_call(
            functools.partial(exchange_kernel, dp, lm, split, chunks),
            out_shape=results,
            in_specs=[hbm] * 7,
            out_specs=[vmem] * 4,
            scratch_shapes=held + [
                pltpu.VMEM((pairs, width), bf16),
                pltpu.VMEM((pairs, text_width), bf16),
                pltpu.VMEM((own, width), bf16),
                pltpu.VMEM((text_own, text_width), bf16),
                dma((7,)),
                dma((dp,)), dma((dp,)), dma((dp,)), dma((dp,)),
                dma((dp,)), dma((dp,)), dma((dp,)), dma((dp,)),
                dma((dp, chunks)), dma((dp, chunks)), dma((dp, chunks)),
                dma((lm,)), dma((lm,)),
            ],
            compiler_params=params,
            name="exchange",
        )(*operands)
    rows, columns = dp * own, lm * text_own
    ahead = rows - late_rows
    tile = math.gcd(math.gcd(own, own - late_rows), 256)
    slots = min(4, ahead // tile)
    if late_rows:
        got = lax.ppermute(relay, "dp", ((dp - 2, dp - 1), (1, 0)))
    zstat, image_mean, text_mean = pl.pallas_call(
        functools.partial(product_kernel, tile, slots, dp, late_rows),
        out_shape=(
            jax.ShapeDtypeStruct((rows, columns), f32),
            jax.ShapeDtypeStruct((1, own), f32),
            jax.ShapeDtypeStruct((1, text_own), f32),
        ),
        in_specs=[vmem] * 4,
        out_specs=(hbm, vmem, vmem),
        scratch_shapes=[pltpu.VMEM((slots, tile, columns), f32), dma((slots,))],
        compiler_params=pltpu.CompilerParams(vmem_limit_bytes=40 * 2**20),
        cost_estimate=pl.CostEstimate(
            flops=2 * ahead * columns * pairs, bytes_accessed=4 * ahead * columns, transcendentals=0
        ),
        name="product",
    )(f, g, image_mean, text_mean)
    if late_rows:
        zstat = pl.pallas_call(
            functools.partial(late_kernel, tile, dp),
            out_shape=jax.ShapeDtypeStruct((rows, columns), f32),
            in_specs=[vmem, vmem, vmem, hbm],
            out_specs=hbm,
            scratch_shapes=[
                pltpu.VMEM((late_rows // tile, tile, columns), f32), dma((late_rows // tile,)),
            ],
            input_output_aliases={3: 0},
            compiler_params=pltpu.CompilerParams(vmem_limit_bytes=40 * 2**20),
            cost_estimate=pl.CostEstimate(
                flops=2 * late_rows * columns * pairs, bytes_accessed=4 * late_rows * columns,
                transcendentals=0,
            ),
            name="late_product",
        )(f, got, g, zstat)
    return (zstat, image_mean[0], text_mean[0])


def solution(mesh):
    in_specs = (
        P(("groups", "dp"), None),
        P(("groups", "dp"), None),
        P(("groups", "dp")),
        P(("landmark", "dp"), None),
        P(("landmark", "dp")),
        P(("dp", "landmark"), None),
        P(("dp", "landmark")),
    )
    out_specs = (
        P(("groups", "landmark"), "dp"),
        P(("groups", "landmark", "dp")),
        P(("groups", "dp", "landmark")),
    )
    return jax.shard_map(
        per_device, mesh=mesh, in_specs=in_specs, out_specs=out_specs, check_vma=False
    )
```

```python
import functools
import math

import jax
import jax.numpy as jnp
from jax import lax
from jax.experimental import pallas as pl
from jax.experimental.pallas import tpu as pltpu
from jax.sharding import PartitionSpec as P

MESH = pl.DeviceIdType.MESH
EPS = 1e-06
LATE = 2
U_WAYS = 2
C_WAYS = 4
FORWARD = 1
FIRST = 2
SWAP = False
SLOTS = 16


def unit_rows(wide):
    return wide * lax.rsqrt(jnp.sum(wide * wide, axis=-1, keepdims=True) + EPS)


def diagonal(size):
    return lax.broadcasted_iota(jnp.int32, (size, size), 0) == lax.broadcasted_iota(
        jnp.int32, (size, size), 1
    )


def scaled_keys(marks_ref, gamma_ref, keys_ref):
    total = marks_ref.shape[0]
    size = min(128, total)

    def step(at, carry):
        rows = pl.ds(pl.multiple_of(at * size, size), size)
        unit = unit_rows(marks_ref[rows, :].astype(jnp.float32))
        gamma = jnp.sum(
            jnp.where(diagonal(size), gamma_ref[:, rows], 0.0), axis=1, keepdims=True
        )
        keys_ref[rows, :] = (unit * gamma).astype(jnp.bfloat16)
        return carry

    lax.fori_loop(0, total // size, step, 0)


def standard_features(keys, units, mean_ref, start, scale):
    rows, pairs = keys.shape[0], units.shape[0]
    inner = lax.dot_general(
        keys, units, (((1,), (1,)), ((), ())), preferred_element_type=jnp.float32
    )
    feats = jnp.exp(inner).astype(jnp.bfloat16).astype(jnp.float32)
    mean = jnp.sum(feats, axis=1, keepdims=True) * (1.0 / pairs)
    dev = feats - mean
    var = jnp.sum(dev * dev, axis=1, keepdims=True) * (1.0 / pairs)
    size = min(128, rows)
    for at in range(0, rows, size):
        mean_ref[:, start + at : start + at + size] = jnp.sum(
            jnp.where(diagonal(size), mean[at : at + size], 0.0), axis=0, keepdims=True
        )
    return (dev * (lax.rsqrt(var + EPS) * scale)).astype(jnp.bfloat16)


def exchange_kernel(
    dp, lm, split, chunks,
    images_hbm, captions_hbm, order_hbm, marks_hbm, gamma_hbm, words_hbm, text_gamma_hbm,
    f_all, g_all, image_mean_ref, text_mean_ref,
    images_ref, captions_ref, order_ref, marks, gamma_ref, words, text_gamma_ref,
    u_all, c_all, keys, text_keys,
    load_sem,
    u_send, u_recv, u_mate_send, u_mate_recv,
    c_send, c_recv, c_mate_send, c_mate_recv,
    right_send, left_send, f_recv, g_send, g_recv,
):
    me, lane = lax.axis_index("dp"), lax.axis_index("landmark")
    block = images_ref.shape[0]
    part = block // split
    own = marks.shape[0]
    text_own = words.shape[0]
    pairs = u_all.shape[0]
    rows_each = own // chunks

    loads = [
        pltpu.make_async_copy(src, dst, load_sem.at[at])
        for at, (src, dst) in enumerate((
            (images_hbm, images_ref), (marks_hbm, marks), (gamma_hbm, gamma_ref),
            (captions_hbm, captions_ref), (order_hbm, order_ref),
            (words_hbm, words), (text_gamma_hbm, text_gamma_ref),
        ))
    ]
    for load in loads:
        load.start()

    barrier = pltpu.get_barrier_semaphore()
    for k in range(1, dp):
        pl.semaphore_signal(
            barrier, inc=1, device_id={"dp": lax.rem(me + k, dp)}, device_id_type=MESH
        )
    for k in range(1, lm):
        pl.semaphore_signal(
            barrier, inc=1, device_id={"landmark": lax.rem(lane + k, lm)}, device_id_type=MESH
        )

    mine = pl.ds(pl.multiple_of(me * block, block), block)
    loads[0].wait()
    u_all[mine, :] = unit_rows(images_ref[...].astype(jnp.float32)).astype(jnp.bfloat16)
    pl.semaphore_wait(barrier, dp - 1 + lm - 1)

    side = lax.rem(lane, split)
    mate = lane + 1 - 2 * side

    def half(shard):
        return pl.ds(pl.multiple_of(shard * block + side * part, part), part)

    def other_half(shard):
        return pl.ds(pl.multiple_of(shard * block + (1 - side) * part, part), part)

    def block_copy(buf, send, recv, k, shard, target):
        return pltpu.make_async_remote_copy(
            src_ref=buf.at[half(shard), :], dst_ref=buf.at[half(shard), :],
            send_sem=send.at[k], recv_sem=recv.at[shard],
            device_id={"dp": target}, device_id_type=MESH,
        )

    def mate_copy(buf, send, recv, k, shard, rows):
        return pltpu.make_async_remote_copy(
            src_ref=buf.at[rows, :], dst_ref=buf.at[rows, :],
            send_sem=send.at[k], recv_sem=recv.at[shard],
            device_id={"landmark": mate}, device_id_type=MESH,
        )

    sends = []

    def spread(buf, send, recv):
        for k in range(1, dp):
            copy = block_copy(buf, send, recv, k - 1, me, lax.rem(me + k, dp))
            copy.start()
            sends.append(copy)

    spread(u_all, u_send, u_recv)

    def collect(buf, send, recv, mate_send, mate_recv):
        for k in range(1, dp):
            shard = lax.rem(me + dp - k, dp)
            block_copy(buf, send, recv, k - 1, shard, me).wait_recv()
            if split > 1:
                copy = mate_copy(buf, mate_send, mate_recv, k - 1, shard, half(shard))
                copy.start()
                sends.append(copy)
        if split > 1:
            for k in range(1, dp):
                shard = lax.rem(me + dp - k, dp)
                mate_copy(
                    buf, mate_send, mate_recv, k - 1, shard, other_half(shard)
                ).wait_recv()

    loads[3].wait()
    loads[4].wait()
    picks = (
        lax.broadcasted_iota(jnp.int32, (block, block), 0) == order_ref[...]
    ).astype(jnp.bfloat16)
    paired = lax.dot_general(
        picks, captions_ref[...], (((0,), (0,)), ((), ())), preferred_element_type=jnp.float32
    )
    c_all[mine, :] = unit_rows(paired).astype(jnp.bfloat16)
    spread(c_all, c_send, c_recv)
    loads[1].wait()
    loads[2].wait()
    scaled_keys(marks, gamma_ref, keys)
    def f_rows(shard, c):
        return pl.ds(pl.multiple_of(shard * own + c * rows_each, rows_each), rows_each)

    def hop(shard, c, send, target):
        return pltpu.make_async_remote_copy(
            src_ref=f_all.at[f_rows(shard, c), :], dst_ref=f_all.at[f_rows(shard, c), :],
            send_sem=send.at[shard, c], recv_sem=f_recv.at[shard, c],
            device_id={"dp": target}, device_id_type=MESH,
        )

    def to_right(shard, c):
        return hop(shard, c, right_send, jnp.minimum(me + 1, dp - 1))

    def to_left(shard, c):
        return hop(shard, c, left_send, jnp.maximum(me - 1, 0))

    collect(u_all, u_send, u_recv, u_mate_send, u_mate_recv)
    for c in range(chunks):
        at = c * rows_each
        f_all[f_rows(me, c), :] = standard_features(
            keys[at : at + rows_each, :], u_all[...], image_mean_ref, at, 1.0
        )

        @pl.when(me < dp - 1)
        def _():
            to_right(me, c).start()

        @pl.when(me > 0)
        def _():
            to_left(me, c).start()

    loads[5].wait()
    loads[6].wait()
    scaled_keys(words, text_gamma_ref, text_keys)
    collect(c_all, c_send, c_recv, c_mate_send, c_mate_recv)
    text_mine = pl.ds(pl.multiple_of(lane * text_own, text_own), text_own)
    g_all[text_mine, :] = standard_features(
        text_keys[...], c_all[...], text_mean_ref, 0, 1.0 / math.sqrt(pairs)
    )

    def g_copy(k, shard, target):
        rows = pl.ds(pl.multiple_of(shard * text_own, text_own), text_own)
        return pltpu.make_async_remote_copy(
            src_ref=g_all.at[rows, :], dst_ref=g_all.at[rows, :],
            send_sem=g_send.at[k], recv_sem=g_recv.at[shard],
            device_id={"landmark": target}, device_id_type=MESH,
        )

    for k in range(1, lm):
        copy = g_copy(k - 1, lane, lax.rem(lane + k, lm))
        copy.start()
        sends.append(copy)

    for d in range(1, dp):
        for c in range(chunks):

            @pl.when(me - d >= 0)
            def _():
                to_left(me - d, c).wait_recv()

                @pl.when(me < dp - 1)
                def _():
                    to_right(me - d, c).start()

            @pl.when(me + d < dp)
            def _():
                to_right(me + d, c).wait_recv()

                @pl.when(me > 0)
                def _():
                    to_left(me + d, c).start()

    for k in range(1, lm):
        shard = lax.rem(lane + lm - k, lm)
        g_copy(k - 1, shard, lane).wait_recv()

    for copy in sends:
        copy.wait_send()
    for shard in range(dp):
        for c in range(chunks):

            @pl.when(jnp.logical_and(shard <= me, me < dp - 1))
            def _():
                to_right(shard, c).wait_send()

            @pl.when(jnp.logical_and(shard >= me, me > 0))
            def _():
                to_left(shard, c).wait_send()


def near_first(shard):
    return (
        shard,
        shard + 1 - 2 * lax.rem(shard, 2),
        2 - shard // 2,
        3 - 3 * (shard // 2),
    )


def place(shard, p):
    upper = shard // 2
    same = 1 - (upper - p // 2) * (upper - p // 2)
    far = (1 - upper) * p + upper * (3 - p)
    return same * (p - shard) * (p - shard) + (1 - same) * far


def aligned(start, size):
    return pl.ds(pl.multiple_of(start, size), size)


def standard_columns(feats, scale):
    pairs = feats.shape[0]
    mean = jnp.sum(feats, axis=0, keepdims=True) * (1.0 / pairs)
    dev = feats - mean
    var = jnp.sum(dev * dev, axis=0, keepdims=True) * (1.0 / pairs)
    return jnp.transpose(dev * (lax.rsqrt(var + EPS) * scale)).astype(jnp.bfloat16), mean


def blocks_kernel(
    late,
    images_hbm, captions_hbm, order_hbm, marks_hbm, gamma_hbm, words_hbm, text_gamma_hbm,
    f_all, g_all, image_mean_ref, text_mean_ref, relay,
    images_ref, captions_ref, order_ref, marks, gamma_ref, words, text_gamma_ref,
    u_all, c_all, keys, text_keys, raw,
    load_sem, mark_sem, u_sems, c_sems,
    right_send, left_send, f_recv, g_send, g_recv,
):
    dp, lm, cuts = 4, 4, 4
    me, lane = lax.axis_index("dp"), lax.axis_index("landmark")
    block = images_ref.shape[0]
    part = block // 2
    own = marks.shape[0]
    text_own = words.shape[0]
    pairs = block * dp
    piece = own // cuts

    loads = [
        pltpu.make_async_copy(src, dst, load_sem.at[at])
        for at, (src, dst) in enumerate((
            (images_hbm, images_ref), (captions_hbm, captions_ref), (order_hbm, order_ref),
            (gamma_hbm, gamma_ref), (words_hbm, words), (text_gamma_hbm, text_gamma_ref),
        ))
    ]
    mark_loads = [
        pltpu.make_async_copy(
            marks_hbm.at[pl.ds(at * piece, piece), :], marks.at[pl.ds(at * piece, piece), :],
            mark_sem.at[at],
        )
        for at in range(cuts)
    ]
    loads[0].start()
    barrier = pltpu.get_barrier_semaphore()
    for k in range(1, dp):
        pl.semaphore_signal(
            barrier, inc=1, device_id={"dp": lax.rem(me + k, dp)}, device_id_type=MESH
        )
    for k in range(1, lm):
        pl.semaphore_signal(
            barrier, inc=1, device_id={"landmark": lax.rem(lane + k, lm)}, device_id_type=MESH
        )
    for load in loads[1:4] + mark_loads + loads[4:]:
        load.start()

    half, core = lane // 2, lax.rem(lane, 2)
    mate = lane + 1 - 2 * core
    across = lax.rem(lane + 2, lm)
    order = near_first(me)
    mine = aligned(me * block, block)
    sends = []

    def launch(copy):
        copy.start()
        sends.append(copy)

    def portion(buf, sems, stage, k, shard, h, side, device):
        wide = buf.shape[1] // 2
        columns = pl.ds(0, 2 * wide) if h is None else aligned(h * wide, wide)
        ref = buf.at[aligned(shard * block + side * part, part), columns]
        return pltpu.make_async_remote_copy(
            src_ref=ref, dst_ref=ref, send_sem=sems.at[0, stage, k],
            recv_sem=sems.at[1, stage, shard], device_id=device, device_id_type=MESH,
        )

    def routes(ways):
        yield mate, half, 1 - core
        if ways == 4:
            yield across, 1 - half, core
            yield lm - 1 - lane, 1 - half, 1 - core

    def z_copy(buf, sems, ways, k, shard):
        h = half if ways == 4 else None
        return portion(buf, sems, 0, k, shard, h, core, {"dp": order[k]})

    def spread(buf, sems, ways):
        for k in range(1, dp):
            launch(z_copy(buf, sems, ways, k, me))

    def pass_on(buf, sems, ways, blocks=range(1, 4)):
        for k in blocks:
            z_copy(buf, sems, ways, k, order[k]).wait_recv()
            h = half if ways == 4 else None
            for stage, (target, _, _) in reversed(list(enumerate(routes(ways), 1))):
                launch(portion(buf, sems, stage, k, order[k], h, core, {"landmark": target}))

    def gather(buf, sems, ways, blocks=range(1, 4)):
        for k in blocks:
            for stage, (target, h, side) in enumerate(routes(ways), 1):
                h = h if ways == 4 else None
                portion(buf, sems, stage, k, order[k], h, side, {"landmark": target}).wait_recv()

    loads[0].wait()
    u_all[mine, :] = unit_rows(images_ref[...].astype(jnp.float32)).astype(jnp.bfloat16)
    pl.semaphore_wait(barrier, dp - 1 + lm - 1)
    spread(u_all, u_sems, U_WAYS)
    loads[1].wait()
    loads[2].wait()
    picks = (
        lax.broadcasted_iota(jnp.int32, (block, block), 0) == order_ref[...]
    ).astype(jnp.bfloat16)
    paired = lax.dot_general(
        picks, captions_ref[...], (((0,), (0,)), ((), ())), preferred_element_type=jnp.float32
    )
    c_all[mine, :] = unit_rows(paired).astype(jnp.bfloat16)

    loads[3].wait()
    for at in range(cuts):
        mark_loads[at].wait()
        rows = pl.ds(at * piece, piece)
        scaled_keys(marks.at[rows, :], gamma_ref.at[:, rows], keys.at[rows, :])

    def hop(shard, j, send, target, rows):
        if j < FIRST:
            ref = raw.at[shard, pl.ds(j * block, block), pl.ds(0, rows)]
        else:
            ref = raw.at[
                shard, pl.ds(FIRST * block, pairs - FIRST * block),
                pl.ds((j - FIRST) * piece, piece),
            ]
        return pltpu.make_async_remote_copy(
            src_ref=ref, dst_ref=ref,
            send_sem=send.at[shard, j], recv_sem=f_recv.at[shard, j],
            device_id={"dp": target}, device_id_type=MESH,
        )

    def to_right(shard, j, rows=own):
        return hop(shard, j, right_send, jnp.minimum(me + 1, dp - 1), rows)

    def to_left(shard, j, rows=own):
        return hop(shard, j, left_send, jnp.maximum(me - 1, 0), rows)

    def send_own(j):
        @pl.when(me < dp - 1)
        def _():
            to_right(me, j).start()

        @pl.when(me > 0)
        def _():
            to_left(me, j).start()

    def features(units, rows):
        inner = lax.dot_general(
            units, keys[rows, :], (((1,), (1,)), ((), ())), preferred_element_type=jnp.float32
        )
        return jnp.exp(inner).astype(jnp.bfloat16)

    def first_block(j):
        units = u_all[aligned(order[j] * block, block), :]
        raw[me, j * block : (j + 1) * block, :] = features(units, pl.ds(0, own))
        send_own(j)

    first_block(0)
    spread(c_all, c_sems, C_WAYS)
    loads[4].wait()
    loads[5].wait()
    if not SWAP:
        scaled_keys(words, text_gamma_ref, text_keys)
    hops = dp - 2 if late == cuts else dp - 1
    early_rows = own - late * piece

    def rows_of(d):
        return early_rows if d == dp - 1 else own

    def last_of(d):
        return FIRST - 1 + (cuts - late if d == dp - 1 else cuts)

    def receive(d, j):
        @pl.when(me - d >= 0)
        def _():
            to_left(me - d, j, rows_of(d)).wait_recv()
            if d < hops and j <= last_of(d + 1):

                @pl.when(me < dp - 1)
                def _():
                    to_right(me - d, j, rows_of(d + 1)).start()

        @pl.when(me + d < dp)
        def _():
            to_right(me + d, j, rows_of(d)).wait_recv()
            if d < hops and j <= last_of(d + 1):

                @pl.when(me > 0)
                def _():
                    to_left(me + d, j, rows_of(d + 1)).start()

    pass_on(u_all, u_sems, U_WAYS, range(1, FIRST))
    if SWAP:
        scaled_keys(words, text_gamma_ref, text_keys)
    for j in range(1, FIRST):
        gather(u_all, u_sems, U_WAYS, (j,))
        first_block(j)
    pass_on(u_all, u_sems, U_WAYS, range(FIRST, dp))
    if FORWARD == 0:
        receive(1, 0)
    gather(u_all, u_sems, U_WAYS, range(FIRST, dp))
    others = jnp.concatenate(
        [u_all[aligned(order[k] * block, block), :] for k in range(FIRST, dp)], axis=0
    )
    for j in range(1, cuts + 1):
        rows = pl.ds((j - 1) * piece, piece)
        raw[me, FIRST * block :, (j - 1) * piece : j * piece] = features(others, rows)
        send_own(j + FIRST - 1)
        if j == 1:
            pass_on(c_all, c_sems, C_WAYS)

    def standardize(shard, j, mean_ref=None):
        for at in range((j - 1) * piece, j * piece, 128):
            columns = slice(at, at + 128)
            feats = jnp.concatenate(
                [
                    raw[shard, aligned(place(shard, p) * block, block), columns]
                    for p in range(dp)
                ],
                axis=0,
            )
            rows, mean = standard_columns(feats.astype(jnp.float32), 1.0)
            f_all[aligned(shard * own + at, 128), :] = rows
            if mean_ref is not None:
                mean_ref[:, columns] = mean

    for j in range(FIRST):
        if FORWARD or j:
            receive(1, j)
    for j in range(1, cuts + 1):
        standardize(me, j, image_mean_ref)
    receive(1, FIRST)
    gather(c_all, c_sems, C_WAYS)
    inner = lax.dot_general(
        c_all[...], text_keys[...], (((1,), (1,)), ((), ())), preferred_element_type=jnp.float32
    )
    rows, text_mean_ref[...] = standard_columns(
        jnp.exp(inner).astype(jnp.bfloat16).astype(jnp.float32), 1.0 / math.sqrt(pairs)
    )
    g_all[aligned(lane * text_own, text_own), :] = rows

    def g_copy(k, shard, target):
        rows = aligned(shard * text_own, text_own)
        return pltpu.make_async_remote_copy(
            src_ref=g_all.at[rows, :], dst_ref=g_all.at[rows, :],
            send_sem=g_send.at[k], recv_sem=g_recv.at[shard],
            device_id={"landmark": target}, device_id_type=MESH,
        )

    for k in range(1, lm):
        launch(g_copy(k - 1, lane, lax.rem(lane + k, lm)))

    for d in range(1, hops + 1):
        for j in range(FIRST if d == 1 else 0, last_of(d) + 1):
            if d > 1 or j > FIRST:
                receive(d, j)
            if j < FIRST:
                continue
            cut = j - FIRST + 1

            @pl.when(me - d >= 0)
            def _():
                standardize(me - d, cut)

            @pl.when(me + d < dp)
            def _():
                standardize(me + d, cut)

            if d == dp - 2 and cut > cuts - late:
                at = (cut - 1) * piece
                rows = pl.ds(at - early_rows, piece)

                @pl.when(me == dp - 2)
                def _():
                    relay[rows, :] = f_all[pl.ds(at, piece), :]

                @pl.when(me == 1)
                def _():
                    relay[rows, :] = f_all[pl.ds((dp - 1) * own + at, piece), :]

    for k in range(1, lm):
        shard = lax.rem(lane + lm - k, lm)
        g_copy(k - 1, shard, lane).wait_recv()
    for copy in sends:
        copy.wait_send()
    for d in range(hops):

        @pl.when(jnp.logical_and(me >= d, me < dp - 1))
        def _():
            for j in range(last_of(d + 1) + 1):
                to_right(me - d, j, rows_of(d + 1)).wait_send()

        @pl.when(jnp.logical_and(me < dp - d, me > 0))
        def _():
            for j in range(last_of(d + 1) + 1):
                to_left(me + d, j, rows_of(d + 1)).wait_send()


def product_kernel(
    tile, slots, dp, late_rows, f_ref, g_ref, image_mean_in, text_mean_in,
    z_hbm, image_mean_ref, text_mean_ref, buf, sem, mean_sem,
):
    means = [
        pltpu.make_async_copy(image_mean_in, image_mean_ref, mean_sem.at[0]),
        pltpu.make_async_copy(text_mean_in, text_mean_ref, mean_sem.at[1]),
    ]
    for copy in means:
        copy.start()
    total = f_ref.shape[0]
    steps = (total - late_rows) // tile
    edge = total // dp - late_rows

    def rows(at):
        start = at * tile
        if late_rows:
            skip = jnp.logical_and(lax.axis_index("dp") > 0, start >= edge)
            start = start + jnp.where(skip, late_rows, 0)
        return pl.ds(pl.multiple_of(start, tile), tile)

    def out(at):
        slot = lax.rem(at, slots)
        return pltpu.make_async_copy(buf.at[slot], z_hbm.at[rows(at), :], sem.at[slot])

    def make(at):
        buf[lax.rem(at, slots)] = lax.dot_general(
            f_ref[rows(at), :], g_ref[...], (((1,), (1,)), ((), ())),
            preferred_element_type=jnp.float32,
        )
        out(at).start()

    def step(at, carry):
        @pl.when(at >= slots)
        def _():
            out(at - slots).wait()

        make(at)
        return carry

    if steps == slots:
        for at in range(steps):
            make(jnp.int32(at))
    else:
        lax.fori_loop(0, steps, step, 0)
    for at in range(max(0, steps - slots), steps):
        out(jnp.int32(at)).wait()
    for copy in means:
        copy.wait()


def late_kernel(tile, dp, f_ref, got_ref, g_ref, z_in, z_hbm, buf, sem):
    me = lax.axis_index("dp")
    late_rows = got_ref.shape[0]
    own = f_ref.shape[0] // dp
    first = jnp.where(me == 0, dp * own, own) - late_rows
    inner = jnp.logical_and(me > 0, me < dp - 1)

    def rows(at):
        return pl.ds(pl.multiple_of(first + at * tile, tile), tile)

    def out(at):
        return pltpu.make_async_copy(buf.at[at], z_hbm.at[rows(at), :], sem.at[at])

    for at in range(late_rows // tile):
        buf[at] = lax.dot_general(
            jnp.where(inner, f_ref[rows(at), :], got_ref[pl.ds(at * tile, tile), :]),
            g_ref[...], (((1,), (1,)), ((), ())), preferred_element_type=jnp.float32,
        )
        out(at).start()
    for at in range(late_rows // tile):
        out(at).wait()


def per_device(
    images, captions, caption_of, image_landmarks, image_gamma, text_landmarks, text_gamma
):
    dp, lm = lax.axis_size("dp"), lax.axis_size("landmark")
    block, width = images.shape
    text_width = captions.shape[1]
    own, text_own = image_landmarks.shape[0], text_landmarks.shape[0]
    pairs = block * dp
    bf16, f32 = jnp.bfloat16, jnp.float32
    vmem = pl.BlockSpec(memory_space=pltpu.VMEM)
    hbm = pl.BlockSpec(memory_space=pltpu.HBM)
    dma = pltpu.SemaphoreType.DMA
    blocks = (
        dp == 4 and lm == 4 and block % 32 == 0 and own % 512 == 0 and text_own % 128 == 0
        and width % 256 == 0 and text_width % 256 == 0
    )
    late_rows = own * LATE // 4 if blocks else 0
    operands = [
        pltpu.with_memory_space_constraint(value, pltpu.HBM)
        for value in (
            images, captions, caption_of[None, :], image_landmarks, image_gamma[None, :],
            text_landmarks, text_gamma[None, :],
        )
    ]
    results = [
        jax.ShapeDtypeStruct((dp * own, pairs), bf16),
        jax.ShapeDtypeStruct((lm * text_own, pairs), bf16),
        jax.ShapeDtypeStruct((1, own), f32),
        jax.ShapeDtypeStruct((1, text_own), f32),
    ]
    held = [
        pltpu.VMEM((block, width), bf16),
        pltpu.VMEM((block, text_width), bf16),
        pltpu.VMEM((1, block), jnp.int32),
        pltpu.VMEM((own, width), bf16),
        pltpu.VMEM((1, own), f32),
        pltpu.VMEM((text_own, text_width), bf16),
        pltpu.VMEM((1, text_own), f32),
    ]
    params = pltpu.CompilerParams(
        collective_id=0, has_side_effects=True, vmem_limit_bytes=40 * 2**20
    )
    if blocks:
        f, g, image_mean, text_mean, relay = pl.pallas_call(
            functools.partial(blocks_kernel, LATE),
            out_shape=results + [jax.ShapeDtypeStruct((max(late_rows, 16), pairs), bf16)],
            in_specs=[hbm] * 7,
            out_specs=[vmem] * 5,
            scratch_shapes=held + [
                pltpu.VMEM((pairs, width), bf16),
                pltpu.VMEM((pairs, text_width), bf16),
                pltpu.VMEM((own, width), bf16),
                pltpu.VMEM((text_own, text_width), bf16),
                pltpu.VMEM((dp, pairs, own), bf16),
                dma((6,)), dma((4,)), dma((2, 4, dp)), dma((2, 4, dp)),
                dma((dp, 6)), dma((dp, 6)), dma((dp, 6)),
                dma((lm,)), dma((lm,)),
            ],
            compiler_params=params,
            name="block_exchange",
        )(*operands)
    else:
        split = 2 if lm % 2 == 0 else 1
        chunks = max(1, own // 256)
        f, g, image_mean, text_mean = pl.pallas_call(
            functools.partial(exchange_kernel, dp, lm, split, chunks),
            out_shape=results,
            in_specs=[hbm] * 7,
            out_specs=[vmem] * 4,
            scratch_shapes=held + [
                pltpu.VMEM((pairs, width), bf16),
                pltpu.VMEM((pairs, text_width), bf16),
                pltpu.VMEM((own, width), bf16),
                pltpu.VMEM((text_own, text_width), bf16),
                dma((7,)),
                dma((dp,)), dma((dp,)), dma((dp,)), dma((dp,)),
                dma((dp,)), dma((dp,)), dma((dp,)), dma((dp,)),
                dma((dp, chunks)), dma((dp, chunks)), dma((dp, chunks)),
                dma((lm,)), dma((lm,)),
            ],
            compiler_params=params,
            name="exchange",
        )(*operands)
    rows, columns = dp * own, lm * text_own
    ahead = rows - late_rows
    tile = math.gcd(math.gcd(own, own - late_rows), 256)
    slots = min(SLOTS, ahead // tile)
    if late_rows:
        got = lax.ppermute(relay, "dp", ((dp - 2, dp - 1), (1, 0)))
    zstat, image_mean, text_mean = pl.pallas_call(
        functools.partial(product_kernel, tile, slots, dp, late_rows),
        out_shape=(
            jax.ShapeDtypeStruct((rows, columns), f32),
            jax.ShapeDtypeStruct((1, own), f32),
            jax.ShapeDtypeStruct((1, text_own), f32),
        ),
        in_specs=[vmem] * 4,
        out_specs=(hbm, hbm, hbm),
        scratch_shapes=[pltpu.VMEM((slots, tile, columns), f32), dma((slots,)), dma((2,))],
        compiler_params=pltpu.CompilerParams(vmem_limit_bytes=40 * 2**20),
        cost_estimate=pl.CostEstimate(
            flops=2 * ahead * columns * pairs, bytes_accessed=4 * ahead * columns, transcendentals=0
        ),
        name="product",
    )(f, g, image_mean, text_mean)
    if late_rows:
        zstat = pl.pallas_call(
            functools.partial(late_kernel, tile, dp),
            out_shape=jax.ShapeDtypeStruct((rows, columns), f32),
            in_specs=[vmem, vmem, vmem, hbm],
            out_specs=hbm,
            scratch_shapes=[
                pltpu.VMEM((late_rows // tile, tile, columns), f32), dma((late_rows // tile,)),
            ],
            input_output_aliases={3: 0},
            compiler_params=pltpu.CompilerParams(vmem_limit_bytes=40 * 2**20),
            cost_estimate=pl.CostEstimate(
                flops=2 * late_rows * columns * pairs, bytes_accessed=4 * late_rows * columns,
                transcendentals=0,
            ),
            name="late_product",
        )(f, got, g, zstat)
    return (zstat, image_mean[0], text_mean[0])


def solution(mesh):
    in_specs = (
        P(("groups", "dp"), None),
        P(("groups", "dp"), None),
        P(("groups", "dp")),
        P(("landmark", "dp"), None),
        P(("landmark", "dp")),
        P(("dp", "landmark"), None),
        P(("dp", "landmark")),
    )
    out_specs = (
        P(("groups", "landmark"), "dp"),
        P(("groups", "landmark", "dp")),
        P(("groups", "dp", "landmark")),
    )
    return jax.shard_map(
        per_device, mesh=mesh, in_specs=in_specs, out_specs=out_specs, check_vma=False
    )
```

```python
import functools
import math

import jax
import jax.numpy as jnp
from jax import lax
from jax.experimental import pallas as pl
from jax.experimental.pallas import tpu as pltpu
from jax.sharding import PartitionSpec as P

MESH = pl.DeviceIdType.MESH
EPS = 1e-06
LATE = 2
U_WAYS = (0, 2, 2, 2)
C_WAYS = (0, 4, 4, 4)
FORWARD = 1
FIRST = 2
SWAP = False
HOLD = 0
C_AT = 0
C_ON = 1
G_AT = 2
Z_AT = 1
READY = 1
SLOTS = 6


def unit_rows(wide):
    return wide * lax.rsqrt(jnp.sum(wide * wide, axis=-1, keepdims=True) + EPS)


def diagonal(size):
    return lax.broadcasted_iota(jnp.int32, (size, size), 0) == lax.broadcasted_iota(
        jnp.int32, (size, size), 1
    )


def scaled_keys(marks_ref, gamma_ref, keys_ref):
    total = marks_ref.shape[0]
    size = min(128, total)

    def step(at, carry):
        rows = pl.ds(pl.multiple_of(at * size, size), size)
        unit = unit_rows(marks_ref[rows, :].astype(jnp.float32))
        gamma = jnp.sum(
            jnp.where(diagonal(size), gamma_ref[:, rows], 0.0), axis=1, keepdims=True
        )
        keys_ref[rows, :] = (unit * gamma).astype(jnp.bfloat16)
        return carry

    lax.fori_loop(0, total // size, step, 0)


def standard_features(keys, units, mean_ref, start, scale):
    rows, pairs = keys.shape[0], units.shape[0]
    inner = lax.dot_general(
        keys, units, (((1,), (1,)), ((), ())), preferred_element_type=jnp.float32
    )
    feats = jnp.exp(inner).astype(jnp.bfloat16).astype(jnp.float32)
    mean = jnp.sum(feats, axis=1, keepdims=True) * (1.0 / pairs)
    dev = feats - mean
    var = jnp.sum(dev * dev, axis=1, keepdims=True) * (1.0 / pairs)
    size = min(128, rows)
    for at in range(0, rows, size):
        mean_ref[:, start + at : start + at + size] = jnp.sum(
            jnp.where(diagonal(size), mean[at : at + size], 0.0), axis=0, keepdims=True
        )
    return (dev * (lax.rsqrt(var + EPS) * scale)).astype(jnp.bfloat16)


def exchange_kernel(
    dp, lm, split, chunks,
    images_hbm, captions_hbm, order_hbm, marks_hbm, gamma_hbm, words_hbm, text_gamma_hbm,
    f_all, g_all, image_mean_ref, text_mean_ref,
    images_ref, captions_ref, order_ref, marks, gamma_ref, words, text_gamma_ref,
    u_all, c_all, keys, text_keys,
    load_sem,
    u_send, u_recv, u_mate_send, u_mate_recv,
    c_send, c_recv, c_mate_send, c_mate_recv,
    right_send, left_send, f_recv, g_send, g_recv,
):
    me, lane = lax.axis_index("dp"), lax.axis_index("landmark")
    block = images_ref.shape[0]
    part = block // split
    own = marks.shape[0]
    text_own = words.shape[0]
    pairs = u_all.shape[0]
    rows_each = own // chunks

    loads = [
        pltpu.make_async_copy(src, dst, load_sem.at[at])
        for at, (src, dst) in enumerate((
            (images_hbm, images_ref), (marks_hbm, marks), (gamma_hbm, gamma_ref),
            (captions_hbm, captions_ref), (order_hbm, order_ref),
            (words_hbm, words), (text_gamma_hbm, text_gamma_ref),
        ))
    ]
    for load in loads:
        load.start()

    barrier = pltpu.get_barrier_semaphore()
    for k in range(1, dp):
        pl.semaphore_signal(
            barrier, inc=1, device_id={"dp": lax.rem(me + k, dp)}, device_id_type=MESH
        )
    for k in range(1, lm):
        pl.semaphore_signal(
            barrier, inc=1, device_id={"landmark": lax.rem(lane + k, lm)}, device_id_type=MESH
        )

    mine = pl.ds(pl.multiple_of(me * block, block), block)
    loads[0].wait()
    u_all[mine, :] = unit_rows(images_ref[...].astype(jnp.float32)).astype(jnp.bfloat16)
    pl.semaphore_wait(barrier, dp - 1 + lm - 1)

    side = lax.rem(lane, split)
    mate = lane + 1 - 2 * side

    def half(shard):
        return pl.ds(pl.multiple_of(shard * block + side * part, part), part)

    def other_half(shard):
        return pl.ds(pl.multiple_of(shard * block + (1 - side) * part, part), part)

    def block_copy(buf, send, recv, k, shard, target):
        return pltpu.make_async_remote_copy(
            src_ref=buf.at[half(shard), :], dst_ref=buf.at[half(shard), :],
            send_sem=send.at[k], recv_sem=recv.at[shard],
            device_id={"dp": target}, device_id_type=MESH,
        )

    def mate_copy(buf, send, recv, k, shard, rows):
        return pltpu.make_async_remote_copy(
            src_ref=buf.at[rows, :], dst_ref=buf.at[rows, :],
            send_sem=send.at[k], recv_sem=recv.at[shard],
            device_id={"landmark": mate}, device_id_type=MESH,
        )

    sends = []

    def spread(buf, send, recv):
        for k in range(1, dp):
            copy = block_copy(buf, send, recv, k - 1, me, lax.rem(me + k, dp))
            copy.start()
            sends.append(copy)

    spread(u_all, u_send, u_recv)

    def collect(buf, send, recv, mate_send, mate_recv):
        for k in range(1, dp):
            shard = lax.rem(me + dp - k, dp)
            block_copy(buf, send, recv, k - 1, shard, me).wait_recv()
            if split > 1:
                copy = mate_copy(buf, mate_send, mate_recv, k - 1, shard, half(shard))
                copy.start()
                sends.append(copy)
        if split > 1:
            for k in range(1, dp):
                shard = lax.rem(me + dp - k, dp)
                mate_copy(
                    buf, mate_send, mate_recv, k - 1, shard, other_half(shard)
                ).wait_recv()

    loads[3].wait()
    loads[4].wait()
    picks = (
        lax.broadcasted_iota(jnp.int32, (block, block), 0) == order_ref[...]
    ).astype(jnp.bfloat16)
    paired = lax.dot_general(
        picks, captions_ref[...], (((0,), (0,)), ((), ())), preferred_element_type=jnp.float32
    )
    c_all[mine, :] = unit_rows(paired).astype(jnp.bfloat16)
    spread(c_all, c_send, c_recv)
    loads[1].wait()
    loads[2].wait()
    scaled_keys(marks, gamma_ref, keys)
    def f_rows(shard, c):
        return pl.ds(pl.multiple_of(shard * own + c * rows_each, rows_each), rows_each)

    def hop(shard, c, send, target):
        return pltpu.make_async_remote_copy(
            src_ref=f_all.at[f_rows(shard, c), :], dst_ref=f_all.at[f_rows(shard, c), :],
            send_sem=send.at[shard, c], recv_sem=f_recv.at[shard, c],
            device_id={"dp": target}, device_id_type=MESH,
        )

    def to_right(shard, c):
        return hop(shard, c, right_send, jnp.minimum(me + 1, dp - 1))

    def to_left(shard, c):
        return hop(shard, c, left_send, jnp.maximum(me - 1, 0))

    collect(u_all, u_send, u_recv, u_mate_send, u_mate_recv)
    for c in range(chunks):
        at = c * rows_each
        f_all[f_rows(me, c), :] = standard_features(
            keys[at : at + rows_each, :], u_all[...], image_mean_ref, at, 1.0
        )

        @pl.when(me < dp - 1)
        def _():
            to_right(me, c).start()

        @pl.when(me > 0)
        def _():
            to_left(me, c).start()

    loads[5].wait()
    loads[6].wait()
    scaled_keys(words, text_gamma_ref, text_keys)
    collect(c_all, c_send, c_recv, c_mate_send, c_mate_recv)
    text_mine = pl.ds(pl.multiple_of(lane * text_own, text_own), text_own)
    g_all[text_mine, :] = standard_features(
        text_keys[...], c_all[...], text_mean_ref, 0, 1.0 / math.sqrt(pairs)
    )

    def g_copy(k, shard, target):
        rows = pl.ds(pl.multiple_of(shard * text_own, text_own), text_own)
        return pltpu.make_async_remote_copy(
            src_ref=g_all.at[rows, :], dst_ref=g_all.at[rows, :],
            send_sem=g_send.at[k], recv_sem=g_recv.at[shard],
            device_id={"landmark": target}, device_id_type=MESH,
        )

    for k in range(1, lm):
        copy = g_copy(k - 1, lane, lax.rem(lane + k, lm))
        copy.start()
        sends.append(copy)

    for d in range(1, dp):
        for c in range(chunks):

            @pl.when(me - d >= 0)
            def _():
                to_left(me - d, c).wait_recv()

                @pl.when(me < dp - 1)
                def _():
                    to_right(me - d, c).start()

            @pl.when(me + d < dp)
            def _():
                to_right(me + d, c).wait_recv()

                @pl.when(me > 0)
                def _():
                    to_left(me + d, c).start()

    for k in range(1, lm):
        shard = lax.rem(lane + lm - k, lm)
        g_copy(k - 1, shard, lane).wait_recv()

    for copy in sends:
        copy.wait_send()
    for shard in range(dp):
        for c in range(chunks):

            @pl.when(jnp.logical_and(shard <= me, me < dp - 1))
            def _():
                to_right(shard, c).wait_send()

            @pl.when(jnp.logical_and(shard >= me, me > 0))
            def _():
                to_left(shard, c).wait_send()


def near_first(shard):
    return (
        shard,
        shard + 1 - 2 * lax.rem(shard, 2),
        2 - shard // 2,
        3 - 3 * (shard // 2),
    )


def place(shard, p):
    upper = shard // 2
    same = 1 - (upper - p // 2) * (upper - p // 2)
    far = (1 - upper) * p + upper * (3 - p)
    return same * (p - shard) * (p - shard) + (1 - same) * far


def aligned(start, size):
    return pl.ds(pl.multiple_of(start, size), size)


def standard_columns(feats, scale):
    pairs = feats.shape[0]
    mean = jnp.sum(feats, axis=0, keepdims=True) * (1.0 / pairs)
    dev = feats - mean
    var = jnp.sum(dev * dev, axis=0, keepdims=True) * (1.0 / pairs)
    return jnp.transpose(dev * (lax.rsqrt(var + EPS) * scale)).astype(jnp.bfloat16), mean


def blocks_kernel(
    late,
    images_hbm, captions_hbm, order_hbm, marks_hbm, gamma_hbm, words_hbm, text_gamma_hbm,
    f_all, g_all, image_mean_ref, text_mean_ref, relay, z_own,
    images_ref, captions_ref, order_ref, marks, gamma_ref, words, text_gamma_ref,
    u_all, c_all, keys, text_keys, raw,
    load_sem, mark_sem, u_sems, c_sems,
    right_send, left_send, f_recv, g_send, g_recv,
):
    dp, lm, cuts = 4, 4, 4
    me, lane = lax.axis_index("dp"), lax.axis_index("landmark")
    block = images_ref.shape[0]
    part = block // 2
    own = marks.shape[0]
    text_own = words.shape[0]
    pairs = block * dp
    piece = own // cuts

    loads = [
        pltpu.make_async_copy(src, dst, load_sem.at[at])
        for at, (src, dst) in enumerate((
            (images_hbm, images_ref), (captions_hbm, captions_ref), (order_hbm, order_ref),
            (gamma_hbm, gamma_ref), (words_hbm, words), (text_gamma_hbm, text_gamma_ref),
        ))
    ]
    mark_loads = [
        pltpu.make_async_copy(
            marks_hbm.at[pl.ds(at * piece, piece), :], marks.at[pl.ds(at * piece, piece), :],
            mark_sem.at[at],
        )
        for at in range(cuts)
    ]
    loads[0].start()
    barrier = pltpu.get_barrier_semaphore()
    for k in range(1, dp):
        pl.semaphore_signal(
            barrier, inc=1, device_id={"dp": lax.rem(me + k, dp)}, device_id_type=MESH
        )
    for k in range(1, lm):
        pl.semaphore_signal(
            barrier, inc=1, device_id={"landmark": lax.rem(lane + k, lm)}, device_id_type=MESH
        )
    for load in loads[1:4] + mark_loads + loads[4:]:
        load.start()

    half, core = lane // 2, lax.rem(lane, 2)
    mate = lane + 1 - 2 * core
    across = lax.rem(lane + 2, lm)
    order = near_first(me)
    mine = aligned(me * block, block)
    sends = []

    def launch(copy):
        copy.start()
        sends.append(copy)

    def portion(buf, sems, stage, k, shard, h, side, device):
        wide = buf.shape[1] // 2
        columns = pl.ds(0, 2 * wide) if h is None else aligned(h * wide, wide)
        ref = buf.at[aligned(shard * block + side * part, part), columns]
        return pltpu.make_async_remote_copy(
            src_ref=ref, dst_ref=ref, send_sem=sems.at[0, stage, k],
            recv_sem=sems.at[1, stage, shard], device_id=device, device_id_type=MESH,
        )

    def routes(ways):
        yield mate, half, 1 - core
        if ways == 4:
            yield across, 1 - half, core
            yield lm - 1 - lane, 1 - half, 1 - core

    def z_copy(buf, sems, ways, k, shard):
        h = half if ways[k] == 4 else None
        return portion(buf, sems, 0, k, shard, h, core, {"dp": order[k]})

    def spread(buf, sems, ways):
        for k in range(1, dp):
            launch(z_copy(buf, sems, ways, k, me))

    def pass_on(buf, sems, ways, blocks=range(1, 4)):
        for k in blocks:
            z_copy(buf, sems, ways, k, order[k]).wait_recv()
            h = half if ways[k] == 4 else None
            for stage, (target, _, _) in reversed(list(enumerate(routes(ways[k]), 1))):
                launch(portion(buf, sems, stage, k, order[k], h, core, {"landmark": target}))

    def gather(buf, sems, ways, blocks=range(1, 4)):
        for k in blocks:
            for stage, (target, h, side) in enumerate(routes(ways[k]), 1):
                h = h if ways[k] == 4 else None
                portion(buf, sems, stage, k, order[k], h, side, {"landmark": target}).wait_recv()

    loads[0].wait()
    u_all[mine, :] = unit_rows(images_ref[...].astype(jnp.float32)).astype(jnp.bfloat16)
    pl.semaphore_wait(barrier, dp - 1 + lm - 1)
    spread(u_all, u_sems, U_WAYS)
    loads[1].wait()
    loads[2].wait()
    picks = (
        lax.broadcasted_iota(jnp.int32, (block, block), 0) == order_ref[...]
    ).astype(jnp.bfloat16)
    paired = lax.dot_general(
        picks, captions_ref[...], (((0,), (0,)), ((), ())), preferred_element_type=jnp.float32
    )
    c_all[mine, :] = unit_rows(paired).astype(jnp.bfloat16)

    loads[3].wait()
    for at in range(cuts):
        mark_loads[at].wait()
        rows = pl.ds(at * piece, piece)
        scaled_keys(marks.at[rows, :], gamma_ref.at[:, rows], keys.at[rows, :])

    def hop(shard, j, send, target, rows):
        if j < FIRST:
            ref = raw.at[shard, pl.ds(j * block, block), pl.ds(0, rows)]
        else:
            ref = raw.at[
                shard, pl.ds(FIRST * block, pairs - FIRST * block),
                pl.ds((j - FIRST) * piece, piece),
            ]
        return pltpu.make_async_remote_copy(
            src_ref=ref, dst_ref=ref,
            send_sem=send.at[shard, j], recv_sem=f_recv.at[shard, j],
            device_id={"dp": target}, device_id_type=MESH,
        )

    def to_right(shard, j, rows=own):
        return hop(shard, j, right_send, jnp.minimum(me + 1, dp - 1), rows)

    def to_left(shard, j, rows=own):
        return hop(shard, j, left_send, jnp.maximum(me - 1, 0), rows)

    def send_own(j):
        @pl.when(me < dp - 1)
        def _():
            to_right(me, j).start()

        @pl.when(me > 0)
        def _():
            to_left(me, j).start()

    def features(units, rows):
        inner = lax.dot_general(
            units, keys[rows, :], (((1,), (1,)), ((), ())), preferred_element_type=jnp.float32
        )
        return jnp.exp(inner).astype(jnp.bfloat16)

    def first_block(j):
        units = u_all[aligned(order[j] * block, block), :]
        raw[me, j * block : (j + 1) * block, :] = features(units, pl.ds(0, own))
        if HOLD == 0 or j:
            send_own(j)

    first_block(0)
    if C_AT == 0:
        spread(c_all, c_sems, C_WAYS)
    loads[4].wait()
    loads[5].wait()
    if not SWAP:
        scaled_keys(words, text_gamma_ref, text_keys)
    hops = dp - 2 if late == cuts else dp - 1
    early_rows = own - late * piece

    def rows_of(d):
        return early_rows if d == dp - 1 else own

    def last_of(d):
        return FIRST - 1 + (cuts - late if d == dp - 1 else cuts)

    def receive(d, j):
        @pl.when(me + d < dp)
        def _():
            to_right(me + d, j, rows_of(d)).wait_recv()
            if d < hops and j <= last_of(d + 1):

                @pl.when(me > 0)
                def _():
                    to_left(me + d, j, rows_of(d + 1)).start()

        @pl.when(me - d >= 0)
        def _():
            to_left(me - d, j, rows_of(d)).wait_recv()
            if d < hops and j <= last_of(d + 1):

                @pl.when(me < dp - 1)
                def _():
                    to_right(me - d, j, rows_of(d + 1)).start()

    pass_on(u_all, u_sems, U_WAYS, range(1, dp if HOLD else FIRST))
    if HOLD:
        send_own(0)
    if SWAP:
        scaled_keys(words, text_gamma_ref, text_keys)
    for j in range(1, FIRST):
        gather(u_all, u_sems, U_WAYS, (j,))
        first_block(j)
    if C_AT == 1:
        spread(c_all, c_sems, C_WAYS)
    pass_on(u_all, u_sems, U_WAYS, range(dp if HOLD else FIRST, dp))
    if FORWARD == 0:
        receive(1, 0)
    gather(u_all, u_sems, U_WAYS, range(FIRST, dp))
    others = jnp.concatenate(
        [u_all[aligned(order[k] * block, block), :] for k in range(FIRST, dp)], axis=0
    )
    for j in range(1, cuts + 1):
        rows = pl.ds((j - 1) * piece, piece)
        raw[me, FIRST * block :, (j - 1) * piece : j * piece] = features(others, rows)
        send_own(j + FIRST - 1)
        if j == C_ON:
            pass_on(c_all, c_sems, C_WAYS)

    def standardize(shard, j, mean_ref=None):
        for at in range((j - 1) * piece, j * piece, 128):
            columns = slice(at, at + 128)
            feats = jnp.concatenate(
                [
                    raw[shard, aligned(place(shard, p) * block, block), columns]
                    for p in range(dp)
                ],
                axis=0,
            )
            rows, mean = standard_columns(feats.astype(jnp.float32), 1.0)
            f_all[aligned(shard * own + at, 128), :] = rows
            if mean_ref is not None:
                mean_ref[:, columns] = mean

    for j in range(FIRST):
        if FORWARD or j:
            receive(1, j)
    for j in range(1, cuts + 1):
        standardize(me, j, image_mean_ref)
    def g_copy(k, shard, target):
        rows = aligned(shard * text_own, text_own)
        return pltpu.make_async_remote_copy(
            src_ref=g_all.at[rows, :], dst_ref=g_all.at[rows, :],
            send_sem=g_send.at[k], recv_sem=g_recv.at[shard],
            device_id={"landmark": target}, device_id_type=MESH,
        )

    def text_features():
        gather(c_all, c_sems, C_WAYS)
        inner = lax.dot_general(
            c_all[...], text_keys[...], (((1,), (1,)), ((), ())), preferred_element_type=jnp.float32
        )
        rows, text_mean_ref[...] = standard_columns(
            jnp.exp(inner).astype(jnp.bfloat16).astype(jnp.float32), 1.0 / math.sqrt(pairs)
        )
        g_all[aligned(lane * text_own, text_own), :] = rows
        for k in range(1, lm):
            launch(g_copy(k - 1, lane, lax.rem(lane + k, lm)))

    def own_product():
        for k in range(1, lm):
            shard = lax.rem(lane + lm - k, lm)
            g_copy(k - 1, shard, lane).wait_recv()
        for at in range(0, z_own.shape[0], 256):
            z_own[at : at + 256, :] = lax.dot_general(
                f_all[aligned(me * own + at, 256), :], g_all[...],
                (((1,), (1,)), ((), ())), preferred_element_type=jnp.float32,
            )

    for d in range(1, hops + 1):
        for j in range(FIRST if d == 1 else 0, last_of(d) + 1):
            receive(d, j)
            if d == 1 and j == G_AT:
                text_features()
            if d == hops and j == Z_AT:
                own_product()
            if j < FIRST:
                continue
            cut = j - FIRST + 1

            @pl.when(me - d >= 0)
            def _():
                standardize(me - d, cut)

            @pl.when(me + d < dp)
            def _():
                standardize(me + d, cut)

            if d == dp - 2 and cut > cuts - late:
                at = (cut - 1) * piece
                rows = pl.ds(at - early_rows, piece)

                @pl.when(me == dp - 2)
                def _():
                    relay[rows, :] = f_all[pl.ds(at, piece), :]

                @pl.when(me == 1)
                def _():
                    relay[rows, :] = f_all[pl.ds((dp - 1) * own + at, piece), :]

    for copy in sends:
        copy.wait_send()
    for d in range(hops):

        @pl.when(jnp.logical_and(me >= d, me < dp - 1))
        def _():
            for j in range(last_of(d + 1) + 1):
                to_right(me - d, j, rows_of(d + 1)).wait_send()

        @pl.when(jnp.logical_and(me < dp - d, me > 0))
        def _():
            for j in range(last_of(d + 1) + 1):
                to_left(me + d, j, rows_of(d + 1)).wait_send()


def product_kernel(
    tile, slots, dp, late_rows, f_ref, g_ref, image_mean_in, text_mean_in, *refs
):
    z_own = refs[0] if late_rows else None
    z_hbm, image_mean_ref, text_mean_ref, buf, sem, extra_sem = refs[-6:]
    means = [
        pltpu.make_async_copy(image_mean_in, image_mean_ref, extra_sem.at[0]),
        pltpu.make_async_copy(text_mean_in, text_mean_ref, extra_sem.at[1]),
    ]
    total = f_ref.shape[0]
    own = total // dp
    steps = (total - late_rows) // tile
    edge = own - late_rows
    if late_rows:
        me = lax.axis_index("dp")
        ready = z_own.shape[0]
        steps -= ready // tile
        mine = pl.ds(pl.multiple_of(me * own, ready), ready)
        means.insert(0, pltpu.make_async_copy(z_own, z_hbm.at[mine, :], extra_sem.at[2]))
    for copy in means:
        copy.start()

    def rows(at):
        start = at * tile
        if late_rows:
            skip = jnp.logical_and(me > 0, start >= edge)
            start = start + jnp.where(skip, late_rows, 0)
            start = start + jnp.where(start >= me * own, ready, 0)
        return pl.ds(pl.multiple_of(start, tile), tile)

    def out(at):
        slot = lax.rem(at, slots)
        return pltpu.make_async_copy(buf.at[slot], z_hbm.at[rows(at), :], sem.at[slot])

    def step(at, carry):
        @pl.when(at >= slots)
        def _():
            out(at - slots).wait()

        buf[lax.rem(at, slots)] = lax.dot_general(
            f_ref[rows(at), :], g_ref[...], (((1,), (1,)), ((), ())),
            preferred_element_type=jnp.float32,
        )
        out(at).start()
        return carry

    lax.fori_loop(0, steps, step, 0)
    for at in range(max(0, steps - slots), steps):
        out(jnp.int32(at)).wait()
    for copy in means:
        copy.wait()


def late_kernel(tile, dp, f_ref, got_ref, g_ref, z_in, z_hbm, buf, sem):
    me = lax.axis_index("dp")
    late_rows = got_ref.shape[0]
    own = f_ref.shape[0] // dp
    first = jnp.where(me == 0, dp * own, own) - late_rows
    inner = jnp.logical_and(me > 0, me < dp - 1)

    def rows(at):
        return pl.ds(pl.multiple_of(first + at * tile, tile), tile)

    def out(at):
        return pltpu.make_async_copy(buf.at[at], z_hbm.at[rows(at), :], sem.at[at])

    for at in range(late_rows // tile):
        buf[at] = lax.dot_general(
            jnp.where(inner, f_ref[rows(at), :], got_ref[pl.ds(at * tile, tile), :]),
            g_ref[...], (((1,), (1,)), ((), ())), preferred_element_type=jnp.float32,
        )
        out(at).start()
    for at in range(late_rows // tile):
        out(at).wait()


def per_device(
    images, captions, caption_of, image_landmarks, image_gamma, text_landmarks, text_gamma
):
    dp, lm = lax.axis_size("dp"), lax.axis_size("landmark")
    block, width = images.shape
    text_width = captions.shape[1]
    own, text_own = image_landmarks.shape[0], text_landmarks.shape[0]
    pairs = block * dp
    bf16, f32 = jnp.bfloat16, jnp.float32
    vmem = pl.BlockSpec(memory_space=pltpu.VMEM)
    hbm = pl.BlockSpec(memory_space=pltpu.HBM)
    dma = pltpu.SemaphoreType.DMA
    blocks = (
        dp == 4 and lm == 4 and block % 32 == 0 and own % 512 == 0 and text_own % 128 == 0
        and width % 256 == 0 and text_width % 256 == 0
    )
    late_rows = own * LATE // 4 if blocks else 0
    operands = [
        pltpu.with_memory_space_constraint(value, pltpu.HBM)
        for value in (
            images, captions, caption_of[None, :], image_landmarks, image_gamma[None, :],
            text_landmarks, text_gamma[None, :],
        )
    ]
    results = [
        jax.ShapeDtypeStruct((dp * own, pairs), bf16),
        jax.ShapeDtypeStruct((lm * text_own, pairs), bf16),
        jax.ShapeDtypeStruct((1, own), f32),
        jax.ShapeDtypeStruct((1, text_own), f32),
    ]
    held = [
        pltpu.VMEM((block, width), bf16),
        pltpu.VMEM((block, text_width), bf16),
        pltpu.VMEM((1, block), jnp.int32),
        pltpu.VMEM((own, width), bf16),
        pltpu.VMEM((1, own), f32),
        pltpu.VMEM((text_own, text_width), bf16),
        pltpu.VMEM((1, text_own), f32),
    ]
    params = pltpu.CompilerParams(
        collective_id=0, has_side_effects=True, vmem_limit_bytes=40 * 2**20
    )
    if blocks:
        f, g, image_mean, text_mean, relay, *z_own = pl.pallas_call(
            functools.partial(blocks_kernel, LATE),
            out_shape=results + [
                jax.ShapeDtypeStruct((late_rows, pairs), bf16),
                jax.ShapeDtypeStruct((own * READY // 4, lm * text_own), f32),
            ],
            in_specs=[hbm] * 7,
            out_specs=[vmem] * 6,
            scratch_shapes=held + [
                pltpu.VMEM((pairs, width), bf16),
                pltpu.VMEM((pairs, text_width), bf16),
                pltpu.VMEM((own, width), bf16),
                pltpu.VMEM((text_own, text_width), bf16),
                pltpu.VMEM((dp, pairs, own), bf16),
                dma((6,)), dma((4,)), dma((2, 4, dp)), dma((2, 4, dp)),
                dma((dp, 6)), dma((dp, 6)), dma((dp, 6)),
                dma((lm,)), dma((lm,)),
            ],
            compiler_params=params,
            name="block_exchange",
        )(*operands)
    else:
        z_own = []
        split = 2 if lm % 2 == 0 else 1
        chunks = max(1, own // 256)
        f, g, image_mean, text_mean = pl.pallas_call(
            functools.partial(exchange_kernel, dp, lm, split, chunks),
            out_shape=results,
            in_specs=[hbm] * 7,
            out_specs=[vmem] * 4,
            scratch_shapes=held + [
                pltpu.VMEM((pairs, width), bf16),
                pltpu.VMEM((pairs, text_width), bf16),
                pltpu.VMEM((own, width), bf16),
                pltpu.VMEM((text_own, text_width), bf16),
                dma((7,)),
                dma((dp,)), dma((dp,)), dma((dp,)), dma((dp,)),
                dma((dp,)), dma((dp,)), dma((dp,)), dma((dp,)),
                dma((dp, chunks)), dma((dp, chunks)), dma((dp, chunks)),
                dma((lm,)), dma((lm,)),
            ],
            compiler_params=params,
            name="exchange",
        )(*operands)
    rows, columns = dp * own, lm * text_own
    ahead = rows - late_rows
    tile = math.gcd(math.gcd(own, own - late_rows), 256)
    slots = min(SLOTS, ahead // tile)
    if late_rows:
        got = lax.ppermute(relay, "dp", ((dp - 2, dp - 1), (1, 0)))
    zstat, image_mean, text_mean = pl.pallas_call(
        functools.partial(product_kernel, tile, slots, dp, late_rows),
        out_shape=(
            jax.ShapeDtypeStruct((rows, columns), f32),
            jax.ShapeDtypeStruct((1, own), f32),
            jax.ShapeDtypeStruct((1, text_own), f32),
        ),
        in_specs=[vmem] * (4 + len(z_own)),
        out_specs=(hbm, hbm, hbm),
        scratch_shapes=[pltpu.VMEM((slots, tile, columns), f32), dma((slots,)), dma((3,))],
        compiler_params=pltpu.CompilerParams(vmem_limit_bytes=40 * 2**20),
        cost_estimate=pl.CostEstimate(
            flops=2 * ahead * columns * pairs, bytes_accessed=4 * ahead * columns, transcendentals=0
        ),
        name="product",
    )(f, g, image_mean, text_mean, *z_own)
    if late_rows:
        zstat = pl.pallas_call(
            functools.partial(late_kernel, tile, dp),
            out_shape=jax.ShapeDtypeStruct((rows, columns), f32),
            in_specs=[vmem, vmem, vmem, hbm],
            out_specs=hbm,
            scratch_shapes=[
                pltpu.VMEM((late_rows // tile, tile, columns), f32), dma((late_rows // tile,)),
            ],
            input_output_aliases={3: 0},
            compiler_params=pltpu.CompilerParams(vmem_limit_bytes=40 * 2**20),
            cost_estimate=pl.CostEstimate(
                flops=2 * late_rows * columns * pairs, bytes_accessed=4 * late_rows * columns,
                transcendentals=0,
            ),
            name="late_product",
        )(f, got, g, zstat)
    return (zstat, image_mean[0], text_mean[0])


def solution(mesh):
    in_specs = (
        P(("groups", "dp"), None),
        P(("groups", "dp"), None),
        P(("groups", "dp")),
        P(("landmark", "dp"), None),
        P(("landmark", "dp")),
        P(("dp", "landmark"), None),
        P(("dp", "landmark")),
    )
    out_specs = (
        P(("groups", "landmark"), "dp"),
        P(("groups", "landmark", "dp")),
        P(("groups", "dp", "landmark")),
    )
    return jax.shard_map(
        per_device, mesh=mesh, in_specs=in_specs, out_specs=out_specs, check_vma=False
    )
```

```python
import functools
import math

import jax
import jax.numpy as jnp
from jax import lax
from jax.experimental import pallas as pl
from jax.experimental.pallas import tpu as pltpu
from jax.sharding import PartitionSpec as P

MESH = pl.DeviceIdType.MESH
EPS = 1e-06
CUTS = 2
LATE = 1
FIRST = 2
U_WAYS = (0, 2, 2, 2)
C_WAYS = (0, 4, 4, 4)
TILE, LATE_TILE, SLOTS = 256, 128, 6


def unit_rows(wide):
    return wide * lax.rsqrt(jnp.sum(wide * wide, axis=-1, keepdims=True) + EPS)


def diagonal(size):
    return lax.broadcasted_iota(jnp.int32, (size, size), 0) == lax.broadcasted_iota(
        jnp.int32, (size, size), 1
    )


def scaled_keys(marks_ref, gamma_ref, keys_ref):
    total = marks_ref.shape[0]
    size = min(128, total)

    def step(at, carry):
        rows = pl.ds(pl.multiple_of(at * size, size), size)
        unit = unit_rows(marks_ref[rows, :].astype(jnp.float32))
        gamma = jnp.sum(
            jnp.where(diagonal(size), gamma_ref[:, rows], 0.0), axis=1, keepdims=True
        )
        keys_ref[rows, :] = (unit * gamma).astype(jnp.bfloat16)
        return carry

    lax.fori_loop(0, total // size, step, 0)


def standard_features(keys, units, mean_ref, start, scale):
    rows, pairs = keys.shape[0], units.shape[0]
    inner = lax.dot_general(
        keys, units, (((1,), (1,)), ((), ())), preferred_element_type=jnp.float32
    )
    feats = jnp.exp(inner).astype(jnp.bfloat16).astype(jnp.float32)
    mean = jnp.sum(feats, axis=1, keepdims=True) * (1.0 / pairs)
    dev = feats - mean
    var = jnp.sum(dev * dev, axis=1, keepdims=True) * (1.0 / pairs)
    size = min(128, rows)
    for at in range(0, rows, size):
        mean_ref[:, start + at : start + at + size] = jnp.sum(
            jnp.where(diagonal(size), mean[at : at + size], 0.0), axis=0, keepdims=True
        )
    return (dev * (lax.rsqrt(var + EPS) * scale)).astype(jnp.bfloat16)


def exchange_kernel(
    dp, lm, split, chunks,
    images_hbm, captions_hbm, order_hbm, marks_hbm, gamma_hbm, words_hbm, text_gamma_hbm,
    f_all, g_all, image_mean_ref, text_mean_ref,
    images_ref, captions_ref, order_ref, marks, gamma_ref, words, text_gamma_ref,
    u_all, c_all, keys, text_keys,
    load_sem,
    u_send, u_recv, u_mate_send, u_mate_recv,
    c_send, c_recv, c_mate_send, c_mate_recv,
    right_send, left_send, f_recv, g_send, g_recv,
):
    me, lane = lax.axis_index("dp"), lax.axis_index("landmark")
    block = images_ref.shape[0]
    part = block // split
    own = marks.shape[0]
    text_own = words.shape[0]
    pairs = u_all.shape[0]
    rows_each = own // chunks

    loads = [
        pltpu.make_async_copy(src, dst, load_sem.at[at])
        for at, (src, dst) in enumerate((
            (images_hbm, images_ref), (marks_hbm, marks), (gamma_hbm, gamma_ref),
            (captions_hbm, captions_ref), (order_hbm, order_ref),
            (words_hbm, words), (text_gamma_hbm, text_gamma_ref),
        ))
    ]
    for load in loads:
        load.start()

    barrier = pltpu.get_barrier_semaphore()
    for k in range(1, dp):
        pl.semaphore_signal(
            barrier, inc=1, device_id={"dp": lax.rem(me + k, dp)}, device_id_type=MESH
        )
    for k in range(1, lm):
        pl.semaphore_signal(
            barrier, inc=1, device_id={"landmark": lax.rem(lane + k, lm)}, device_id_type=MESH
        )

    mine = pl.ds(pl.multiple_of(me * block, block), block)
    loads[0].wait()
    u_all[mine, :] = unit_rows(images_ref[...].astype(jnp.float32)).astype(jnp.bfloat16)
    pl.semaphore_wait(barrier, dp - 1 + lm - 1)

    side = lax.rem(lane, split)
    mate = lane + 1 - 2 * side

    def half(shard):
        return pl.ds(pl.multiple_of(shard * block + side * part, part), part)

    def other_half(shard):
        return pl.ds(pl.multiple_of(shard * block + (1 - side) * part, part), part)

    def block_copy(buf, send, recv, k, shard, target):
        return pltpu.make_async_remote_copy(
            src_ref=buf.at[half(shard), :], dst_ref=buf.at[half(shard), :],
            send_sem=send.at[k], recv_sem=recv.at[shard],
            device_id={"dp": target}, device_id_type=MESH,
        )

    def mate_copy(buf, send, recv, k, shard, rows):
        return pltpu.make_async_remote_copy(
            src_ref=buf.at[rows, :], dst_ref=buf.at[rows, :],
            send_sem=send.at[k], recv_sem=recv.at[shard],
            device_id={"landmark": mate}, device_id_type=MESH,
        )

    sends = []

    def spread(buf, send, recv):
        for k in range(1, dp):
            copy = block_copy(buf, send, recv, k - 1, me, lax.rem(me + k, dp))
            copy.start()
            sends.append(copy)

    spread(u_all, u_send, u_recv)

    def collect(buf, send, recv, mate_send, mate_recv):
        for k in range(1, dp):
            shard = lax.rem(me + dp - k, dp)
            block_copy(buf, send, recv, k - 1, shard, me).wait_recv()
            if split > 1:
                copy = mate_copy(buf, mate_send, mate_recv, k - 1, shard, half(shard))
                copy.start()
                sends.append(copy)
        if split > 1:
            for k in range(1, dp):
                shard = lax.rem(me + dp - k, dp)
                mate_copy(
                    buf, mate_send, mate_recv, k - 1, shard, other_half(shard)
                ).wait_recv()

    loads[3].wait()
    loads[4].wait()
    picks = (
        lax.broadcasted_iota(jnp.int32, (block, block), 0) == order_ref[...]
    ).astype(jnp.bfloat16)
    paired = lax.dot_general(
        picks, captions_ref[...], (((0,), (0,)), ((), ())), preferred_element_type=jnp.float32
    )
    c_all[mine, :] = unit_rows(paired).astype(jnp.bfloat16)
    spread(c_all, c_send, c_recv)
    loads[1].wait()
    loads[2].wait()
    scaled_keys(marks, gamma_ref, keys)
    def f_rows(shard, c):
        return pl.ds(pl.multiple_of(shard * own + c * rows_each, rows_each), rows_each)

    def hop(shard, c, send, target):
        return pltpu.make_async_remote_copy(
            src_ref=f_all.at[f_rows(shard, c), :], dst_ref=f_all.at[f_rows(shard, c), :],
            send_sem=send.at[shard, c], recv_sem=f_recv.at[shard, c],
            device_id={"dp": target}, device_id_type=MESH,
        )

    def to_right(shard, c):
        return hop(shard, c, right_send, jnp.minimum(me + 1, dp - 1))

    def to_left(shard, c):
        return hop(shard, c, left_send, jnp.maximum(me - 1, 0))

    collect(u_all, u_send, u_recv, u_mate_send, u_mate_recv)
    for c in range(chunks):
        at = c * rows_each
        f_all[f_rows(me, c), :] = standard_features(
            keys[at : at + rows_each, :], u_all[...], image_mean_ref, at, 1.0
        )

        @pl.when(me < dp - 1)
        def _():
            to_right(me, c).start()

        @pl.when(me > 0)
        def _():
            to_left(me, c).start()

    loads[5].wait()
    loads[6].wait()
    scaled_keys(words, text_gamma_ref, text_keys)
    collect(c_all, c_send, c_recv, c_mate_send, c_mate_recv)
    text_mine = pl.ds(pl.multiple_of(lane * text_own, text_own), text_own)
    g_all[text_mine, :] = standard_features(
        text_keys[...], c_all[...], text_mean_ref, 0, 1.0 / math.sqrt(pairs)
    )

    def g_copy(k, shard, target):
        rows = pl.ds(pl.multiple_of(shard * text_own, text_own), text_own)
        return pltpu.make_async_remote_copy(
            src_ref=g_all.at[rows, :], dst_ref=g_all.at[rows, :],
            send_sem=g_send.at[k], recv_sem=g_recv.at[shard],
            device_id={"landmark": target}, device_id_type=MESH,
        )

    for k in range(1, lm):
        copy = g_copy(k - 1, lane, lax.rem(lane + k, lm))
        copy.start()
        sends.append(copy)

    for d in range(1, dp):
        for c in range(chunks):

            @pl.when(me - d >= 0)
            def _():
                to_left(me - d, c).wait_recv()

                @pl.when(me < dp - 1)
                def _():
                    to_right(me - d, c).start()

            @pl.when(me + d < dp)
            def _():
                to_right(me + d, c).wait_recv()

                @pl.when(me > 0)
                def _():
                    to_left(me + d, c).start()

    for k in range(1, lm):
        shard = lax.rem(lane + lm - k, lm)
        g_copy(k - 1, shard, lane).wait_recv()

    for copy in sends:
        copy.wait_send()
    for shard in range(dp):
        for c in range(chunks):

            @pl.when(jnp.logical_and(shard <= me, me < dp - 1))
            def _():
                to_right(shard, c).wait_send()

            @pl.when(jnp.logical_and(shard >= me, me > 0))
            def _():
                to_left(shard, c).wait_send()


def near_first(shard):
    return (
        shard,
        shard + 1 - 2 * lax.rem(shard, 2),
        2 - shard // 2,
        3 - 3 * (shard // 2),
    )


def place(shard, p):
    upper = shard // 2
    same = 1 - (upper - p // 2) * (upper - p // 2)
    far = (1 - upper) * p + upper * (3 - p)
    return same * (p - shard) * (p - shard) + (1 - same) * far


def aligned(start, size):
    return pl.ds(pl.multiple_of(start, size), size)


def standard_columns(feats, scale):
    pairs = feats.shape[0]
    mean = jnp.sum(feats, axis=0, keepdims=True) * (1.0 / pairs)
    dev = feats - mean
    var = jnp.sum(dev * dev, axis=0, keepdims=True) * (1.0 / pairs)
    return jnp.transpose(dev * (lax.rsqrt(var + EPS) * scale)).astype(jnp.bfloat16), mean


def blocks_kernel(
    late,
    images_hbm, captions_hbm, order_hbm, marks_hbm, gamma_hbm, words_hbm, text_gamma_hbm,
    f_all, g_all, image_mean_ref, text_mean_ref, relay, z_own,
    images_ref, captions_ref, order_ref, marks, gamma_ref, words, text_gamma_ref,
    u_all, c_all, keys, text_keys, raw,
    load_sem, mark_sem, u_sems, c_sems,
    right_send, left_send, f_recv, g_send, g_recv,
):
    dp, lm, cuts = 4, 4, CUTS
    me, lane = lax.axis_index("dp"), lax.axis_index("landmark")
    block = images_ref.shape[0]
    part = block // 2
    own = marks.shape[0]
    text_own = words.shape[0]
    pairs = block * dp
    piece = own // cuts

    loads = [
        pltpu.make_async_copy(src, dst, load_sem.at[at])
        for at, (src, dst) in enumerate((
            (images_hbm, images_ref), (captions_hbm, captions_ref), (order_hbm, order_ref),
            (gamma_hbm, gamma_ref), (words_hbm, words), (text_gamma_hbm, text_gamma_ref),
        ))
    ]
    mark_loads = [
        pltpu.make_async_copy(
            marks_hbm.at[pl.ds(at * piece, piece), :], marks.at[pl.ds(at * piece, piece), :],
            mark_sem.at[at],
        )
        for at in range(cuts)
    ]
    loads[0].start()
    barrier = pltpu.get_barrier_semaphore()
    for k in range(1, dp):
        pl.semaphore_signal(
            barrier, inc=1, device_id={"dp": lax.rem(me + k, dp)}, device_id_type=MESH
        )
    for k in range(1, lm):
        pl.semaphore_signal(
            barrier, inc=1, device_id={"landmark": lax.rem(lane + k, lm)}, device_id_type=MESH
        )
    for load in loads[1:4] + mark_loads + loads[4:]:
        load.start()

    half, core = lane // 2, lax.rem(lane, 2)
    mate = lane + 1 - 2 * core
    across = lax.rem(lane + 2, lm)
    order = near_first(me)
    mine = aligned(me * block, block)
    sends = []

    def launch(copy):
        copy.start()
        sends.append(copy)

    def portion(buf, sems, stage, k, shard, h, side, device):
        wide = buf.shape[1] // 2
        columns = pl.ds(0, 2 * wide) if h is None else aligned(h * wide, wide)
        ref = buf.at[aligned(shard * block + side * part, part), columns]
        return pltpu.make_async_remote_copy(
            src_ref=ref, dst_ref=ref, send_sem=sems.at[0, stage, k],
            recv_sem=sems.at[1, stage, shard], device_id=device, device_id_type=MESH,
        )

    def routes(ways):
        yield mate, half, 1 - core
        if ways == 4:
            yield across, 1 - half, core
            yield lm - 1 - lane, 1 - half, 1 - core

    def z_copy(buf, sems, ways, k, shard):
        h = half if ways[k] == 4 else None
        return portion(buf, sems, 0, k, shard, h, core, {"dp": order[k]})

    def spread(buf, sems, ways):
        for k in range(1, dp):
            launch(z_copy(buf, sems, ways, k, me))

    def pass_on(buf, sems, ways, blocks=range(1, 4)):
        for k in blocks:
            z_copy(buf, sems, ways, k, order[k]).wait_recv()
            h = half if ways[k] == 4 else None
            for stage, (target, _, _) in reversed(list(enumerate(routes(ways[k]), 1))):
                launch(portion(buf, sems, stage, k, order[k], h, core, {"landmark": target}))

    def gather(buf, sems, ways, blocks=range(1, 4)):
        for k in blocks:
            for stage, (target, h, side) in enumerate(routes(ways[k]), 1):
                h = h if ways[k] == 4 else None
                portion(buf, sems, stage, k, order[k], h, side, {"landmark": target}).wait_recv()

    loads[0].wait()
    u_all[mine, :] = unit_rows(images_ref[...].astype(jnp.float32)).astype(jnp.bfloat16)
    pl.semaphore_wait(barrier, dp - 1 + lm - 1)
    spread(u_all, u_sems, U_WAYS)
    loads[1].wait()
    loads[2].wait()
    picks = (
        lax.broadcasted_iota(jnp.int32, (block, block), 0) == order_ref[...]
    ).astype(jnp.bfloat16)
    paired = lax.dot_general(
        picks, captions_ref[...], (((0,), (0,)), ((), ())), preferred_element_type=jnp.float32
    )
    c_all[mine, :] = unit_rows(paired).astype(jnp.bfloat16)

    loads[3].wait()
    for at in range(cuts):
        mark_loads[at].wait()
        rows = pl.ds(at * piece, piece)
        scaled_keys(marks.at[rows, :], gamma_ref.at[:, rows], keys.at[rows, :])

    def hop(shard, j, send, target, rows):
        if j < FIRST:
            ref = raw.at[shard, pl.ds(j * block, block), pl.ds(0, rows)]
        else:
            ref = raw.at[
                shard, pl.ds(FIRST * block, pairs - FIRST * block),
                pl.ds((j - FIRST) * piece, piece),
            ]
        return pltpu.make_async_remote_copy(
            src_ref=ref, dst_ref=ref,
            send_sem=send.at[shard, j], recv_sem=f_recv.at[shard, j],
            device_id={"dp": target}, device_id_type=MESH,
        )

    def to_right(shard, j, rows=own):
        return hop(shard, j, right_send, jnp.minimum(me + 1, dp - 1), rows)

    def to_left(shard, j, rows=own):
        return hop(shard, j, left_send, jnp.maximum(me - 1, 0), rows)

    def send_own(j):
        @pl.when(me < dp - 1)
        def _():
            to_right(me, j).start()

        @pl.when(me > 0)
        def _():
            to_left(me, j).start()

    def features(units, rows):
        inner = lax.dot_general(
            units, keys[rows, :], (((1,), (1,)), ((), ())), preferred_element_type=jnp.float32
        )
        return jnp.exp(inner).astype(jnp.bfloat16)

    def first_block(j):
        units = u_all[aligned(order[j] * block, block), :]
        raw[me, j * block : (j + 1) * block, :] = features(units, pl.ds(0, own))
        send_own(j)

    first_block(0)
    spread(c_all, c_sems, C_WAYS)
    loads[4].wait()
    loads[5].wait()
    scaled_keys(words, text_gamma_ref, text_keys)
    hops = dp - 2 if late == cuts else dp - 1
    early_rows = own - late * piece

    def rows_of(d):
        return early_rows if d == dp - 1 else own

    def last_of(d):
        return FIRST - 1 + (cuts - late if d == dp - 1 else cuts)

    def receive(d, j):
        @pl.when(me + d < dp)
        def _():
            to_right(me + d, j, rows_of(d)).wait_recv()
            if d < hops and j <= last_of(d + 1):

                @pl.when(me > 0)
                def _():
                    to_left(me + d, j, rows_of(d + 1)).start()

        @pl.when(me - d >= 0)
        def _():
            to_left(me - d, j, rows_of(d)).wait_recv()
            if d < hops and j <= last_of(d + 1):

                @pl.when(me < dp - 1)
                def _():
                    to_right(me - d, j, rows_of(d + 1)).start()

    pass_on(u_all, u_sems, U_WAYS, range(1, FIRST))
    for j in range(1, FIRST):
        gather(u_all, u_sems, U_WAYS, (j,))
        first_block(j)
    pass_on(u_all, u_sems, U_WAYS, range(FIRST, dp))
    gather(u_all, u_sems, U_WAYS, range(FIRST, dp))
    others = jnp.concatenate(
        [u_all[aligned(order[k] * block, block), :] for k in range(FIRST, dp)], axis=0
    )
    for j in range(1, cuts + 1):
        rows = pl.ds((j - 1) * piece, piece)
        raw[me, FIRST * block :, (j - 1) * piece : j * piece] = features(others, rows)
        send_own(j + FIRST - 1)
        if j == CUTS:
            pass_on(c_all, c_sems, C_WAYS)

    def standardize(shard, j, mean_ref=None):
        for at in range((j - 1) * piece, j * piece, 128):
            columns = slice(at, at + 128)
            feats = jnp.concatenate(
                [
                    raw[shard, aligned(place(shard, p) * block, block), columns]
                    for p in range(dp)
                ],
                axis=0,
            )
            rows, mean = standard_columns(feats.astype(jnp.float32), 1.0)
            f_all[aligned(shard * own + at, 128), :] = rows
            if mean_ref is not None:
                mean_ref[:, columns] = mean

    for j in range(FIRST):
        receive(1, j)
    for j in range(1, cuts + 1):
        standardize(me, j, image_mean_ref)
    def g_copy(k, shard, target):
        rows = aligned(shard * text_own, text_own)
        return pltpu.make_async_remote_copy(
            src_ref=g_all.at[rows, :], dst_ref=g_all.at[rows, :],
            send_sem=g_send.at[k], recv_sem=g_recv.at[shard],
            device_id={"landmark": target}, device_id_type=MESH,
        )

    def text_features():
        gather(c_all, c_sems, C_WAYS)
        inner = lax.dot_general(
            c_all[...], text_keys[...], (((1,), (1,)), ((), ())), preferred_element_type=jnp.float32
        )
        rows, text_mean_ref[...] = standard_columns(
            jnp.exp(inner).astype(jnp.bfloat16).astype(jnp.float32), 1.0 / math.sqrt(pairs)
        )
        g_all[aligned(lane * text_own, text_own), :] = rows
        for k in range(1, lm):
            launch(g_copy(k - 1, lane, lax.rem(lane + k, lm)))

    def own_product():
        for k in range(1, lm):
            shard = lax.rem(lane + lm - k, lm)
            g_copy(k - 1, shard, lane).wait_recv()
        for at in range(0, z_own.shape[0], 256):
            z_own[at : at + 256, :] = lax.dot_general(
                f_all[aligned(me * own + at, 256), :], g_all[...],
                (((1,), (1,)), ((), ())), preferred_element_type=jnp.float32,
            )

    for d in range(1, hops + 1):
        for j in range(FIRST if d == 1 else 0, last_of(d) + 1):
            receive(d, j)
            if d == 1 and j == FIRST:
                text_features()
            if d == hops and j == 1:
                own_product()
            if j < FIRST:
                continue
            cut = j - FIRST + 1

            @pl.when(me - d >= 0)
            def _():
                standardize(me - d, cut)

            @pl.when(me + d < dp)
            def _():
                standardize(me + d, cut)

            if d == dp - 2 and cut > cuts - late:
                at = (cut - 1) * piece
                rows = pl.ds(at - early_rows, piece)

                @pl.when(me == dp - 2)
                def _():
                    relay[rows, :] = f_all[pl.ds(at, piece), :]

                @pl.when(me == 1)
                def _():
                    relay[rows, :] = f_all[pl.ds((dp - 1) * own + at, piece), :]

    for copy in sends:
        copy.wait_send()
    for d in range(hops):

        @pl.when(jnp.logical_and(me >= d, me < dp - 1))
        def _():
            for j in range(last_of(d + 1) + 1):
                to_right(me - d, j, rows_of(d + 1)).wait_send()

        @pl.when(jnp.logical_and(me < dp - d, me > 0))
        def _():
            for j in range(last_of(d + 1) + 1):
                to_left(me + d, j, rows_of(d + 1)).wait_send()


def product_kernel(
    tile, slots, dp, late_rows, f_ref, g_ref, image_mean_in, text_mean_in, *refs
):
    z_own = refs[0] if late_rows else None
    z_hbm, image_mean_ref, text_mean_ref, buf, sem, extra_sem = refs[-6:]
    means = [
        pltpu.make_async_copy(image_mean_in, image_mean_ref, extra_sem.at[0]),
        pltpu.make_async_copy(text_mean_in, text_mean_ref, extra_sem.at[1]),
    ]
    total = f_ref.shape[0]
    own = total // dp
    steps = (total - late_rows) // tile
    edge = own - late_rows
    if late_rows:
        me = lax.axis_index("dp")
        ready = z_own.shape[0]
        steps -= ready // tile
        mine = pl.ds(pl.multiple_of(me * own, ready), ready)
        means.insert(0, pltpu.make_async_copy(z_own, z_hbm.at[mine, :], extra_sem.at[2]))
    for copy in means:
        copy.start()

    def rows(at):
        start = at * tile
        if late_rows:
            skip = jnp.logical_and(me > 0, start >= edge)
            start = start + jnp.where(skip, late_rows, 0)
            start = start + jnp.where(start >= me * own, ready, 0)
        return pl.ds(pl.multiple_of(start, tile), tile)

    def out(at):
        slot = lax.rem(at, slots)
        return pltpu.make_async_copy(buf.at[slot], z_hbm.at[rows(at), :], sem.at[slot])

    def step(at, carry):
        @pl.when(at >= slots)
        def _():
            out(at - slots).wait()

        buf[lax.rem(at, slots)] = lax.dot_general(
            f_ref[rows(at), :], g_ref[...], (((1,), (1,)), ((), ())),
            preferred_element_type=jnp.float32,
        )
        out(at).start()
        return carry

    lax.fori_loop(0, steps, step, 0)
    for at in range(max(0, steps - slots), steps):
        out(jnp.int32(at)).wait()
    for copy in means:
        copy.wait()


def late_kernel(tile, dp, f_ref, got_ref, g_ref, z_in, z_hbm, buf, sem):
    me = lax.axis_index("dp")
    late_rows = got_ref.shape[0]
    own = f_ref.shape[0] // dp
    first = jnp.where(me == 0, dp * own, own) - late_rows
    inner = jnp.logical_and(me > 0, me < dp - 1)

    def rows(at):
        return pl.ds(pl.multiple_of(first + at * tile, tile), tile)

    def out(at):
        return pltpu.make_async_copy(buf.at[at], z_hbm.at[rows(at), :], sem.at[at])

    for at in range(late_rows // tile):
        buf[at] = lax.dot_general(
            jnp.where(inner, f_ref[rows(at), :], got_ref[pl.ds(at * tile, tile), :]),
            g_ref[...], (((1,), (1,)), ((), ())), preferred_element_type=jnp.float32,
        )
        out(at).start()
    for at in range(late_rows // tile):
        out(at).wait()


def per_device(
    images, captions, caption_of, image_landmarks, image_gamma, text_landmarks, text_gamma
):
    dp, lm = lax.axis_size("dp"), lax.axis_size("landmark")
    block, width = images.shape
    text_width = captions.shape[1]
    own, text_own = image_landmarks.shape[0], text_landmarks.shape[0]
    pairs = block * dp
    bf16, f32 = jnp.bfloat16, jnp.float32
    vmem = pl.BlockSpec(memory_space=pltpu.VMEM)
    hbm = pl.BlockSpec(memory_space=pltpu.HBM)
    dma = pltpu.SemaphoreType.DMA
    blocks = (
        dp == 4 and lm == 4 and block % 32 == 0 and own % 1024 == 0 and text_own % 128 == 0
        and width % 256 == 0 and text_width % 256 == 0
    )
    late_rows = own * LATE // CUTS if blocks else 0
    operands = [
        pltpu.with_memory_space_constraint(value, pltpu.HBM)
        for value in (
            images, captions, caption_of[None, :], image_landmarks, image_gamma[None, :],
            text_landmarks, text_gamma[None, :],
        )
    ]
    results = [
        jax.ShapeDtypeStruct((dp * own, pairs), bf16),
        jax.ShapeDtypeStruct((lm * text_own, pairs), bf16),
        jax.ShapeDtypeStruct((1, own), f32),
        jax.ShapeDtypeStruct((1, text_own), f32),
    ]
    held = [
        pltpu.VMEM((block, width), bf16),
        pltpu.VMEM((block, text_width), bf16),
        pltpu.VMEM((1, block), jnp.int32),
        pltpu.VMEM((own, width), bf16),
        pltpu.VMEM((1, own), f32),
        pltpu.VMEM((text_own, text_width), bf16),
        pltpu.VMEM((1, text_own), f32),
    ]
    params = pltpu.CompilerParams(
        collective_id=0, has_side_effects=True, vmem_limit_bytes=40 * 2**20
    )
    if blocks:
        f, g, image_mean, text_mean, relay, *z_own = pl.pallas_call(
            functools.partial(blocks_kernel, LATE),
            out_shape=results + [
                jax.ShapeDtypeStruct((late_rows, pairs), bf16),
                jax.ShapeDtypeStruct((own // 4, lm * text_own), f32),
            ],
            in_specs=[hbm] * 7,
            out_specs=[vmem] * 6,
            scratch_shapes=held + [
                pltpu.VMEM((pairs, width), bf16),
                pltpu.VMEM((pairs, text_width), bf16),
                pltpu.VMEM((own, width), bf16),
                pltpu.VMEM((text_own, text_width), bf16),
                pltpu.VMEM((dp, pairs, own), bf16),
                dma((6,)), dma((CUTS,)), dma((2, 4, dp)), dma((2, 4, dp)),
                dma((dp, FIRST + CUTS)), dma((dp, FIRST + CUTS)), dma((dp, FIRST + CUTS)),
                dma((lm,)), dma((lm,)),
            ],
            compiler_params=params,
            name="block_exchange",
        )(*operands)
    else:
        z_own = []
        split = 2 if lm % 2 == 0 else 1
        chunks = max(1, own // 256)
        f, g, image_mean, text_mean = pl.pallas_call(
            functools.partial(exchange_kernel, dp, lm, split, chunks),
            out_shape=results,
            in_specs=[hbm] * 7,
            out_specs=[vmem] * 4,
            scratch_shapes=held + [
                pltpu.VMEM((pairs, width), bf16),
                pltpu.VMEM((pairs, text_width), bf16),
                pltpu.VMEM((own, width), bf16),
                pltpu.VMEM((text_own, text_width), bf16),
                dma((7,)),
                dma((dp,)), dma((dp,)), dma((dp,)), dma((dp,)),
                dma((dp,)), dma((dp,)), dma((dp,)), dma((dp,)),
                dma((dp, chunks)), dma((dp, chunks)), dma((dp, chunks)),
                dma((lm,)), dma((lm,)),
            ],
            compiler_params=params,
            name="exchange",
        )(*operands)
    rows, columns = dp * own, lm * text_own
    ahead = rows - late_rows
    tile = math.gcd(math.gcd(own, own - late_rows), TILE)
    slots = min(SLOTS, ahead // tile)
    if late_rows:
        got = lax.ppermute(relay, "dp", ((dp - 2, dp - 1), (1, 0)))
    zstat, image_mean, text_mean = pl.pallas_call(
        functools.partial(product_kernel, tile, slots, dp, late_rows),
        out_shape=(
            jax.ShapeDtypeStruct((rows, columns), f32),
            jax.ShapeDtypeStruct((1, own), f32),
            jax.ShapeDtypeStruct((1, text_own), f32),
        ),
        in_specs=[vmem] * (4 + len(z_own)),
        out_specs=(hbm, hbm, hbm),
        scratch_shapes=[pltpu.VMEM((slots, tile, columns), f32), dma((slots,)), dma((3,))],
        compiler_params=pltpu.CompilerParams(vmem_limit_bytes=40 * 2**20),
        cost_estimate=pl.CostEstimate(
            flops=2 * ahead * columns * pairs, bytes_accessed=4 * ahead * columns, transcendentals=0
        ),
        name="product",
    )(f, g, image_mean, text_mean, *z_own)
    if late_rows:
        zstat = pl.pallas_call(
            functools.partial(late_kernel, LATE_TILE, dp),
            out_shape=jax.ShapeDtypeStruct((rows, columns), f32),
            in_specs=[vmem, vmem, vmem, hbm],
            out_specs=hbm,
            scratch_shapes=[
                pltpu.VMEM((late_rows // LATE_TILE, LATE_TILE, columns), f32), dma((late_rows // LATE_TILE,)),
            ],
            input_output_aliases={3: 0},
            compiler_params=pltpu.CompilerParams(vmem_limit_bytes=40 * 2**20),
            cost_estimate=pl.CostEstimate(
                flops=2 * late_rows * columns * pairs, bytes_accessed=4 * late_rows * columns,
                transcendentals=0,
            ),
            name="late_product",
        )(f, got, g, zstat)
    return (zstat, image_mean[0], text_mean[0])


def solution(mesh):
    in_specs = (
        P(("groups", "dp"), None),
        P(("groups", "dp"), None),
        P(("groups", "dp")),
        P(("landmark", "dp"), None),
        P(("landmark", "dp")),
        P(("dp", "landmark"), None),
        P(("dp", "landmark")),
    )
    out_specs = (
        P(("groups", "landmark"), "dp"),
        P(("groups", "landmark", "dp")),
        P(("groups", "dp", "landmark")),
    )
    return jax.shard_map(
        per_device, mesh=mesh, in_specs=in_specs, out_specs=out_specs, check_vma=False
    )
```

```python
import functools
import math

import jax
import jax.numpy as jnp
from jax import lax
from jax.experimental import pallas as pl
from jax.experimental.pallas import tpu as pltpu
from jax.sharding import PartitionSpec as P

MESH = pl.DeviceIdType.MESH
EPS = 1e-06
CUTS = 2
LATE = 1
FIRST = 2
U_WAYS = (0, 2, 2, 2)
C_WAYS = (0, 4, 4, 4)
TILE, LATE_TILE, SLOTS = 256, 128, 6


def unit_rows(wide):
    return wide * lax.rsqrt(jnp.sum(wide * wide, axis=-1, keepdims=True) + EPS)


def diagonal(size):
    return lax.broadcasted_iota(jnp.int32, (size, size), 0) == lax.broadcasted_iota(
        jnp.int32, (size, size), 1
    )


def scaled_keys(marks_ref, gamma_ref, keys_ref):
    total = marks_ref.shape[0]
    size = min(128, total)

    def step(at, carry):
        rows = pl.ds(pl.multiple_of(at * size, size), size)
        unit = unit_rows(marks_ref[rows, :].astype(jnp.float32))
        gamma = jnp.sum(
            jnp.where(diagonal(size), gamma_ref[:, rows], 0.0), axis=1, keepdims=True
        )
        keys_ref[rows, :] = (unit * gamma).astype(jnp.bfloat16)
        return carry

    lax.fori_loop(0, total // size, step, 0)


def standard_features(keys, units, mean_ref, start, scale):
    rows, pairs = keys.shape[0], units.shape[0]
    inner = lax.dot_general(
        keys, units, (((1,), (1,)), ((), ())), preferred_element_type=jnp.float32
    )
    feats = jnp.exp(inner).astype(jnp.bfloat16).astype(jnp.float32)
    mean = jnp.sum(feats, axis=1, keepdims=True) * (1.0 / pairs)
    dev = feats - mean
    var = jnp.sum(dev * dev, axis=1, keepdims=True) * (1.0 / pairs)
    size = min(128, rows)
    for at in range(0, rows, size):
        mean_ref[:, start + at : start + at + size] = jnp.sum(
            jnp.where(diagonal(size), mean[at : at + size], 0.0), axis=0, keepdims=True
        )
    return (dev * (lax.rsqrt(var + EPS) * scale)).astype(jnp.bfloat16)


def exchange_kernel(
    dp, lm, split, chunks,
    images_hbm, captions_hbm, order_hbm, marks_hbm, gamma_hbm, words_hbm, text_gamma_hbm,
    f_all, g_all, image_mean_ref, text_mean_ref,
    images_ref, captions_ref, order_ref, marks, gamma_ref, words, text_gamma_ref,
    u_all, c_all, keys, text_keys,
    load_sem,
    u_send, u_recv, u_mate_send, u_mate_recv,
    c_send, c_recv, c_mate_send, c_mate_recv,
    right_send, left_send, f_recv, g_send, g_recv,
):
    me, lane = lax.axis_index("dp"), lax.axis_index("landmark")
    block = images_ref.shape[0]
    part = block // split
    own = marks.shape[0]
    text_own = words.shape[0]
    pairs = u_all.shape[0]
    rows_each = own // chunks

    loads = [
        pltpu.make_async_copy(src, dst, load_sem.at[at])
        for at, (src, dst) in enumerate((
            (images_hbm, images_ref), (marks_hbm, marks), (gamma_hbm, gamma_ref),
            (captions_hbm, captions_ref), (order_hbm, order_ref),
            (words_hbm, words), (text_gamma_hbm, text_gamma_ref),
        ))
    ]
    for load in loads:
        load.start()

    barrier = pltpu.get_barrier_semaphore()
    for k in range(1, dp):
        pl.semaphore_signal(
            barrier, inc=1, device_id={"dp": lax.rem(me + k, dp)}, device_id_type=MESH
        )
    for k in range(1, lm):
        pl.semaphore_signal(
            barrier, inc=1, device_id={"landmark": lax.rem(lane + k, lm)}, device_id_type=MESH
        )

    mine = pl.ds(pl.multiple_of(me * block, block), block)
    loads[0].wait()
    u_all[mine, :] = unit_rows(images_ref[...].astype(jnp.float32)).astype(jnp.bfloat16)
    pl.semaphore_wait(barrier, dp - 1 + lm - 1)

    side = lax.rem(lane, split)
    mate = lane + 1 - 2 * side

    def half(shard):
        return pl.ds(pl.multiple_of(shard * block + side * part, part), part)

    def other_half(shard):
        return pl.ds(pl.multiple_of(shard * block + (1 - side) * part, part), part)

    def block_copy(buf, send, recv, k, shard, target):
        return pltpu.make_async_remote_copy(
            src_ref=buf.at[half(shard), :], dst_ref=buf.at[half(shard), :],
            send_sem=send.at[k], recv_sem=recv.at[shard],
            device_id={"dp": target}, device_id_type=MESH,
        )

    def mate_copy(buf, send, recv, k, shard, rows):
        return pltpu.make_async_remote_copy(
            src_ref=buf.at[rows, :], dst_ref=buf.at[rows, :],
            send_sem=send.at[k], recv_sem=recv.at[shard],
            device_id={"landmark": mate}, device_id_type=MESH,
        )

    sends = []

    def spread(buf, send, recv):
        for k in range(1, dp):
            copy = block_copy(buf, send, recv, k - 1, me, lax.rem(me + k, dp))
            copy.start()
            sends.append(copy)

    spread(u_all, u_send, u_recv)

    def collect(buf, send, recv, mate_send, mate_recv):
        for k in range(1, dp):
            shard = lax.rem(me + dp - k, dp)
            block_copy(buf, send, recv, k - 1, shard, me).wait_recv()
            if split > 1:
                copy = mate_copy(buf, mate_send, mate_recv, k - 1, shard, half(shard))
                copy.start()
                sends.append(copy)
        if split > 1:
            for k in range(1, dp):
                shard = lax.rem(me + dp - k, dp)
                mate_copy(
                    buf, mate_send, mate_recv, k - 1, shard, other_half(shard)
                ).wait_recv()

    loads[3].wait()
    loads[4].wait()
    picks = (
        lax.broadcasted_iota(jnp.int32, (block, block), 0) == order_ref[...]
    ).astype(jnp.bfloat16)
    paired = lax.dot_general(
        picks, captions_ref[...], (((0,), (0,)), ((), ())), preferred_element_type=jnp.float32
    )
    c_all[mine, :] = unit_rows(paired).astype(jnp.bfloat16)
    spread(c_all, c_send, c_recv)
    loads[1].wait()
    loads[2].wait()
    scaled_keys(marks, gamma_ref, keys)
    def f_rows(shard, c):
        return pl.ds(pl.multiple_of(shard * own + c * rows_each, rows_each), rows_each)

    def hop(shard, c, send, target):
        return pltpu.make_async_remote_copy(
            src_ref=f_all.at[f_rows(shard, c), :], dst_ref=f_all.at[f_rows(shard, c), :],
            send_sem=send.at[shard, c], recv_sem=f_recv.at[shard, c],
            device_id={"dp": target}, device_id_type=MESH,
        )

    def to_right(shard, c):
        return hop(shard, c, right_send, jnp.minimum(me + 1, dp - 1))

    def to_left(shard, c):
        return hop(shard, c, left_send, jnp.maximum(me - 1, 0))

    collect(u_all, u_send, u_recv, u_mate_send, u_mate_recv)
    for c in range(chunks):
        at = c * rows_each
        f_all[f_rows(me, c), :] = standard_features(
            keys[at : at + rows_each, :], u_all[...], image_mean_ref, at, 1.0
        )

        @pl.when(me < dp - 1)
        def _():
            to_right(me, c).start()

        @pl.when(me > 0)
        def _():
            to_left(me, c).start()

    loads[5].wait()
    loads[6].wait()
    scaled_keys(words, text_gamma_ref, text_keys)
    collect(c_all, c_send, c_recv, c_mate_send, c_mate_recv)
    text_mine = pl.ds(pl.multiple_of(lane * text_own, text_own), text_own)
    g_all[text_mine, :] = standard_features(
        text_keys[...], c_all[...], text_mean_ref, 0, 1.0 / math.sqrt(pairs)
    )

    def g_copy(k, shard, target):
        rows = pl.ds(pl.multiple_of(shard * text_own, text_own), text_own)
        return pltpu.make_async_remote_copy(
            src_ref=g_all.at[rows, :], dst_ref=g_all.at[rows, :],
            send_sem=g_send.at[k], recv_sem=g_recv.at[shard],
            device_id={"landmark": target}, device_id_type=MESH,
        )

    for k in range(1, lm):
        copy = g_copy(k - 1, lane, lax.rem(lane + k, lm))
        copy.start()
        sends.append(copy)

    for d in range(1, dp):
        for c in range(chunks):

            @pl.when(me - d >= 0)
            def _():
                to_left(me - d, c).wait_recv()

                @pl.when(me < dp - 1)
                def _():
                    to_right(me - d, c).start()

            @pl.when(me + d < dp)
            def _():
                to_right(me + d, c).wait_recv()

                @pl.when(me > 0)
                def _():
                    to_left(me + d, c).start()

    for k in range(1, lm):
        shard = lax.rem(lane + lm - k, lm)
        g_copy(k - 1, shard, lane).wait_recv()

    for copy in sends:
        copy.wait_send()
    for shard in range(dp):
        for c in range(chunks):

            @pl.when(jnp.logical_and(shard <= me, me < dp - 1))
            def _():
                to_right(shard, c).wait_send()

            @pl.when(jnp.logical_and(shard >= me, me > 0))
            def _():
                to_left(shard, c).wait_send()


def near_first(shard):
    return (
        shard,
        shard + 1 - 2 * lax.rem(shard, 2),
        2 - shard // 2,
        3 - 3 * (shard // 2),
    )


def place(shard, p):
    upper = shard // 2
    same = 1 - (upper - p // 2) * (upper - p // 2)
    far = (1 - upper) * p + upper * (3 - p)
    return same * (p - shard) * (p - shard) + (1 - same) * far


def aligned(start, size):
    return pl.ds(pl.multiple_of(start, size), size)


def standard_columns(feats, scale):
    pairs = feats.shape[0]
    mean = jnp.sum(feats, axis=0, keepdims=True) * (1.0 / pairs)
    dev = feats - mean
    var = jnp.sum(dev * dev, axis=0, keepdims=True) * (1.0 / pairs)
    return jnp.transpose(dev * (lax.rsqrt(var + EPS) * scale)).astype(jnp.bfloat16), mean


def blocks_kernel(
    late,
    images_hbm, captions_hbm, order_hbm, marks_hbm, gamma_hbm, words_hbm, text_gamma_hbm,
    f_all, g_all, image_mean_ref, text_mean_ref, relay, z_own,
    images_ref, captions_ref, order_ref, marks, gamma_ref, words, text_gamma_ref,
    u_all, c_all, keys, text_keys, raw,
    load_sem, mark_sem, u_sems, c_sems,
    right_send, left_send, f_recv, g_send, g_recv,
):
    dp, lm, cuts = 4, 4, CUTS
    me, lane = lax.axis_index("dp"), lax.axis_index("landmark")
    block = images_ref.shape[0]
    part = block // 2
    own = marks.shape[0]
    text_own = words.shape[0]
    pairs = block * dp
    piece = own // cuts

    loads = [
        pltpu.make_async_copy(src, dst, load_sem.at[at])
        for at, (src, dst) in enumerate((
            (images_hbm, images_ref), (captions_hbm, captions_ref), (order_hbm, order_ref),
            (gamma_hbm, gamma_ref), (words_hbm, words), (text_gamma_hbm, text_gamma_ref),
        ))
    ]
    mark_loads = [
        pltpu.make_async_copy(
            marks_hbm.at[pl.ds(at * piece, piece), :], marks.at[pl.ds(at * piece, piece), :],
            mark_sem.at[at],
        )
        for at in range(cuts)
    ]
    barrier = pltpu.get_barrier_semaphore()
    for k in range(1, dp):
        pl.semaphore_signal(
            barrier, inc=1, device_id={"dp": lax.rem(me + k, dp)}, device_id_type=MESH
        )
    for k in range(1, lm):
        pl.semaphore_signal(
            barrier, inc=1, device_id={"landmark": lax.rem(lane + k, lm)}, device_id_type=MESH
        )
    for load in loads[:4] + mark_loads + loads[4:]:
        load.start()

    half, core = lane // 2, lax.rem(lane, 2)
    mate = lane + 1 - 2 * core
    across = lax.rem(lane + 2, lm)
    order = near_first(me)
    mine = aligned(me * block, block)
    sends = []

    def launch(copy):
        copy.start()
        sends.append(copy)

    def portion(buf, sems, stage, k, shard, h, side, device):
        wide = buf.shape[1] // 2
        columns = pl.ds(0, 2 * wide) if h is None else aligned(h * wide, wide)
        ref = buf.at[aligned(shard * block + side * part, part), columns]
        return pltpu.make_async_remote_copy(
            src_ref=ref, dst_ref=ref, send_sem=sems.at[0, stage, k],
            recv_sem=sems.at[1, stage, shard], device_id=device, device_id_type=MESH,
        )

    def routes(ways):
        yield mate, half, 1 - core
        if ways == 4:
            yield across, 1 - half, core
            yield lm - 1 - lane, 1 - half, 1 - core

    def z_copy(buf, sems, ways, k, shard):
        h = half if ways[k] == 4 else None
        return portion(buf, sems, 0, k, shard, h, core, {"dp": order[k]})

    def spread(buf, sems, ways):
        for k in range(1, dp):
            launch(z_copy(buf, sems, ways, k, me))

    def pass_on(buf, sems, ways, blocks=range(1, 4)):
        for k in blocks:
            z_copy(buf, sems, ways, k, order[k]).wait_recv()
            h = half if ways[k] == 4 else None
            for stage, (target, _, _) in reversed(list(enumerate(routes(ways[k]), 1))):
                launch(portion(buf, sems, stage, k, order[k], h, core, {"landmark": target}))

    def gather(buf, sems, ways, blocks=range(1, 4)):
        for k in blocks:
            for stage, (target, h, side) in enumerate(routes(ways[k]), 1):
                h = h if ways[k] == 4 else None
                portion(buf, sems, stage, k, order[k], h, side, {"landmark": target}).wait_recv()

    loads[0].wait()
    u_all[mine, :] = unit_rows(images_ref[...].astype(jnp.float32)).astype(jnp.bfloat16)
    pl.semaphore_wait(barrier, dp - 1 + lm - 1)
    spread(u_all, u_sems, U_WAYS)
    loads[1].wait()
    loads[2].wait()
    picks = (
        lax.broadcasted_iota(jnp.int32, (block, block), 0) == order_ref[...]
    ).astype(jnp.bfloat16)
    paired = lax.dot_general(
        picks, captions_ref[...], (((0,), (0,)), ((), ())), preferred_element_type=jnp.float32
    )
    c_all[mine, :] = unit_rows(paired).astype(jnp.bfloat16)

    loads[3].wait()
    for at in range(cuts):
        mark_loads[at].wait()
        rows = pl.ds(at * piece, piece)
        scaled_keys(marks.at[rows, :], gamma_ref.at[:, rows], keys.at[rows, :])

    def hop(shard, j, send, target, rows):
        if j < FIRST:
            ref = raw.at[shard, pl.ds(j * block, block), pl.ds(0, rows)]
        else:
            ref = raw.at[
                shard, pl.ds(FIRST * block, pairs - FIRST * block),
                pl.ds((j - FIRST) * piece, piece),
            ]
        return pltpu.make_async_remote_copy(
            src_ref=ref, dst_ref=ref,
            send_sem=send.at[shard, j], recv_sem=f_recv.at[shard, j],
            device_id={"dp": target}, device_id_type=MESH,
        )

    def to_right(shard, j, rows=own):
        return hop(shard, j, right_send, jnp.minimum(me + 1, dp - 1), rows)

    def to_left(shard, j, rows=own):
        return hop(shard, j, left_send, jnp.maximum(me - 1, 0), rows)

    def send_own(j):
        @pl.when(me < dp - 1)
        def _():
            to_right(me, j).start()

        @pl.when(me > 0)
        def _():
            to_left(me, j).start()

    def features(units, rows):
        inner = lax.dot_general(
            units, keys[rows, :], (((1,), (1,)), ((), ())), preferred_element_type=jnp.float32
        )
        return jnp.exp(inner).astype(jnp.bfloat16)

    def first_block(j):
        units = u_all[aligned(order[j] * block, block), :]
        raw[me, j * block : (j + 1) * block, :] = features(units, pl.ds(0, own))
        send_own(j)

    first_block(0)
    spread(c_all, c_sems, C_WAYS)
    loads[4].wait()
    loads[5].wait()
    scaled_keys(words, text_gamma_ref, text_keys)
    hops = dp - 2 if late == cuts else dp - 1
    early_rows = own - late * piece

    def rows_of(d):
        return early_rows if d == dp - 1 else own

    def last_of(d):
        return FIRST - 1 + (cuts - late if d == dp - 1 else cuts)

    def receive(d, j):
        @pl.when(me + d < dp)
        def _():
            to_right(me + d, j, rows_of(d)).wait_recv()
            if d < hops and j <= last_of(d + 1):

                @pl.when(me > 0)
                def _():
                    to_left(me + d, j, rows_of(d + 1)).start()

        @pl.when(me - d >= 0)
        def _():
            to_left(me - d, j, rows_of(d)).wait_recv()
            if d < hops and j <= last_of(d + 1):

                @pl.when(me < dp - 1)
                def _():
                    to_right(me - d, j, rows_of(d + 1)).start()

    pass_on(u_all, u_sems, U_WAYS, range(1, FIRST))
    for j in range(1, FIRST):
        gather(u_all, u_sems, U_WAYS, (j,))
        first_block(j)
    pass_on(u_all, u_sems, U_WAYS, range(FIRST, dp))
    gather(u_all, u_sems, U_WAYS, range(FIRST, dp))
    others = jnp.concatenate(
        [u_all[aligned(order[k] * block, block), :] for k in range(FIRST, dp)], axis=0
    )
    for j in range(1, cuts + 1):
        rows = pl.ds((j - 1) * piece, piece)
        raw[me, FIRST * block :, (j - 1) * piece : j * piece] = features(others, rows)
        send_own(j + FIRST - 1)
        if j == CUTS:
            pass_on(c_all, c_sems, C_WAYS)

    def standardize(shard, j, mean_ref=None):
        for at in range((j - 1) * piece, j * piece, 128):
            columns = slice(at, at + 128)
            feats = jnp.concatenate(
                [
                    raw[shard, aligned(place(shard, p) * block, block), columns]
                    for p in range(dp)
                ],
                axis=0,
            )
            rows, mean = standard_columns(feats.astype(jnp.float32), 1.0)
            f_all[aligned(shard * own + at, 128), :] = rows
            if mean_ref is not None:
                mean_ref[:, columns] = mean

    for j in range(FIRST):
        receive(1, j)
    for j in range(1, cuts + 1):
        standardize(me, j, image_mean_ref)
    def g_copy(k, shard, target):
        rows = aligned(shard * text_own, text_own)
        return pltpu.make_async_remote_copy(
            src_ref=g_all.at[rows, :], dst_ref=g_all.at[rows, :],
            send_sem=g_send.at[k], recv_sem=g_recv.at[shard],
            device_id={"landmark": target}, device_id_type=MESH,
        )

    def text_features():
        gather(c_all, c_sems, C_WAYS)
        inner = lax.dot_general(
            c_all[...], text_keys[...], (((1,), (1,)), ((), ())), preferred_element_type=jnp.float32
        )
        rows, text_mean_ref[...] = standard_columns(
            jnp.exp(inner).astype(jnp.bfloat16).astype(jnp.float32), 1.0 / math.sqrt(pairs)
        )
        g_all[aligned(lane * text_own, text_own), :] = rows
        for k in range(1, lm):
            launch(g_copy(k - 1, lane, lax.rem(lane + k, lm)))

    def own_product():
        for k in range(1, lm):
            shard = lax.rem(lane + lm - k, lm)
            g_copy(k - 1, shard, lane).wait_recv()
        for at in range(0, z_own.shape[0], 256):
            z_own[at : at + 256, :] = lax.dot_general(
                f_all[aligned(me * own + at, 256), :], g_all[...],
                (((1,), (1,)), ((), ())), preferred_element_type=jnp.float32,
            )

    for d in range(1, hops + 1):
        for j in range(FIRST if d == 1 else 0, last_of(d) + 1):
            receive(d, j)
            if d == 1 and j == FIRST:
                text_features()
            if d == hops and j == 1:
                own_product()
            if j < FIRST:
                continue
            cut = j - FIRST + 1

            @pl.when(me - d >= 0)
            def _():
                standardize(me - d, cut)

            @pl.when(me + d < dp)
            def _():
                standardize(me + d, cut)

            if d == dp - 2 and cut > cuts - late:
                at = (cut - 1) * piece
                rows = pl.ds(at - early_rows, piece)

                @pl.when(me == dp - 2)
                def _():
                    relay[rows, :] = f_all[pl.ds(at, piece), :]

                @pl.when(me == 1)
                def _():
                    relay[rows, :] = f_all[pl.ds((dp - 1) * own + at, piece), :]

    for copy in sends:
        copy.wait_send()
    for d in range(hops):

        @pl.when(jnp.logical_and(me >= d, me < dp - 1))
        def _():
            for j in range(last_of(d + 1) + 1):
                to_right(me - d, j, rows_of(d + 1)).wait_send()

        @pl.when(jnp.logical_and(me < dp - d, me > 0))
        def _():
            for j in range(last_of(d + 1) + 1):
                to_left(me + d, j, rows_of(d + 1)).wait_send()


def product_kernel(
    tile, slots, dp, late_rows, f_ref, g_ref, image_mean_in, text_mean_in, *refs
):
    z_own = refs[0] if late_rows else None
    z_hbm, image_mean_ref, text_mean_ref, buf, sem, extra_sem = refs[-6:]
    means = [
        pltpu.make_async_copy(image_mean_in, image_mean_ref, extra_sem.at[0]),
        pltpu.make_async_copy(text_mean_in, text_mean_ref, extra_sem.at[1]),
    ]
    total = f_ref.shape[0]
    own = total // dp
    steps = (total - late_rows) // tile
    edge = own - late_rows
    if late_rows:
        me = lax.axis_index("dp")
        ready = z_own.shape[0]
        steps -= ready // tile
        mine = pl.ds(pl.multiple_of(me * own, ready), ready)
        means.insert(0, pltpu.make_async_copy(z_own, z_hbm.at[mine, :], extra_sem.at[2]))
    for copy in means:
        copy.start()

    def rows(at):
        start = at * tile
        if late_rows:
            skip = jnp.logical_and(me > 0, start >= edge)
            start = start + jnp.where(skip, late_rows, 0)
            start = start + jnp.where(start >= me * own, ready, 0)
        return pl.ds(pl.multiple_of(start, tile), tile)

    def out(at):
        slot = lax.rem(at, slots)
        return pltpu.make_async_copy(buf.at[slot], z_hbm.at[rows(at), :], sem.at[slot])

    def step(at, carry):
        @pl.when(at >= slots)
        def _():
            out(at - slots).wait()

        buf[lax.rem(at, slots)] = lax.dot_general(
            f_ref[rows(at), :], g_ref[...], (((1,), (1,)), ((), ())),
            preferred_element_type=jnp.float32,
        )
        out(at).start()
        return carry

    lax.fori_loop(0, steps, step, 0)
    for at in range(max(0, steps - slots), steps):
        out(jnp.int32(at)).wait()
    for copy in means:
        copy.wait()


def late_kernel(tile, dp, f_ref, got_ref, g_ref, z_in, z_hbm, buf, sem):
    me = lax.axis_index("dp")
    late_rows = got_ref.shape[0]
    own = f_ref.shape[0] // dp
    first = jnp.where(me == 0, dp * own, own) - late_rows
    inner = jnp.logical_and(me > 0, me < dp - 1)

    def rows(at):
        return pl.ds(pl.multiple_of(first + at * tile, tile), tile)

    def out(at):
        return pltpu.make_async_copy(buf.at[at], z_hbm.at[rows(at), :], sem.at[at])

    for at in range(late_rows // tile):
        buf[at] = lax.dot_general(
            jnp.where(inner, f_ref[rows(at), :], got_ref[pl.ds(at * tile, tile), :]),
            g_ref[...], (((1,), (1,)), ((), ())), preferred_element_type=jnp.float32,
        )
        out(at).start()
    for at in range(late_rows // tile):
        out(at).wait()


def per_device(
    images, captions, caption_of, image_landmarks, image_gamma, text_landmarks, text_gamma
):
    dp, lm = lax.axis_size("dp"), lax.axis_size("landmark")
    block, width = images.shape
    text_width = captions.shape[1]
    own, text_own = image_landmarks.shape[0], text_landmarks.shape[0]
    pairs = block * dp
    bf16, f32 = jnp.bfloat16, jnp.float32
    vmem = pl.BlockSpec(memory_space=pltpu.VMEM)
    hbm = pl.BlockSpec(memory_space=pltpu.HBM)
    dma = pltpu.SemaphoreType.DMA
    blocks = (
        dp == 4 and lm == 4 and block % 32 == 0 and own % 1024 == 0 and text_own % 128 == 0
        and width % 256 == 0 and text_width % 256 == 0
    )
    late_rows = own * LATE // CUTS if blocks else 0
    operands = [
        pltpu.with_memory_space_constraint(value, pltpu.HBM)
        for value in (
            images, captions, caption_of[None, :], image_landmarks, image_gamma[None, :],
            text_landmarks, text_gamma[None, :],
        )
    ]
    results = [
        jax.ShapeDtypeStruct((dp * own, pairs), bf16),
        jax.ShapeDtypeStruct((lm * text_own, pairs), bf16),
        jax.ShapeDtypeStruct((1, own), f32),
        jax.ShapeDtypeStruct((1, text_own), f32),
    ]
    held = [
        pltpu.VMEM((block, width), bf16),
        pltpu.VMEM((block, text_width), bf16),
        pltpu.VMEM((1, block), jnp.int32),
        pltpu.VMEM((own, width), bf16),
        pltpu.VMEM((1, own), f32),
        pltpu.VMEM((text_own, text_width), bf16),
        pltpu.VMEM((1, text_own), f32),
    ]
    params = pltpu.CompilerParams(
        collective_id=0, has_side_effects=True, vmem_limit_bytes=40 * 2**20
    )
    if blocks:
        f, g, image_mean, text_mean, relay, *z_own = pl.pallas_call(
            functools.partial(blocks_kernel, LATE),
            out_shape=results + [
                jax.ShapeDtypeStruct((late_rows, pairs), bf16),
                jax.ShapeDtypeStruct((own // 4, lm * text_own), f32),
            ],
            in_specs=[hbm] * 7,
            out_specs=[vmem] * 6,
            scratch_shapes=held + [
                pltpu.VMEM((pairs, width), bf16),
                pltpu.VMEM((pairs, text_width), bf16),
                pltpu.VMEM((own, width), bf16),
                pltpu.VMEM((text_own, text_width), bf16),
                pltpu.VMEM((dp, pairs, own), bf16),
                dma((6,)), dma((CUTS,)), dma((2, 4, dp)), dma((2, 4, dp)),
                dma((dp, FIRST + CUTS)), dma((dp, FIRST + CUTS)), dma((dp, FIRST + CUTS)),
                dma((lm,)), dma((lm,)),
            ],
            compiler_params=params,
            name="block_exchange",
        )(*operands)
    else:
        z_own = []
        split = 2 if lm % 2 == 0 else 1
        chunks = max(1, own // 256)
        f, g, image_mean, text_mean = pl.pallas_call(
            functools.partial(exchange_kernel, dp, lm, split, chunks),
            out_shape=results,
            in_specs=[hbm] * 7,
            out_specs=[vmem] * 4,
            scratch_shapes=held + [
                pltpu.VMEM((pairs, width), bf16),
                pltpu.VMEM((pairs, text_width), bf16),
                pltpu.VMEM((own, width), bf16),
                pltpu.VMEM((text_own, text_width), bf16),
                dma((7,)),
                dma((dp,)), dma((dp,)), dma((dp,)), dma((dp,)),
                dma((dp,)), dma((dp,)), dma((dp,)), dma((dp,)),
                dma((dp, chunks)), dma((dp, chunks)), dma((dp, chunks)),
                dma((lm,)), dma((lm,)),
            ],
            compiler_params=params,
            name="exchange",
        )(*operands)
    rows, columns = dp * own, lm * text_own
    ahead = rows - late_rows
    tile = math.gcd(math.gcd(own, own - late_rows), TILE)
    slots = min(SLOTS, ahead // tile)
    if late_rows:
        got = lax.ppermute(relay, "dp", ((dp - 2, dp - 1), (1, 0)))
    zstat, image_mean, text_mean = pl.pallas_call(
        functools.partial(product_kernel, tile, slots, dp, late_rows),
        out_shape=(
            jax.ShapeDtypeStruct((rows, columns), f32),
            jax.ShapeDtypeStruct((1, own), f32),
            jax.ShapeDtypeStruct((1, text_own), f32),
        ),
        in_specs=[vmem] * (4 + len(z_own)),
        out_specs=(hbm, hbm, hbm),
        scratch_shapes=[pltpu.VMEM((slots, tile, columns), f32), dma((slots,)), dma((3,))],
        compiler_params=pltpu.CompilerParams(vmem_limit_bytes=40 * 2**20),
        cost_estimate=pl.CostEstimate(
            flops=2 * ahead * columns * pairs, bytes_accessed=4 * ahead * columns, transcendentals=0
        ),
        name="product",
    )(f, g, image_mean, text_mean, *z_own)
    if late_rows:
        zstat = pl.pallas_call(
            functools.partial(late_kernel, LATE_TILE, dp),
            out_shape=jax.ShapeDtypeStruct((rows, columns), f32),
            in_specs=[vmem, vmem, vmem, hbm],
            out_specs=hbm,
            scratch_shapes=[
                pltpu.VMEM((late_rows // LATE_TILE, LATE_TILE, columns), f32), dma((late_rows // LATE_TILE,)),
            ],
            input_output_aliases={3: 0},
            compiler_params=pltpu.CompilerParams(vmem_limit_bytes=40 * 2**20),
            cost_estimate=pl.CostEstimate(
                flops=2 * late_rows * columns * pairs, bytes_accessed=4 * late_rows * columns,
                transcendentals=0,
            ),
            name="late_product",
        )(f, got, g, zstat)
    return (zstat, image_mean[0], text_mean[0])


def solution(mesh):
    in_specs = (
        P(("groups", "dp"), None),
        P(("groups", "dp"), None),
        P(("groups", "dp")),
        P(("landmark", "dp"), None),
        P(("landmark", "dp")),
        P(("dp", "landmark"), None),
        P(("dp", "landmark")),
    )
    out_specs = (
        P(("groups", "landmark"), "dp"),
        P(("groups", "landmark", "dp")),
        P(("groups", "dp", "landmark")),
    )
    return jax.shard_map(
        per_device, mesh=mesh, in_specs=in_specs, out_specs=out_specs, check_vma=False
    )
```

```python
import functools
import math

import jax
import jax.numpy as jnp
from jax import lax
from jax.experimental import pallas as pl
from jax.experimental.pallas import tpu as pltpu
from jax.sharding import PartitionSpec as P

MESH = pl.DeviceIdType.MESH
EPS = 1e-06
CUTS = 2
LATE = 1
FIRST = 2
U_WAYS = (0, 2, 2, 2)
C_WAYS = (0, 4, 4, 4)
TILE, LATE_TILE, SLOTS = 256, 128, 4


def unit_rows(wide):
    return wide * lax.rsqrt(jnp.sum(wide * wide, axis=-1, keepdims=True) + EPS)


def diagonal(size):
    return lax.broadcasted_iota(jnp.int32, (size, size), 0) == lax.broadcasted_iota(
        jnp.int32, (size, size), 1
    )


def scaled_keys(marks_ref, gamma_ref, keys_ref):
    total = marks_ref.shape[0]
    size = min(128, total)

    def step(at, carry):
        rows = pl.ds(pl.multiple_of(at * size, size), size)
        unit = unit_rows(marks_ref[rows, :].astype(jnp.float32))
        gamma = jnp.sum(
            jnp.where(diagonal(size), gamma_ref[:, rows], 0.0), axis=1, keepdims=True
        )
        keys_ref[rows, :] = (unit * gamma).astype(jnp.bfloat16)
        return carry

    lax.fori_loop(0, total // size, step, 0)


def standard_features(keys, units, mean_ref, start, scale):
    rows, pairs = keys.shape[0], units.shape[0]
    inner = lax.dot_general(
        keys, units, (((1,), (1,)), ((), ())), preferred_element_type=jnp.float32
    )
    feats = jnp.exp(inner).astype(jnp.bfloat16).astype(jnp.float32)
    mean = jnp.sum(feats, axis=1, keepdims=True) * (1.0 / pairs)
    dev = feats - mean
    var = jnp.sum(dev * dev, axis=1, keepdims=True) * (1.0 / pairs)
    size = min(128, rows)
    for at in range(0, rows, size):
        mean_ref[:, start + at : start + at + size] = jnp.sum(
            jnp.where(diagonal(size), mean[at : at + size], 0.0), axis=0, keepdims=True
        )
    return (dev * (lax.rsqrt(var + EPS) * scale)).astype(jnp.bfloat16)


def exchange_kernel(
    dp, lm, split, chunks,
    images_hbm, captions_hbm, order_hbm, marks_hbm, gamma_hbm, words_hbm, text_gamma_hbm,
    f_all, g_all, image_mean_ref, text_mean_ref,
    images_ref, captions_ref, order_ref, marks, gamma_ref, words, text_gamma_ref,
    u_all, c_all, keys, text_keys,
    load_sem,
    u_send, u_recv, u_mate_send, u_mate_recv,
    c_send, c_recv, c_mate_send, c_mate_recv,
    right_send, left_send, f_recv, g_send, g_recv,
):
    me, lane = lax.axis_index("dp"), lax.axis_index("landmark")
    block = images_ref.shape[0]
    part = block // split
    own = marks.shape[0]
    text_own = words.shape[0]
    pairs = u_all.shape[0]
    rows_each = own // chunks

    loads = [
        pltpu.make_async_copy(src, dst, load_sem.at[at])
        for at, (src, dst) in enumerate((
            (images_hbm, images_ref), (marks_hbm, marks), (gamma_hbm, gamma_ref),
            (captions_hbm, captions_ref), (order_hbm, order_ref),
            (words_hbm, words), (text_gamma_hbm, text_gamma_ref),
        ))
    ]
    for load in loads:
        load.start()

    barrier = pltpu.get_barrier_semaphore()
    for k in range(1, dp):
        pl.semaphore_signal(
            barrier, inc=1, device_id={"dp": lax.rem(me + k, dp)}, device_id_type=MESH
        )
    for k in range(1, lm):
        pl.semaphore_signal(
            barrier, inc=1, device_id={"landmark": lax.rem(lane + k, lm)}, device_id_type=MESH
        )

    mine = pl.ds(pl.multiple_of(me * block, block), block)
    loads[0].wait()
    u_all[mine, :] = unit_rows(images_ref[...].astype(jnp.float32)).astype(jnp.bfloat16)
    pl.semaphore_wait(barrier, dp - 1 + lm - 1)

    side = lax.rem(lane, split)
    mate = lane + 1 - 2 * side

    def half(shard):
        return pl.ds(pl.multiple_of(shard * block + side * part, part), part)

    def other_half(shard):
        return pl.ds(pl.multiple_of(shard * block + (1 - side) * part, part), part)

    def block_copy(buf, send, recv, k, shard, target):
        return pltpu.make_async_remote_copy(
            src_ref=buf.at[half(shard), :], dst_ref=buf.at[half(shard), :],
            send_sem=send.at[k], recv_sem=recv.at[shard],
            device_id={"dp": target}, device_id_type=MESH,
        )

    def mate_copy(buf, send, recv, k, shard, rows):
        return pltpu.make_async_remote_copy(
            src_ref=buf.at[rows, :], dst_ref=buf.at[rows, :],
            send_sem=send.at[k], recv_sem=recv.at[shard],
            device_id={"landmark": mate}, device_id_type=MESH,
        )

    sends = []

    def spread(buf, send, recv):
        for k in range(1, dp):
            copy = block_copy(buf, send, recv, k - 1, me, lax.rem(me + k, dp))
            copy.start()
            sends.append(copy)

    spread(u_all, u_send, u_recv)

    def collect(buf, send, recv, mate_send, mate_recv):
        for k in range(1, dp):
            shard = lax.rem(me + dp - k, dp)
            block_copy(buf, send, recv, k - 1, shard, me).wait_recv()
            if split > 1:
                copy = mate_copy(buf, mate_send, mate_recv, k - 1, shard, half(shard))
                copy.start()
                sends.append(copy)
        if split > 1:
            for k in range(1, dp):
                shard = lax.rem(me + dp - k, dp)
                mate_copy(
                    buf, mate_send, mate_recv, k - 1, shard, other_half(shard)
                ).wait_recv()

    loads[3].wait()
    loads[4].wait()
    picks = (
        lax.broadcasted_iota(jnp.int32, (block, block), 0) == order_ref[...]
    ).astype(jnp.bfloat16)
    paired = lax.dot_general(
        picks, captions_ref[...], (((0,), (0,)), ((), ())), preferred_element_type=jnp.float32
    )
    c_all[mine, :] = unit_rows(paired).astype(jnp.bfloat16)
    spread(c_all, c_send, c_recv)
    loads[1].wait()
    loads[2].wait()
    scaled_keys(marks, gamma_ref, keys)
    def f_rows(shard, c):
        return pl.ds(pl.multiple_of(shard * own + c * rows_each, rows_each), rows_each)

    def hop(shard, c, send, target):
        return pltpu.make_async_remote_copy(
            src_ref=f_all.at[f_rows(shard, c), :], dst_ref=f_all.at[f_rows(shard, c), :],
            send_sem=send.at[shard, c], recv_sem=f_recv.at[shard, c],
            device_id={"dp": target}, device_id_type=MESH,
        )

    def to_right(shard, c):
        return hop(shard, c, right_send, jnp.minimum(me + 1, dp - 1))

    def to_left(shard, c):
        return hop(shard, c, left_send, jnp.maximum(me - 1, 0))

    collect(u_all, u_send, u_recv, u_mate_send, u_mate_recv)
    for c in range(chunks):
        at = c * rows_each
        f_all[f_rows(me, c), :] = standard_features(
            keys[at : at + rows_each, :], u_all[...], image_mean_ref, at, 1.0
        )

        @pl.when(me < dp - 1)
        def _():
            to_right(me, c).start()

        @pl.when(me > 0)
        def _():
            to_left(me, c).start()

    loads[5].wait()
    loads[6].wait()
    scaled_keys(words, text_gamma_ref, text_keys)
    collect(c_all, c_send, c_recv, c_mate_send, c_mate_recv)
    text_mine = pl.ds(pl.multiple_of(lane * text_own, text_own), text_own)
    g_all[text_mine, :] = standard_features(
        text_keys[...], c_all[...], text_mean_ref, 0, 1.0 / math.sqrt(pairs)
    )

    def g_copy(k, shard, target):
        rows = pl.ds(pl.multiple_of(shard * text_own, text_own), text_own)
        return pltpu.make_async_remote_copy(
            src_ref=g_all.at[rows, :], dst_ref=g_all.at[rows, :],
            send_sem=g_send.at[k], recv_sem=g_recv.at[shard],
            device_id={"landmark": target}, device_id_type=MESH,
        )

    for k in range(1, lm):
        copy = g_copy(k - 1, lane, lax.rem(lane + k, lm))
        copy.start()
        sends.append(copy)

    for d in range(1, dp):
        for c in range(chunks):

            @pl.when(me - d >= 0)
            def _():
                to_left(me - d, c).wait_recv()

                @pl.when(me < dp - 1)
                def _():
                    to_right(me - d, c).start()

            @pl.when(me + d < dp)
            def _():
                to_right(me + d, c).wait_recv()

                @pl.when(me > 0)
                def _():
                    to_left(me + d, c).start()

    for k in range(1, lm):
        shard = lax.rem(lane + lm - k, lm)
        g_copy(k - 1, shard, lane).wait_recv()

    for copy in sends:
        copy.wait_send()
    for shard in range(dp):
        for c in range(chunks):

            @pl.when(jnp.logical_and(shard <= me, me < dp - 1))
            def _():
                to_right(shard, c).wait_send()

            @pl.when(jnp.logical_and(shard >= me, me > 0))
            def _():
                to_left(shard, c).wait_send()


def near_first(shard):
    return (
        shard,
        shard + 1 - 2 * lax.rem(shard, 2),
        2 - shard // 2,
        3 - 3 * (shard // 2),
    )


def place(shard, p):
    upper = shard // 2
    same = 1 - (upper - p // 2) * (upper - p // 2)
    far = (1 - upper) * p + upper * (3 - p)
    return same * (p - shard) * (p - shard) + (1 - same) * far


def aligned(start, size):
    return pl.ds(pl.multiple_of(start, size), size)


def standard_columns(feats, scale):
    pairs = feats.shape[0]
    mean = jnp.sum(feats, axis=0, keepdims=True) * (1.0 / pairs)
    dev = feats - mean
    var = jnp.sum(dev * dev, axis=0, keepdims=True) * (1.0 / pairs)
    return jnp.transpose(dev * (lax.rsqrt(var + EPS) * scale)).astype(jnp.bfloat16), mean


def blocks_kernel(
    late,
    images_hbm, captions_hbm, order_hbm, marks_hbm, gamma_hbm, words_hbm, text_gamma_hbm,
    f_all, g_all, image_mean_ref, text_mean_ref, relay, z_own,
    images_ref, captions_ref, order_ref, marks, gamma_ref, words, text_gamma_ref,
    u_all, c_all, keys, text_keys, raw,
    load_sem, mark_sem, u_sems, c_sems,
    right_send, left_send, f_recv, g_send, g_recv,
):
    dp, lm, cuts = 4, 4, CUTS
    me, lane = lax.axis_index("dp"), lax.axis_index("landmark")
    block = images_ref.shape[0]
    part = block // 2
    own = marks.shape[0]
    text_own = words.shape[0]
    pairs = block * dp
    piece = own // cuts

    loads = [
        pltpu.make_async_copy(src, dst, load_sem.at[at])
        for at, (src, dst) in enumerate((
            (images_hbm, images_ref), (captions_hbm, captions_ref), (order_hbm, order_ref),
            (gamma_hbm, gamma_ref), (words_hbm, words), (text_gamma_hbm, text_gamma_ref),
        ))
    ]
    mark_loads = [
        pltpu.make_async_copy(
            marks_hbm.at[pl.ds(at * piece, piece), :], marks.at[pl.ds(at * piece, piece), :],
            mark_sem.at[at],
        )
        for at in range(cuts)
    ]
    loads[0].start()
    barrier = pltpu.get_barrier_semaphore()
    for k in range(1, dp):
        pl.semaphore_signal(
            barrier, inc=1, device_id={"dp": lax.rem(me + k, dp)}, device_id_type=MESH
        )
    for k in range(1, lm):
        pl.semaphore_signal(
            barrier, inc=1, device_id={"landmark": lax.rem(lane + k, lm)}, device_id_type=MESH
        )
    for load in loads[1:4] + mark_loads + loads[4:]:
        load.start()

    half, core = lane // 2, lax.rem(lane, 2)
    mate = lane + 1 - 2 * core
    across = lax.rem(lane + 2, lm)
    order = near_first(me)
    mine = aligned(me * block, block)
    sends = []

    def launch(copy):
        copy.start()
        sends.append(copy)

    def portion(buf, sems, stage, k, shard, h, side, device):
        wide = buf.shape[1] // 2
        columns = pl.ds(0, 2 * wide) if h is None else aligned(h * wide, wide)
        ref = buf.at[aligned(shard * block + side * part, part), columns]
        return pltpu.make_async_remote_copy(
            src_ref=ref, dst_ref=ref, send_sem=sems.at[0, stage, k],
            recv_sem=sems.at[1, stage, shard], device_id=device, device_id_type=MESH,
        )

    def routes(ways):
        yield mate, half, 1 - core
        if ways == 4:
            yield across, 1 - half, core
            yield lm - 1 - lane, 1 - half, 1 - core

    def z_copy(buf, sems, ways, k, shard):
        h = half if ways[k] == 4 else None
        return portion(buf, sems, 0, k, shard, h, core, {"dp": order[k]})

    def spread(buf, sems, ways):
        for k in range(1, dp):
            launch(z_copy(buf, sems, ways, k, me))

    def pass_on(buf, sems, ways, blocks=range(1, 4)):
        for k in blocks:
            z_copy(buf, sems, ways, k, order[k]).wait_recv()
            h = half if ways[k] == 4 else None
            for stage, (target, _, _) in reversed(list(enumerate(routes(ways[k]), 1))):
                launch(portion(buf, sems, stage, k, order[k], h, core, {"landmark": target}))

    def gather(buf, sems, ways, blocks=range(1, 4)):
        for k in blocks:
            for stage, (target, h, side) in enumerate(routes(ways[k]), 1):
                h = h if ways[k] == 4 else None
                portion(buf, sems, stage, k, order[k], h, side, {"landmark": target}).wait_recv()

    loads[0].wait()
    u_all[mine, :] = unit_rows(images_ref[...].astype(jnp.float32)).astype(jnp.bfloat16)
    pl.semaphore_wait(barrier, dp - 1 + lm - 1)
    spread(u_all, u_sems, U_WAYS)
    loads[1].wait()
    loads[2].wait()
    picks = (
        lax.broadcasted_iota(jnp.int32, (block, block), 0) == order_ref[...]
    ).astype(jnp.bfloat16)
    paired = lax.dot_general(
        picks, captions_ref[...], (((0,), (0,)), ((), ())), preferred_element_type=jnp.float32
    )
    c_all[mine, :] = unit_rows(paired).astype(jnp.bfloat16)

    loads[3].wait()
    for at in range(cuts):
        mark_loads[at].wait()
        rows = pl.ds(at * piece, piece)
        scaled_keys(marks.at[rows, :], gamma_ref.at[:, rows], keys.at[rows, :])

    def hop(shard, j, send, target, rows):
        if j < FIRST:
            ref = raw.at[shard, pl.ds(j * block, block), pl.ds(0, rows)]
        else:
            ref = raw.at[
                shard, pl.ds(FIRST * block, pairs - FIRST * block),
                pl.ds((j - FIRST) * piece, piece),
            ]
        return pltpu.make_async_remote_copy(
            src_ref=ref, dst_ref=ref,
            send_sem=send.at[shard, j], recv_sem=f_recv.at[shard, j],
            device_id={"dp": target}, device_id_type=MESH,
        )

    def to_right(shard, j, rows=own):
        return hop(shard, j, right_send, jnp.minimum(me + 1, dp - 1), rows)

    def to_left(shard, j, rows=own):
        return hop(shard, j, left_send, jnp.maximum(me - 1, 0), rows)

    def send_own(j):
        @pl.when(me < dp - 1)
        def _():
            to_right(me, j).start()

        @pl.when(me > 0)
        def _():
            to_left(me, j).start()

    def features(units, rows):
        inner = lax.dot_general(
            units, keys[rows, :], (((1,), (1,)), ((), ())), preferred_element_type=jnp.float32
        )
        return jnp.exp(inner).astype(jnp.bfloat16)

    def first_block(j):
        units = u_all[aligned(order[j] * block, block), :]
        raw[me, j * block : (j + 1) * block, :] = features(units, pl.ds(0, own))
        send_own(j)

    first_block(0)
    spread(c_all, c_sems, C_WAYS)
    loads[4].wait()
    loads[5].wait()
    scaled_keys(words, text_gamma_ref, text_keys)
    hops = dp - 2 if late == cuts else dp - 1
    early_rows = own - late * piece

    def rows_of(d):
        return early_rows if d == dp - 1 else own

    def last_of(d):
        return FIRST - 1 + (cuts - late if d == dp - 1 else cuts)

    def receive(d, j):
        @pl.when(me + d < dp)
        def _():
            to_right(me + d, j, rows_of(d)).wait_recv()
            if d < hops and j <= last_of(d + 1):

                @pl.when(me > 0)
                def _():
                    to_left(me + d, j, rows_of(d + 1)).start()

        @pl.when(me - d >= 0)
        def _():
            to_left(me - d, j, rows_of(d)).wait_recv()
            if d < hops and j <= last_of(d + 1):

                @pl.when(me < dp - 1)
                def _():
                    to_right(me - d, j, rows_of(d + 1)).start()

    pass_on(u_all, u_sems, U_WAYS, range(1, FIRST))
    for j in range(1, FIRST):
        gather(u_all, u_sems, U_WAYS, (j,))
        first_block(j)
    pass_on(u_all, u_sems, U_WAYS, range(FIRST, dp))
    gather(u_all, u_sems, U_WAYS, range(FIRST, dp))
    others = jnp.concatenate(
        [u_all[aligned(order[k] * block, block), :] for k in range(FIRST, dp)], axis=0
    )
    for j in range(1, cuts + 1):
        rows = pl.ds((j - 1) * piece, piece)
        raw[me, FIRST * block :, (j - 1) * piece : j * piece] = features(others, rows)
        send_own(j + FIRST - 1)
        if j == CUTS:
            pass_on(c_all, c_sems, C_WAYS)

    def standardize(shard, j, mean_ref=None):
        for at in range((j - 1) * piece, j * piece, 128):
            columns = slice(at, at + 128)
            feats = jnp.concatenate(
                [
                    raw[shard, aligned(place(shard, p) * block, block), columns]
                    for p in range(dp)
                ],
                axis=0,
            )
            rows, mean = standard_columns(feats.astype(jnp.float32), 1.0)
            f_all[aligned(shard * own + at, 128), :] = rows
            if mean_ref is not None:
                mean_ref[:, columns] = mean

    for j in range(FIRST):
        receive(1, j)
    for j in range(1, cuts + 1):
        standardize(me, j, image_mean_ref)
    def g_copy(k, shard, target):
        rows = aligned(shard * text_own, text_own)
        return pltpu.make_async_remote_copy(
            src_ref=g_all.at[rows, :], dst_ref=g_all.at[rows, :],
            send_sem=g_send.at[k], recv_sem=g_recv.at[shard],
            device_id={"landmark": target}, device_id_type=MESH,
        )

    def text_features():
        gather(c_all, c_sems, C_WAYS)
        inner = lax.dot_general(
            c_all[...], text_keys[...], (((1,), (1,)), ((), ())), preferred_element_type=jnp.float32
        )
        rows, text_mean_ref[...] = standard_columns(
            jnp.exp(inner).astype(jnp.bfloat16).astype(jnp.float32), 1.0 / math.sqrt(pairs)
        )
        g_all[aligned(lane * text_own, text_own), :] = rows
        for k in range(1, lm):
            launch(g_copy(k - 1, lane, lax.rem(lane + k, lm)))

    def own_product():
        for k in range(1, lm):
            shard = lax.rem(lane + lm - k, lm)
            g_copy(k - 1, shard, lane).wait_recv()
        for at in range(0, z_own.shape[0], 256):
            z_own[at : at + 256, :] = lax.dot_general(
                f_all[aligned(me * own + at, 256), :], g_all[...],
                (((1,), (1,)), ((), ())), preferred_element_type=jnp.float32,
            )

    for d in range(1, hops + 1):
        for j in range(FIRST if d == 1 else 0, last_of(d) + 1):
            receive(d, j)
            if d == 1 and j == FIRST:
                text_features()
            if d == hops and j == 1:
                own_product()
            if j < FIRST:
                continue
            cut = j - FIRST + 1

            @pl.when(me - d >= 0)
            def _():
                standardize(me - d, cut)

            @pl.when(me + d < dp)
            def _():
                standardize(me + d, cut)

            if d == dp - 2 and cut > cuts - late:
                at = (cut - 1) * piece
                rows = pl.ds(at - early_rows, piece)

                @pl.when(me == dp - 2)
                def _():
                    relay[rows, :] = f_all[pl.ds(at, piece), :]

                @pl.when(me == 1)
                def _():
                    relay[rows, :] = f_all[pl.ds((dp - 1) * own + at, piece), :]

    for copy in sends:
        copy.wait_send()
    for d in range(hops):

        @pl.when(jnp.logical_and(me >= d, me < dp - 1))
        def _():
            for j in range(last_of(d + 1) + 1):
                to_right(me - d, j, rows_of(d + 1)).wait_send()

        @pl.when(jnp.logical_and(me < dp - d, me > 0))
        def _():
            for j in range(last_of(d + 1) + 1):
                to_left(me + d, j, rows_of(d + 1)).wait_send()


def product_kernel(
    tile, slots, dp, late_rows, f_ref, g_ref, image_mean_in, text_mean_in, *refs
):
    z_own = refs[0] if late_rows else None
    z_hbm, image_mean_ref, text_mean_ref, buf, sem, extra_sem = refs[-6:]
    means = [
        pltpu.make_async_copy(image_mean_in, image_mean_ref, extra_sem.at[0]),
        pltpu.make_async_copy(text_mean_in, text_mean_ref, extra_sem.at[1]),
    ]
    total = f_ref.shape[0]
    own = total // dp
    steps = (total - late_rows) // tile
    edge = own - late_rows
    if late_rows:
        me = lax.axis_index("dp")
        ready = z_own.shape[0]
        steps -= ready // tile
        mine = pl.ds(pl.multiple_of(me * own, ready), ready)
        means.insert(0, pltpu.make_async_copy(z_own, z_hbm.at[mine, :], extra_sem.at[2]))
    for copy in means:
        copy.start()

    def rows(at):
        start = at * tile
        if late_rows:
            skip = jnp.logical_and(me > 0, start >= edge)
            start = start + jnp.where(skip, late_rows, 0)
            start = start + jnp.where(start >= me * own, ready, 0)
        return pl.ds(pl.multiple_of(start, tile), tile)

    def out(at):
        slot = lax.rem(at, slots)
        return pltpu.make_async_copy(buf.at[slot], z_hbm.at[rows(at), :], sem.at[slot])

    def step(at, carry):
        @pl.when(at >= slots)
        def _():
            out(at - slots).wait()

        buf[lax.rem(at, slots)] = lax.dot_general(
            f_ref[rows(at), :], g_ref[...], (((1,), (1,)), ((), ())),
            preferred_element_type=jnp.float32,
        )
        out(at).start()
        return carry

    lax.fori_loop(0, steps, step, 0)
    for at in range(max(0, steps - slots), steps):
        out(jnp.int32(at)).wait()
    for copy in means:
        copy.wait()


def late_kernel(tile, dp, f_ref, got_ref, g_ref, z_in, z_hbm, buf, sem):
    me = lax.axis_index("dp")
    late_rows = got_ref.shape[0]
    own = f_ref.shape[0] // dp
    first = jnp.where(me == 0, dp * own, own) - late_rows
    inner = jnp.logical_and(me > 0, me < dp - 1)

    def rows(at):
        return pl.ds(pl.multiple_of(first + at * tile, tile), tile)

    def out(at):
        return pltpu.make_async_copy(buf.at[at], z_hbm.at[rows(at), :], sem.at[at])

    for at in range(late_rows // tile):
        buf[at] = lax.dot_general(
            jnp.where(inner, f_ref[rows(at), :], got_ref[pl.ds(at * tile, tile), :]),
            g_ref[...], (((1,), (1,)), ((), ())), preferred_element_type=jnp.float32,
        )
        out(at).start()
    for at in range(late_rows // tile):
        out(at).wait()


def per_device(
    images, captions, caption_of, image_landmarks, image_gamma, text_landmarks, text_gamma
):
    dp, lm = lax.axis_size("dp"), lax.axis_size("landmark")
    block, width = images.shape
    text_width = captions.shape[1]
    own, text_own = image_landmarks.shape[0], text_landmarks.shape[0]
    pairs = block * dp
    bf16, f32 = jnp.bfloat16, jnp.float32
    vmem = pl.BlockSpec(memory_space=pltpu.VMEM)
    hbm = pl.BlockSpec(memory_space=pltpu.HBM)
    dma = pltpu.SemaphoreType.DMA
    blocks = (
        dp == 4 and lm == 4 and block % 32 == 0 and own % 1024 == 0 and text_own % 128 == 0
        and width % 256 == 0 and text_width % 256 == 0
    )
    late_rows = own * LATE // CUTS if blocks else 0
    operands = [
        pltpu.with_memory_space_constraint(value, pltpu.HBM)
        for value in (
            images, captions, caption_of[None, :], image_landmarks, image_gamma[None, :],
            text_landmarks, text_gamma[None, :],
        )
    ]
    results = [
        jax.ShapeDtypeStruct((dp * own, pairs), bf16),
        jax.ShapeDtypeStruct((lm * text_own, pairs), bf16),
        jax.ShapeDtypeStruct((1, own), f32),
        jax.ShapeDtypeStruct((1, text_own), f32),
    ]
    held = [
        pltpu.VMEM((block, width), bf16),
        pltpu.VMEM((block, text_width), bf16),
        pltpu.VMEM((1, block), jnp.int32),
        pltpu.VMEM((own, width), bf16),
        pltpu.VMEM((1, own), f32),
        pltpu.VMEM((text_own, text_width), bf16),
        pltpu.VMEM((1, text_own), f32),
    ]
    params = pltpu.CompilerParams(
        collective_id=0, has_side_effects=True, vmem_limit_bytes=40 * 2**20
    )
    if blocks:
        f, g, image_mean, text_mean, relay, *z_own = pl.pallas_call(
            functools.partial(blocks_kernel, LATE),
            out_shape=results + [
                jax.ShapeDtypeStruct((late_rows, pairs), bf16),
                jax.ShapeDtypeStruct((own // 4, lm * text_own), f32),
            ],
            in_specs=[hbm] * 7,
            out_specs=[vmem] * 6,
            scratch_shapes=held + [
                pltpu.VMEM((pairs, width), bf16),
                pltpu.VMEM((pairs, text_width), bf16),
                pltpu.VMEM((own, width), bf16),
                pltpu.VMEM((text_own, text_width), bf16),
                pltpu.VMEM((dp, pairs, own), bf16),
                dma((6,)), dma((CUTS,)), dma((2, 4, dp)), dma((2, 4, dp)),
                dma((dp, FIRST + CUTS)), dma((dp, FIRST + CUTS)), dma((dp, FIRST + CUTS)),
                dma((lm,)), dma((lm,)),
            ],
            compiler_params=params,
            name="block_exchange",
        )(*operands)
    else:
        z_own = []
        split = 2 if lm % 2 == 0 else 1
        chunks = max(1, own // 256)
        f, g, image_mean, text_mean = pl.pallas_call(
            functools.partial(exchange_kernel, dp, lm, split, chunks),
            out_shape=results,
            in_specs=[hbm] * 7,
            out_specs=[vmem] * 4,
            scratch_shapes=held + [
                pltpu.VMEM((pairs, width), bf16),
                pltpu.VMEM((pairs, text_width), bf16),
                pltpu.VMEM((own, width), bf16),
                pltpu.VMEM((text_own, text_width), bf16),
                dma((7,)),
                dma((dp,)), dma((dp,)), dma((dp,)), dma((dp,)),
                dma((dp,)), dma((dp,)), dma((dp,)), dma((dp,)),
                dma((dp, chunks)), dma((dp, chunks)), dma((dp, chunks)),
                dma((lm,)), dma((lm,)),
            ],
            compiler_params=params,
            name="exchange",
        )(*operands)
    rows, columns = dp * own, lm * text_own
    ahead = rows - late_rows
    tile = math.gcd(math.gcd(own, own - late_rows), TILE)
    slots = min(SLOTS, ahead // tile)
    if late_rows:
        got = lax.ppermute(relay, "dp", ((dp - 2, dp - 1), (1, 0)))
    zstat, image_mean, text_mean = pl.pallas_call(
        functools.partial(product_kernel, tile, slots, dp, late_rows),
        out_shape=(
            jax.ShapeDtypeStruct((rows, columns), f32),
            jax.ShapeDtypeStruct((1, own), f32),
            jax.ShapeDtypeStruct((1, text_own), f32),
        ),
        in_specs=[vmem] * (4 + len(z_own)),
        out_specs=(hbm, hbm, hbm),
        scratch_shapes=[pltpu.VMEM((slots, tile, columns), f32), dma((slots,)), dma((3,))],
        compiler_params=pltpu.CompilerParams(vmem_limit_bytes=40 * 2**20),
        cost_estimate=pl.CostEstimate(
            flops=2 * ahead * columns * pairs, bytes_accessed=4 * ahead * columns, transcendentals=0
        ),
        name="product",
    )(f, g, image_mean, text_mean, *z_own)
    if late_rows:
        zstat = pl.pallas_call(
            functools.partial(late_kernel, LATE_TILE, dp),
            out_shape=jax.ShapeDtypeStruct((rows, columns), f32),
            in_specs=[vmem, vmem, vmem, hbm],
            out_specs=hbm,
            scratch_shapes=[
                pltpu.VMEM((late_rows // LATE_TILE, LATE_TILE, columns), f32), dma((late_rows // LATE_TILE,)),
            ],
            input_output_aliases={3: 0},
            compiler_params=pltpu.CompilerParams(vmem_limit_bytes=40 * 2**20),
            cost_estimate=pl.CostEstimate(
                flops=2 * late_rows * columns * pairs, bytes_accessed=4 * late_rows * columns,
                transcendentals=0,
            ),
            name="late_product",
        )(f, got, g, zstat)
    return (zstat, image_mean[0], text_mean[0])


def solution(mesh):
    in_specs = (
        P(("groups", "dp"), None),
        P(("groups", "dp"), None),
        P(("groups", "dp")),
        P(("landmark", "dp"), None),
        P(("landmark", "dp")),
        P(("dp", "landmark"), None),
        P(("dp", "landmark")),
    )
    out_specs = (
        P(("groups", "landmark"), "dp"),
        P(("groups", "landmark", "dp")),
        P(("groups", "dp", "landmark")),
    )
    return jax.shard_map(
        per_device, mesh=mesh, in_specs=in_specs, out_specs=out_specs, check_vma=False
    )
```

```python
import functools
import math

import jax
import jax.numpy as jnp
from jax import lax
from jax.experimental import pallas as pl
from jax.experimental.pallas import tpu as pltpu
from jax.sharding import PartitionSpec as P

MESH = pl.DeviceIdType.MESH
EPS = 1e-06
CUTS = 2
LATE = 1
FIRST = 2
U_WAYS = (0, 2, 2, 2)
C_WAYS = (0, 2, 4, 4)
TILE, LATE_TILE, SLOTS = 256, 128, 6


def unit_rows(wide):
    return wide * lax.rsqrt(jnp.sum(wide * wide, axis=-1, keepdims=True) + EPS)


def diagonal(size):
    return lax.broadcasted_iota(jnp.int32, (size, size), 0) == lax.broadcasted_iota(
        jnp.int32, (size, size), 1
    )


def scaled_keys(marks_ref, gamma_ref, keys_ref):
    total = marks_ref.shape[0]
    size = min(128, total)

    def step(at, carry):
        rows = pl.ds(pl.multiple_of(at * size, size), size)
        unit = unit_rows(marks_ref[rows, :].astype(jnp.float32))
        gamma = jnp.sum(
            jnp.where(diagonal(size), gamma_ref[:, rows], 0.0), axis=1, keepdims=True
        )
        keys_ref[rows, :] = (unit * gamma).astype(jnp.bfloat16)
        return carry

    lax.fori_loop(0, total // size, step, 0)


def standard_features(keys, units, mean_ref, start, scale):
    rows, pairs = keys.shape[0], units.shape[0]
    inner = lax.dot_general(
        keys, units, (((1,), (1,)), ((), ())), preferred_element_type=jnp.float32
    )
    feats = jnp.exp(inner).astype(jnp.bfloat16).astype(jnp.float32)
    mean = jnp.sum(feats, axis=1, keepdims=True) * (1.0 / pairs)
    dev = feats - mean
    var = jnp.sum(dev * dev, axis=1, keepdims=True) * (1.0 / pairs)
    size = min(128, rows)
    for at in range(0, rows, size):
        mean_ref[:, start + at : start + at + size] = jnp.sum(
            jnp.where(diagonal(size), mean[at : at + size], 0.0), axis=0, keepdims=True
        )
    return (dev * (lax.rsqrt(var + EPS) * scale)).astype(jnp.bfloat16)


def exchange_kernel(
    dp, lm, split, chunks,
    images_hbm, captions_hbm, order_hbm, marks_hbm, gamma_hbm, words_hbm, text_gamma_hbm,
    f_all, g_all, image_mean_ref, text_mean_ref,
    images_ref, captions_ref, order_ref, marks, gamma_ref, words, text_gamma_ref,
    u_all, c_all, keys, text_keys,
    load_sem,
    u_send, u_recv, u_mate_send, u_mate_recv,
    c_send, c_recv, c_mate_send, c_mate_recv,
    right_send, left_send, f_recv, g_send, g_recv,
):
    me, lane = lax.axis_index("dp"), lax.axis_index("landmark")
    block = images_ref.shape[0]
    part = block // split
    own = marks.shape[0]
    text_own = words.shape[0]
    pairs = u_all.shape[0]
    rows_each = own // chunks

    loads = [
        pltpu.make_async_copy(src, dst, load_sem.at[at])
        for at, (src, dst) in enumerate((
            (images_hbm, images_ref), (marks_hbm, marks), (gamma_hbm, gamma_ref),
            (captions_hbm, captions_ref), (order_hbm, order_ref),
            (words_hbm, words), (text_gamma_hbm, text_gamma_ref),
        ))
    ]
    for load in loads:
        load.start()

    barrier = pltpu.get_barrier_semaphore()
    for k in range(1, dp):
        pl.semaphore_signal(
            barrier, inc=1, device_id={"dp": lax.rem(me + k, dp)}, device_id_type=MESH
        )
    for k in range(1, lm):
        pl.semaphore_signal(
            barrier, inc=1, device_id={"landmark": lax.rem(lane + k, lm)}, device_id_type=MESH
        )

    mine = pl.ds(pl.multiple_of(me * block, block), block)
    loads[0].wait()
    u_all[mine, :] = unit_rows(images_ref[...].astype(jnp.float32)).astype(jnp.bfloat16)
    pl.semaphore_wait(barrier, dp - 1 + lm - 1)

    side = lax.rem(lane, split)
    mate = lane + 1 - 2 * side

    def half(shard):
        return pl.ds(pl.multiple_of(shard * block + side * part, part), part)

    def other_half(shard):
        return pl.ds(pl.multiple_of(shard * block + (1 - side) * part, part), part)

    def block_copy(buf, send, recv, k, shard, target):
        return pltpu.make_async_remote_copy(
            src_ref=buf.at[half(shard), :], dst_ref=buf.at[half(shard), :],
            send_sem=send.at[k], recv_sem=recv.at[shard],
            device_id={"dp": target}, device_id_type=MESH,
        )

    def mate_copy(buf, send, recv, k, shard, rows):
        return pltpu.make_async_remote_copy(
            src_ref=buf.at[rows, :], dst_ref=buf.at[rows, :],
            send_sem=send.at[k], recv_sem=recv.at[shard],
            device_id={"landmark": mate}, device_id_type=MESH,
        )

    sends = []

    def spread(buf, send, recv):
        for k in range(1, dp):
            copy = block_copy(buf, send, recv, k - 1, me, lax.rem(me + k, dp))
            copy.start()
            sends.append(copy)

    spread(u_all, u_send, u_recv)

    def collect(buf, send, recv, mate_send, mate_recv):
        for k in range(1, dp):
            shard = lax.rem(me + dp - k, dp)
            block_copy(buf, send, recv, k - 1, shard, me).wait_recv()
            if split > 1:
                copy = mate_copy(buf, mate_send, mate_recv, k - 1, shard, half(shard))
                copy.start()
                sends.append(copy)
        if split > 1:
            for k in range(1, dp):
                shard = lax.rem(me + dp - k, dp)
                mate_copy(
                    buf, mate_send, mate_recv, k - 1, shard, other_half(shard)
                ).wait_recv()

    loads[3].wait()
    loads[4].wait()
    picks = (
        lax.broadcasted_iota(jnp.int32, (block, block), 0) == order_ref[...]
    ).astype(jnp.bfloat16)
    paired = lax.dot_general(
        picks, captions_ref[...], (((0,), (0,)), ((), ())), preferred_element_type=jnp.float32
    )
    c_all[mine, :] = unit_rows(paired).astype(jnp.bfloat16)
    spread(c_all, c_send, c_recv)
    loads[1].wait()
    loads[2].wait()
    scaled_keys(marks, gamma_ref, keys)
    def f_rows(shard, c):
        return pl.ds(pl.multiple_of(shard * own + c * rows_each, rows_each), rows_each)

    def hop(shard, c, send, target):
        return pltpu.make_async_remote_copy(
            src_ref=f_all.at[f_rows(shard, c), :], dst_ref=f_all.at[f_rows(shard, c), :],
            send_sem=send.at[shard, c], recv_sem=f_recv.at[shard, c],
            device_id={"dp": target}, device_id_type=MESH,
        )

    def to_right(shard, c):
        return hop(shard, c, right_send, jnp.minimum(me + 1, dp - 1))

    def to_left(shard, c):
        return hop(shard, c, left_send, jnp.maximum(me - 1, 0))

    collect(u_all, u_send, u_recv, u_mate_send, u_mate_recv)
    for c in range(chunks):
        at = c * rows_each
        f_all[f_rows(me, c), :] = standard_features(
            keys[at : at + rows_each, :], u_all[...], image_mean_ref, at, 1.0
        )

        @pl.when(me < dp - 1)
        def _():
            to_right(me, c).start()

        @pl.when(me > 0)
        def _():
            to_left(me, c).start()

    loads[5].wait()
    loads[6].wait()
    scaled_keys(words, text_gamma_ref, text_keys)
    collect(c_all, c_send, c_recv, c_mate_send, c_mate_recv)
    text_mine = pl.ds(pl.multiple_of(lane * text_own, text_own), text_own)
    g_all[text_mine, :] = standard_features(
        text_keys[...], c_all[...], text_mean_ref, 0, 1.0 / math.sqrt(pairs)
    )

    def g_copy(k, shard, target):
        rows = pl.ds(pl.multiple_of(shard * text_own, text_own), text_own)
        return pltpu.make_async_remote_copy(
            src_ref=g_all.at[rows, :], dst_ref=g_all.at[rows, :],
            send_sem=g_send.at[k], recv_sem=g_recv.at[shard],
            device_id={"landmark": target}, device_id_type=MESH,
        )

    for k in range(1, lm):
        copy = g_copy(k - 1, lane, lax.rem(lane + k, lm))
        copy.start()
        sends.append(copy)

    for d in range(1, dp):
        for c in range(chunks):

            @pl.when(me - d >= 0)
            def _():
                to_left(me - d, c).wait_recv()

                @pl.when(me < dp - 1)
                def _():
                    to_right(me - d, c).start()

            @pl.when(me + d < dp)
            def _():
                to_right(me + d, c).wait_recv()

                @pl.when(me > 0)
                def _():
                    to_left(me + d, c).start()

    for k in range(1, lm):
        shard = lax.rem(lane + lm - k, lm)
        g_copy(k - 1, shard, lane).wait_recv()

    for copy in sends:
        copy.wait_send()
    for shard in range(dp):
        for c in range(chunks):

            @pl.when(jnp.logical_and(shard <= me, me < dp - 1))
            def _():
                to_right(shard, c).wait_send()

            @pl.when(jnp.logical_and(shard >= me, me > 0))
            def _():
                to_left(shard, c).wait_send()


def near_first(shard):
    return (
        shard,
        shard + 1 - 2 * lax.rem(shard, 2),
        2 - shard // 2,
        3 - 3 * (shard // 2),
    )


def place(shard, p):
    upper = shard // 2
    same = 1 - (upper - p // 2) * (upper - p // 2)
    far = (1 - upper) * p + upper * (3 - p)
    return same * (p - shard) * (p - shard) + (1 - same) * far


def aligned(start, size):
    return pl.ds(pl.multiple_of(start, size), size)


def standard_columns(feats, scale):
    pairs = feats.shape[0]
    mean = jnp.sum(feats, axis=0, keepdims=True) * (1.0 / pairs)
    dev = feats - mean
    var = jnp.sum(dev * dev, axis=0, keepdims=True) * (1.0 / pairs)
    return jnp.transpose(dev * (lax.rsqrt(var + EPS) * scale)).astype(jnp.bfloat16), mean


def blocks_kernel(
    late,
    images_hbm, captions_hbm, order_hbm, marks_hbm, gamma_hbm, words_hbm, text_gamma_hbm,
    f_all, g_all, image_mean_ref, text_mean_ref, relay, z_own,
    images_ref, captions_ref, order_ref, marks, gamma_ref, words, text_gamma_ref,
    u_all, c_all, keys, text_keys, raw,
    load_sem, mark_sem, u_sems, c_sems,
    right_send, left_send, f_recv, g_send, g_recv,
):
    dp, lm, cuts = 4, 4, CUTS
    me, lane = lax.axis_index("dp"), lax.axis_index("landmark")
    block = images_ref.shape[0]
    part = block // 2
    own = marks.shape[0]
    text_own = words.shape[0]
    pairs = block * dp
    piece = own // cuts

    loads = [
        pltpu.make_async_copy(src, dst, load_sem.at[at])
        for at, (src, dst) in enumerate((
            (images_hbm, images_ref), (captions_hbm, captions_ref), (order_hbm, order_ref),
            (gamma_hbm, gamma_ref), (words_hbm, words), (text_gamma_hbm, text_gamma_ref),
        ))
    ]
    mark_loads = [
        pltpu.make_async_copy(
            marks_hbm.at[pl.ds(at * piece, piece), :], marks.at[pl.ds(at * piece, piece), :],
            mark_sem.at[at],
        )
        for at in range(cuts)
    ]
    loads[0].start()
    barrier = pltpu.get_barrier_semaphore()
    for k in range(1, dp):
        pl.semaphore_signal(
            barrier, inc=1, device_id={"dp": lax.rem(me + k, dp)}, device_id_type=MESH
        )
    for k in range(1, lm):
        pl.semaphore_signal(
            barrier, inc=1, device_id={"landmark": lax.rem(lane + k, lm)}, device_id_type=MESH
        )
    for load in loads[1:4] + mark_loads + loads[4:]:
        load.start()

    half, core = lane // 2, lax.rem(lane, 2)
    mate = lane + 1 - 2 * core
    across = lax.rem(lane + 2, lm)
    order = near_first(me)
    mine = aligned(me * block, block)
    sends = []

    def launch(copy):
        copy.start()
        sends.append(copy)

    def portion(buf, sems, stage, k, shard, h, side, device):
        wide = buf.shape[1] // 2
        columns = pl.ds(0, 2 * wide) if h is None else aligned(h * wide, wide)
        ref = buf.at[aligned(shard * block + side * part, part), columns]
        return pltpu.make_async_remote_copy(
            src_ref=ref, dst_ref=ref, send_sem=sems.at[0, stage, k],
            recv_sem=sems.at[1, stage, shard], device_id=device, device_id_type=MESH,
        )

    def routes(ways):
        yield mate, half, 1 - core
        if ways == 4:
            yield across, 1 - half, core
            yield lm - 1 - lane, 1 - half, 1 - core

    def z_copy(buf, sems, ways, k, shard):
        h = half if ways[k] == 4 else None
        return portion(buf, sems, 0, k, shard, h, core, {"dp": order[k]})

    def spread(buf, sems, ways):
        for k in range(1, dp):
            launch(z_copy(buf, sems, ways, k, me))

    def pass_on(buf, sems, ways, blocks=range(1, 4)):
        for k in blocks:
            z_copy(buf, sems, ways, k, order[k]).wait_recv()
            h = half if ways[k] == 4 else None
            for stage, (target, _, _) in reversed(list(enumerate(routes(ways[k]), 1))):
                launch(portion(buf, sems, stage, k, order[k], h, core, {"landmark": target}))

    def gather(buf, sems, ways, blocks=range(1, 4)):
        for k in blocks:
            for stage, (target, h, side) in enumerate(routes(ways[k]), 1):
                h = h if ways[k] == 4 else None
                portion(buf, sems, stage, k, order[k], h, side, {"landmark": target}).wait_recv()

    loads[0].wait()
    u_all[mine, :] = unit_rows(images_ref[...].astype(jnp.float32)).astype(jnp.bfloat16)
    pl.semaphore_wait(barrier, dp - 1 + lm - 1)
    spread(u_all, u_sems, U_WAYS)
    loads[1].wait()
    loads[2].wait()
    picks = (
        lax.broadcasted_iota(jnp.int32, (block, block), 0) == order_ref[...]
    ).astype(jnp.bfloat16)
    paired = lax.dot_general(
        picks, captions_ref[...], (((0,), (0,)), ((), ())), preferred_element_type=jnp.float32
    )
    c_all[mine, :] = unit_rows(paired).astype(jnp.bfloat16)

    loads[3].wait()
    for at in range(cuts):
        mark_loads[at].wait()
        rows = pl.ds(at * piece, piece)
        scaled_keys(marks.at[rows, :], gamma_ref.at[:, rows], keys.at[rows, :])

    def hop(shard, j, send, target, rows):
        if j < FIRST:
            ref = raw.at[shard, pl.ds(j * block, block), pl.ds(0, rows)]
        else:
            ref = raw.at[
                shard, pl.ds(FIRST * block, pairs - FIRST * block),
                pl.ds((j - FIRST) * piece, piece),
            ]
        return pltpu.make_async_remote_copy(
            src_ref=ref, dst_ref=ref,
            send_sem=send.at[shard, j], recv_sem=f_recv.at[shard, j],
            device_id={"dp": target}, device_id_type=MESH,
        )

    def to_right(shard, j, rows=own):
        return hop(shard, j, right_send, jnp.minimum(me + 1, dp - 1), rows)

    def to_left(shard, j, rows=own):
        return hop(shard, j, left_send, jnp.maximum(me - 1, 0), rows)

    def send_own(j):
        @pl.when(me < dp - 1)
        def _():
            to_right(me, j).start()

        @pl.when(me > 0)
        def _():
            to_left(me, j).start()

    def features(units, rows):
        inner = lax.dot_general(
            units, keys[rows, :], (((1,), (1,)), ((), ())), preferred_element_type=jnp.float32
        )
        return jnp.exp(inner).astype(jnp.bfloat16)

    def first_block(j):
        units = u_all[aligned(order[j] * block, block), :]
        raw[me, j * block : (j + 1) * block, :] = features(units, pl.ds(0, own))
        send_own(j)

    first_block(0)
    spread(c_all, c_sems, C_WAYS)
    loads[4].wait()
    loads[5].wait()
    scaled_keys(words, text_gamma_ref, text_keys)
    hops = dp - 2 if late == cuts else dp - 1
    early_rows = own - late * piece

    def rows_of(d):
        return early_rows if d == dp - 1 else own

    def last_of(d):
        return FIRST - 1 + (cuts - late if d == dp - 1 else cuts)

    def receive(d, j):
        @pl.when(me + d < dp)
        def _():
            to_right(me + d, j, rows_of(d)).wait_recv()
            if d < hops and j <= last_of(d + 1):

                @pl.when(me > 0)
                def _():
                    to_left(me + d, j, rows_of(d + 1)).start()

        @pl.when(me - d >= 0)
        def _():
            to_left(me - d, j, rows_of(d)).wait_recv()
            if d < hops and j <= last_of(d + 1):

                @pl.when(me < dp - 1)
                def _():
                    to_right(me - d, j, rows_of(d + 1)).start()

    pass_on(u_all, u_sems, U_WAYS, range(1, FIRST))
    for j in range(1, FIRST):
        gather(u_all, u_sems, U_WAYS, (j,))
        first_block(j)
    pass_on(u_all, u_sems, U_WAYS, range(FIRST, dp))
    gather(u_all, u_sems, U_WAYS, range(FIRST, dp))
    others = jnp.concatenate(
        [u_all[aligned(order[k] * block, block), :] for k in range(FIRST, dp)], axis=0
    )
    for j in range(1, cuts + 1):
        rows = pl.ds((j - 1) * piece, piece)
        raw[me, FIRST * block :, (j - 1) * piece : j * piece] = features(others, rows)
        send_own(j + FIRST - 1)
        if j == CUTS:
            pass_on(c_all, c_sems, C_WAYS)

    def standardize(shard, j, mean_ref=None):
        for at in range((j - 1) * piece, j * piece, 128):
            columns = slice(at, at + 128)
            feats = jnp.concatenate(
                [
                    raw[shard, aligned(place(shard, p) * block, block), columns]
                    for p in range(dp)
                ],
                axis=0,
            )
            rows, mean = standard_columns(feats.astype(jnp.float32), 1.0)
            f_all[aligned(shard * own + at, 128), :] = rows
            if mean_ref is not None:
                mean_ref[:, columns] = mean

    for j in range(FIRST):
        receive(1, j)
    for j in range(1, cuts + 1):
        standardize(me, j, image_mean_ref)
    def g_copy(k, shard, target):
        rows = aligned(shard * text_own, text_own)
        return pltpu.make_async_remote_copy(
            src_ref=g_all.at[rows, :], dst_ref=g_all.at[rows, :],
            send_sem=g_send.at[k], recv_sem=g_recv.at[shard],
            device_id={"landmark": target}, device_id_type=MESH,
        )

    def text_features():
        gather(c_all, c_sems, C_WAYS)
        inner = lax.dot_general(
            c_all[...], text_keys[...], (((1,), (1,)), ((), ())), preferred_element_type=jnp.float32
        )
        rows, text_mean_ref[...] = standard_columns(
            jnp.exp(inner).astype(jnp.bfloat16).astype(jnp.float32), 1.0 / math.sqrt(pairs)
        )
        g_all[aligned(lane * text_own, text_own), :] = rows
        for k in range(1, lm):
            launch(g_copy(k - 1, lane, lax.rem(lane + k, lm)))

    def own_product():
        for k in range(1, lm):
            shard = lax.rem(lane + lm - k, lm)
            g_copy(k - 1, shard, lane).wait_recv()
        for at in range(0, z_own.shape[0], 256):
            z_own[at : at + 256, :] = lax.dot_general(
                f_all[aligned(me * own + at, 256), :], g_all[...],
                (((1,), (1,)), ((), ())), preferred_element_type=jnp.float32,
            )

    for d in range(1, hops + 1):
        for j in range(FIRST if d == 1 else 0, last_of(d) + 1):
            receive(d, j)
            if d == 1 and j == FIRST:
                text_features()
            if d == hops and j == 1:
                own_product()
            if j < FIRST:
                continue
            cut = j - FIRST + 1

            @pl.when(me - d >= 0)
            def _():
                standardize(me - d, cut)

            @pl.when(me + d < dp)
            def _():
                standardize(me + d, cut)

            if d == dp - 2 and cut > cuts - late:
                at = (cut - 1) * piece
                rows = pl.ds(at - early_rows, piece)

                @pl.when(me == dp - 2)
                def _():
                    relay[rows, :] = f_all[pl.ds(at, piece), :]

                @pl.when(me == 1)
                def _():
                    relay[rows, :] = f_all[pl.ds((dp - 1) * own + at, piece), :]

    for copy in sends:
        copy.wait_send()
    for d in range(hops):

        @pl.when(jnp.logical_and(me >= d, me < dp - 1))
        def _():
            for j in range(last_of(d + 1) + 1):
                to_right(me - d, j, rows_of(d + 1)).wait_send()

        @pl.when(jnp.logical_and(me < dp - d, me > 0))
        def _():
            for j in range(last_of(d + 1) + 1):
                to_left(me + d, j, rows_of(d + 1)).wait_send()


def product_kernel(
    tile, slots, dp, late_rows, f_ref, g_ref, image_mean_in, text_mean_in, *refs
):
    z_own = refs[0] if late_rows else None
    z_hbm, image_mean_ref, text_mean_ref, buf, sem, extra_sem = refs[-6:]
    means = [
        pltpu.make_async_copy(image_mean_in, image_mean_ref, extra_sem.at[0]),
        pltpu.make_async_copy(text_mean_in, text_mean_ref, extra_sem.at[1]),
    ]
    total = f_ref.shape[0]
    own = total // dp
    steps = (total - late_rows) // tile
    edge = own - late_rows
    if late_rows:
        me = lax.axis_index("dp")
        ready = z_own.shape[0]
        steps -= ready // tile
        mine = pl.ds(pl.multiple_of(me * own, ready), ready)
        means.insert(0, pltpu.make_async_copy(z_own, z_hbm.at[mine, :], extra_sem.at[2]))
    for copy in means:
        copy.start()

    def rows(at):
        start = at * tile
        if late_rows:
            skip = jnp.logical_and(me > 0, start >= edge)
            start = start + jnp.where(skip, late_rows, 0)
            start = start + jnp.where(start >= me * own, ready, 0)
        return pl.ds(pl.multiple_of(start, tile), tile)

    def out(at):
        slot = lax.rem(at, slots)
        return pltpu.make_async_copy(buf.at[slot], z_hbm.at[rows(at), :], sem.at[slot])

    def step(at, carry):
        @pl.when(at >= slots)
        def _():
            out(at - slots).wait()

        buf[lax.rem(at, slots)] = lax.dot_general(
            f_ref[rows(at), :], g_ref[...], (((1,), (1,)), ((), ())),
            preferred_element_type=jnp.float32,
        )
        out(at).start()
        return carry

    lax.fori_loop(0, steps, step, 0)
    for at in range(max(0, steps - slots), steps):
        out(jnp.int32(at)).wait()
    for copy in means:
        copy.wait()


def late_kernel(tile, dp, f_ref, got_ref, g_ref, z_in, z_hbm, buf, sem):
    me = lax.axis_index("dp")
    late_rows = got_ref.shape[0]
    own = f_ref.shape[0] // dp
    first = jnp.where(me == 0, dp * own, own) - late_rows
    inner = jnp.logical_and(me > 0, me < dp - 1)

    def rows(at):
        return pl.ds(pl.multiple_of(first + at * tile, tile), tile)

    def out(at):
        return pltpu.make_async_copy(buf.at[at], z_hbm.at[rows(at), :], sem.at[at])

    for at in range(late_rows // tile):
        buf[at] = lax.dot_general(
            jnp.where(inner, f_ref[rows(at), :], got_ref[pl.ds(at * tile, tile), :]),
            g_ref[...], (((1,), (1,)), ((), ())), preferred_element_type=jnp.float32,
        )
        out(at).start()
    for at in range(late_rows // tile):
        out(at).wait()


def per_device(
    images, captions, caption_of, image_landmarks, image_gamma, text_landmarks, text_gamma
):
    dp, lm = lax.axis_size("dp"), lax.axis_size("landmark")
    block, width = images.shape
    text_width = captions.shape[1]
    own, text_own = image_landmarks.shape[0], text_landmarks.shape[0]
    pairs = block * dp
    bf16, f32 = jnp.bfloat16, jnp.float32
    vmem = pl.BlockSpec(memory_space=pltpu.VMEM)
    hbm = pl.BlockSpec(memory_space=pltpu.HBM)
    dma = pltpu.SemaphoreType.DMA
    blocks = (
        dp == 4 and lm == 4 and block % 32 == 0 and own % 1024 == 0 and text_own % 128 == 0
        and width % 256 == 0 and text_width % 256 == 0
    )
    late_rows = own * LATE // CUTS if blocks else 0
    operands = [
        pltpu.with_memory_space_constraint(value, pltpu.HBM)
        for value in (
            images, captions, caption_of[None, :], image_landmarks, image_gamma[None, :],
            text_landmarks, text_gamma[None, :],
        )
    ]
    results = [
        jax.ShapeDtypeStruct((dp * own, pairs), bf16),
        jax.ShapeDtypeStruct((lm * text_own, pairs), bf16),
        jax.ShapeDtypeStruct((1, own), f32),
        jax.ShapeDtypeStruct((1, text_own), f32),
    ]
    held = [
        pltpu.VMEM((block, width), bf16),
        pltpu.VMEM((block, text_width), bf16),
        pltpu.VMEM((1, block), jnp.int32),
        pltpu.VMEM((own, width), bf16),
        pltpu.VMEM((1, own), f32),
        pltpu.VMEM((text_own, text_width), bf16),
        pltpu.VMEM((1, text_own), f32),
    ]
    params = pltpu.CompilerParams(
        collective_id=0, has_side_effects=True, vmem_limit_bytes=40 * 2**20
    )
    if blocks:
        f, g, image_mean, text_mean, relay, *z_own = pl.pallas_call(
            functools.partial(blocks_kernel, LATE),
            out_shape=results + [
                jax.ShapeDtypeStruct((late_rows, pairs), bf16),
                jax.ShapeDtypeStruct((own // 4, lm * text_own), f32),
            ],
            in_specs=[hbm] * 7,
            out_specs=[vmem] * 6,
            scratch_shapes=held + [
                pltpu.VMEM((pairs, width), bf16),
                pltpu.VMEM((pairs, text_width), bf16),
                pltpu.VMEM((own, width), bf16),
                pltpu.VMEM((text_own, text_width), bf16),
                pltpu.VMEM((dp, pairs, own), bf16),
                dma((6,)), dma((CUTS,)), dma((2, 4, dp)), dma((2, 4, dp)),
                dma((dp, FIRST + CUTS)), dma((dp, FIRST + CUTS)), dma((dp, FIRST + CUTS)),
                dma((lm,)), dma((lm,)),
            ],
            compiler_params=params,
            name="block_exchange",
        )(*operands)
    else:
        z_own = []
        split = 2 if lm % 2 == 0 else 1
        chunks = max(1, own // 256)
        f, g, image_mean, text_mean = pl.pallas_call(
            functools.partial(exchange_kernel, dp, lm, split, chunks),
            out_shape=results,
            in_specs=[hbm] * 7,
            out_specs=[vmem] * 4,
            scratch_shapes=held + [
                pltpu.VMEM((pairs, width), bf16),
                pltpu.VMEM((pairs, text_width), bf16),
                pltpu.VMEM((own, width), bf16),
                pltpu.VMEM((text_own, text_width), bf16),
                dma((7,)),
                dma((dp,)), dma((dp,)), dma((dp,)), dma((dp,)),
                dma((dp,)), dma((dp,)), dma((dp,)), dma((dp,)),
                dma((dp, chunks)), dma((dp, chunks)), dma((dp, chunks)),
                dma((lm,)), dma((lm,)),
            ],
            compiler_params=params,
            name="exchange",
        )(*operands)
    rows, columns = dp * own, lm * text_own
    ahead = rows - late_rows
    tile = math.gcd(math.gcd(own, own - late_rows), TILE)
    slots = min(SLOTS, ahead // tile)
    if late_rows:
        got = lax.ppermute(relay, "dp", ((dp - 2, dp - 1), (1, 0)))
    zstat, image_mean, text_mean = pl.pallas_call(
        functools.partial(product_kernel, tile, slots, dp, late_rows),
        out_shape=(
            jax.ShapeDtypeStruct((rows, columns), f32),
            jax.ShapeDtypeStruct((1, own), f32),
            jax.ShapeDtypeStruct((1, text_own), f32),
        ),
        in_specs=[vmem] * (4 + len(z_own)),
        out_specs=(hbm, hbm, hbm),
        scratch_shapes=[pltpu.VMEM((slots, tile, columns), f32), dma((slots,)), dma((3,))],
        compiler_params=pltpu.CompilerParams(vmem_limit_bytes=40 * 2**20),
        cost_estimate=pl.CostEstimate(
            flops=2 * ahead * columns * pairs, bytes_accessed=4 * ahead * columns, transcendentals=0
        ),
        name="product",
    )(f, g, image_mean, text_mean, *z_own)
    if late_rows:
        zstat = pl.pallas_call(
            functools.partial(late_kernel, LATE_TILE, dp),
            out_shape=jax.ShapeDtypeStruct((rows, columns), f32),
            in_specs=[vmem, vmem, vmem, hbm],
            out_specs=hbm,
            scratch_shapes=[
                pltpu.VMEM((late_rows // LATE_TILE, LATE_TILE, columns), f32), dma((late_rows // LATE_TILE,)),
            ],
            input_output_aliases={3: 0},
            compiler_params=pltpu.CompilerParams(vmem_limit_bytes=40 * 2**20),
            cost_estimate=pl.CostEstimate(
                flops=2 * late_rows * columns * pairs, bytes_accessed=4 * late_rows * columns,
                transcendentals=0,
            ),
            name="late_product",
        )(f, got, g, zstat)
    return (zstat, image_mean[0], text_mean[0])


def solution(mesh):
    in_specs = (
        P(("groups", "dp"), None),
        P(("groups", "dp"), None),
        P(("groups", "dp")),
        P(("landmark", "dp"), None),
        P(("landmark", "dp")),
        P(("dp", "landmark"), None),
        P(("dp", "landmark")),
    )
    out_specs = (
        P(("groups", "landmark"), "dp"),
        P(("groups", "landmark", "dp")),
        P(("groups", "dp", "landmark")),
    )
    return jax.shard_map(
        per_device, mesh=mesh, in_specs=in_specs, out_specs=out_specs, check_vma=False
    )
```
